32 devices in a mesh: dp: 16 (over z, x, core), mp: 2 (over y).
Axes of the slice: x: 2, y: 2, z: 4, core: 2. Of those that a mesh axis runs over, the one named last changes fastest.
Arguments:
- layer_in: bfloat16 [35840, 1024], P(('dp', 'mp')), may hold values from -6 to 6
- patch_count: int32 [128], P('dp'), may hold values from 100 to 240, as said below
- attn_gain: bfloat16 [1024], replicated, may hold values from 0.5 to 1.5
- attn_shift: bfloat16 [1024], replicated, may hold values from -2 to 2
- query_weight: bfloat16 [1024, 1024], P(None, 'mp'), may hold values from -0.1875 to 0.1875
- query_bias: bfloat16 [1024], P('mp'), may hold values from -2 to 2
- key_weight: bfloat16 [1024, 1024], P(None, 'mp'), may hold values from -0.1875 to 0.1875
- value_weight: bfloat16 [1024, 1024], P(None, 'mp'), may hold values from -0.1875 to 0.1875
- value_bias: bfloat16 [1024], P('mp'), may hold values from -2 to 2
- out_weight: bfloat16 [1024, 1024], P('mp'), may hold values from -0.5 to 0.5
- out_bias: bfloat16 [1024], replicated, may hold values from -2 to 2
- mlp_gain: bfloat16 [1024], replicated, may hold values from 0.5 to 1.5
- mlp_shift: bfloat16 [1024], replicated, may hold values from -2 to 2
- up_weight: bfloat16 [1024, 4096], P(None, 'mp'), may hold values from -0.1875 to 0.1875
- up_bias: bfloat16 [4096], P('mp'), may hold values from -2 to 2
- down_weight: bfloat16 [4096, 1024], P('mp'), may hold values from -0.09375 to 0.09375
- down_bias: bfloat16 [1024], replicated, may hold values from -2 to 2
- layer_cot: bfloat16 [35840, 1024], P(('dp', 'mp')), may hold values from -6 to 6
Outputs:
- layer_out: bfloat16 [35840, 1024], P(('dp', 'mp'))
- grad_in: bfloat16 [35840, 1024], P(('dp', 'mp'))
- grad_attn_gain: float32 [1024], replicated
- grad_attn_shift: float32 [1024], replicated
- grad_query_weight: float32 [1024, 1024], P(None, 'mp')
- grad_query_bias: float32 [1024], P('mp')
- grad_key_weight: float32 [1024, 1024], P(None, 'mp')
- grad_value_weight: float32 [1024, 1024], P(None, 'mp')
- grad_value_bias: float32 [1024], P('mp')
- grad_out_weight: float32 [1024, 1024], P('mp')
- grad_out_bias: float32 [1024], replicated
- grad_mlp_gain: float32 [1024], replicated
- grad_mlp_shift: float32 [1024], replicated
- grad_up_weight: float32 [1024, 4096], P(None, 'mp')
- grad_up_bias: float32 [4096], P('mp')
- grad_down_weight: float32 [4096, 1024], P('mp')
- grad_down_bias: float32 [1024], replicated
The draws below stay inside these ranges and needn't reach their ends.
Inputs may be any that keep to these rules, and one draw needn't show every extreme that they name: Patches of each pair; rows 40 + patch_count and later of a pair are padding.
All inputs are finite; a program needn't handle non-finite values.
Results may differ from the reference program's by a relative error of at most 0.02.
Values may be sent and summed in bfloat16 or wider, within the bound.
No kernel may reach another device: no remote copies, remote signals or barrier semaphores. Data moves between devices by JAX's collectives and lax.ppermute only.
A program may use at most 320 MiB of HBM per device.

```python
import jax
import jax.numpy as jnp
from jax import lax

D = 1024
HEADS = 16
HEAD_DIM = 64
FF = 4096
TEXT = 40
PATCH_MAX = 240
PATCH_MIN = 100
PAIRS_DEV = 8
SEQ = 280
PAIRS = 128
TOKENS = 35840


def draw_patch_count(key, part):
    counts = jax.random.randint(key, (PAIRS,), PATCH_MIN, PATCH_MAX + 1)
    counts = counts.at[0].set(PATCH_MAX).at[1].set(PATCH_MIN)
    return counts.astype(jnp.int32)


def block_levels(key, extent, split, low, high):
    def one(position, parts):
        steps = jax.random.uniform(jax.random.fold_in(jax.random.fold_in(key, 6), position), (parts,), jnp.float32, low / len(split), high / len(split))
        return jnp.repeat(jnp.exp(steps), extent[position] // parts).reshape((-1,) + (1,) * (len(extent) - position - 1))

    level = one(*split[0])
    for cut in split[1:]:
        level = level * one(*cut)
    return level


def centred(own_key, extent, scale, bound, cuts=(), held_as=jnp.bfloat16):
    array = scale * jax.random.normal(own_key, extent, jnp.float32)
    if cuts:
        array = array * block_levels(own_key, extent, cuts, -0.22, 0.18)
    return jnp.clip(array, -bound, bound).astype(held_as)


def setup_inputs(seed: int = 0) -> dict:
    streams_of = jax.random.split(jax.random.key(seed), 19)
    return {
        "layer_in": centred(streams_of[0], (TOKENS, D), 1.0, 6.0, ((0, 32),)),
        "patch_count": draw_patch_count(jax.random.fold_in(streams_of[18], 71), 0),
        "attn_gain": jnp.clip(1.0 + 0.1 * jax.random.normal(streams_of[2], (D,), jnp.float32), 0.5, 1.5).astype(jnp.bfloat16),
        "attn_shift": centred(streams_of[3], (D,), 0.3, 2.0),
        "query_weight": centred(streams_of[4], (D, D), D ** -0.5, 0.1875, ((1, 2),)),
        "query_bias": centred(streams_of[5], (D,), 0.3, 2.0, ((0, 2),)),
        "key_weight": centred(streams_of[6], (D, D), D ** -0.5, 0.1875, ((1, 2),)),
        "value_weight": centred(streams_of[7], (D, D), D ** -0.5, 0.1875, ((1, 2),)),
        "value_bias": centred(streams_of[8], (D,), 0.3, 2.0, ((0, 2),)),
        "out_weight": centred(streams_of[9], (D, D), (D // 8) ** -0.5, 0.5, ((0, 2),)),
        "out_bias": centred(streams_of[10], (D,), 0.3, 2.0),
        "mlp_gain": jnp.clip(1.0 + 0.1 * jax.random.normal(streams_of[11], (D,), jnp.float32), 0.5, 1.5).astype(jnp.bfloat16),
        "mlp_shift": centred(streams_of[12], (D,), 0.3, 2.0),
        "up_weight": centred(streams_of[13], (D, FF), D ** -0.5, 0.1875, ((1, 2),)),
        "up_bias": centred(streams_of[14], (FF,), 0.3, 2.0, ((0, 2),)),
        "down_weight": centred(streams_of[15], (FF, D), FF ** -0.5, 0.09375, ((0, 2),)),
        "down_bias": centred(streams_of[16], (D,), 0.3, 2.0),
        "layer_cot": centred(streams_of[17], (TOKENS, D), 1.0, 6.0, ((0, 32),)),
    }


EPS = 1e-05
SCALE = 0.125
NEGATIVE = -1e+30
PRECISE = lax.Precision.HIGHEST

@jax.custom_vjp
def low(v):
    return lax.optimization_barrier(v.astype(jnp.bfloat16)).astype(jnp.float32)

@jax.custom_vjp
def low_back(v):
    return v

def low_keep(v):
    return (low(v), None)

def low_pass(kept, grad):
    return (grad,)

def back_keep(v):
    return (v, None)

def back_low(kept, grad):
    return (low(grad),)
low.defvjp(low_keep, low_pass)
low_back.defvjp(back_keep, back_low)

def layer_norm(values, gain, shift):
    center = values - lax.optimization_barrier(jnp.mean(values, -1, keepdims=True))
    spread = lax.optimization_barrier(jnp.mean(center * center, -1, keepdims=True))
    return center * lax.rsqrt(spread + EPS) * gain + shift

def product(left, right):
    return jnp.dot(left, right, precision=PRECISE, preferred_element_type=jnp.float32)

def attend(block):
    query_blk, key_blk, value_blk, counts = block
    scores = low_back(jnp.einsum('pqhd,pkhd->phqk', query_blk, key_blk, precision=PRECISE) * SCALE)
    valid = jnp.arange(SEQ)[None, :] < (TEXT + counts)[:, None]
    scores = jnp.where(valid[:, None, None, :], scores, NEGATIVE)
    probs = jax.nn.softmax(scores, axis=-1)
    return jnp.einsum('phqk,pkhd->pqhd', low(probs), value_blk, precision=PRECISE)

def exact_gelu(values):
    return jax.nn.gelu(values, approximate=False)

def forward(layer_in, attn_gain, attn_shift, query_weight, query_bias, key_weight, value_weight, value_bias, out_weight, out_bias, mlp_gain, mlp_shift, up_weight, up_bias, down_weight, down_bias, patch_count):
    groups = PAIRS // PAIRS_DEV
    normed = low(layer_norm(layer_in, attn_gain, attn_shift))
    query_rows = low_back(low(product(normed, query_weight) + query_bias))
    key_rows = low_back(low(product(normed, key_weight)))
    value_rows = low_back(low(product(normed, value_weight) + value_bias))
    shape_five = (groups, PAIRS_DEV, SEQ, HEADS, HEAD_DIM)
    context = lax.map(jax.checkpoint(attend), (query_rows.reshape(shape_five), key_rows.reshape(shape_five), value_rows.reshape(shape_five), patch_count.reshape(groups, PAIRS_DEV)))
    context = low_back(low(context.reshape(TOKENS, D)))
    attended = low_back(product(context, out_weight) + out_bias)
    middle = layer_in + attended
    hidden_in = low(layer_norm(middle, mlp_gain, mlp_shift))
    pre_act = low_back(product(hidden_in, up_weight) + up_bias)
    act_low = low(exact_gelu(pre_act))
    ffn_out = low_back(product(act_low, down_weight) + down_bias)
    return middle + ffn_out

def reference(layer_in, patch_count, attn_gain, attn_shift, query_weight, query_bias, key_weight, value_weight, value_bias, out_weight, out_bias, mlp_gain, mlp_shift, up_weight, up_bias, down_weight, down_bias, layer_cot):
    params = [layer_in, attn_gain, attn_shift, query_weight, query_bias, key_weight, value_weight, value_bias, out_weight, out_bias, mlp_gain, mlp_shift, up_weight, up_bias, down_weight, down_bias]
    params = [item.astype(jnp.float32) for item in params]

    def closed(*values):
        return forward(*values, patch_count)
    result, pull = jax.vjp(closed, *params)
    grads = pull(layer_cot.astype(jnp.float32))
    return (result.astype(jnp.bfloat16), grads[0].astype(jnp.bfloat16), grads[1], grads[2], grads[3], grads[4], grads[5], grads[6], grads[7], grads[8], grads[9], grads[10], grads[11], grads[12], grads[13], grads[14], grads[15])
```

```python
import jax
import jax.numpy as jnp
from jax import lax
from jax.sharding import PartitionSpec as P

HEAD_DIM = 64
TEXT = 40
SEQ = 280


EPS = 1e-05
SCALE = 0.125
NEGATIVE = -1e30


def layer_norm(values, gain, shift):
    center = values - jnp.mean(values, -1, keepdims=True)
    spread = jnp.mean(center * center, -1, keepdims=True)
    return center * lax.rsqrt(spread + EPS) * gain + shift


def exact_gelu(values):
    return jax.nn.gelu(values, approximate=False)


def matmul_rows(left, right):
    return jnp.dot(left, right, preferred_element_type=jnp.float32)


def contract_rows(left, right):
    return lax.dot_general(
        left, right, (((0,), (0,)), ((), ())), preferred_element_type=jnp.float32
    )


def contract_cols(left, right):
    return lax.dot_general(
        left, right, (((1,), (1,)), ((), ())), preferred_element_type=jnp.float32
    )


def column_sum(values):
    return jnp.sum(values.astype(jnp.float32), 0)


def general_body(
    layer_in,
    patch_count,
    attn_gain,
    attn_shift,
    query_weight,
    query_bias,
    key_weight,
    value_weight,
    value_bias,
    out_weight,
    out_bias,
    mlp_gain,
    mlp_shift,
    up_weight,
    up_bias,
    down_weight,
    down_bias,
    layer_cot,
):
    lowtype = jnp.bfloat16
    wide = jnp.float32
    rows_in = layer_in.astype(wide)
    gain_one = attn_gain.astype(wide)
    shift_one = attn_shift.astype(wide)
    gain_two = mlp_gain.astype(wide)
    shift_two = mlp_shift.astype(wide)
    normed_tok, norm_pull = jax.vjp(layer_norm, rows_in, gain_one, shift_one)
    group_rows = lax.all_gather(normed_tok.astype(lowtype), "mp", axis=0, tiled=True)
    query_rows = (matmul_rows(group_rows, query_weight) + query_bias.astype(wide)).astype(lowtype)
    key_rows = matmul_rows(group_rows, key_weight).astype(lowtype)
    value_rows = (matmul_rows(group_rows, value_weight) + value_bias.astype(wide)).astype(lowtype)
    pairs = patch_count.shape[0]
    local_width = query_weight.shape[1]
    local_heads = local_width // HEAD_DIM
    group_total = group_rows.shape[0]
    shape_four = (pairs, SEQ, local_heads, HEAD_DIM)
    query_blk = query_rows.reshape(shape_four)
    key_blk = key_rows.reshape(shape_four)
    value_blk = value_rows.reshape(shape_four)
    scores = jnp.einsum("pqhd,pkhd->phqk", query_blk, key_blk, preferred_element_type=wide) * SCALE
    valid = jnp.arange(SEQ)[None, :] < (TEXT + patch_count)[:, None]
    scores = jnp.where(valid[:, None, None, :], scores, NEGATIVE)
    probs = jax.nn.softmax(scores, axis=-1)
    probs_low = probs.astype(lowtype)
    context = jnp.einsum("phqk,pkhd->pqhd", probs_low, value_blk, preferred_element_type=wide)
    context = context.astype(lowtype).reshape(group_total, local_width)
    context_tok = lax.all_to_all(context, "mp", split_axis=0, concat_axis=1, tiled=True)
    out_full = lax.all_gather(out_weight, "mp", axis=0, tiled=True)
    attended = matmul_rows(context_tok, out_full) + out_bias.astype(wide)
    middle = rows_in + attended
    hidden_wide, mlp_pull = jax.vjp(layer_norm, middle, gain_two, shift_two)
    hidden_in = hidden_wide.astype(lowtype)
    cot_wide = layer_cot.astype(wide)
    up_full, bias_full, down_full = (
        lax.all_gather(up_weight, "mp", axis=1, tiled=True),
        lax.all_gather(up_bias, "mp", axis=0, tiled=True),
        lax.all_gather(down_weight, "mp", axis=0, tiled=True),
    )
    pre_act = matmul_rows(hidden_in, up_full) + bias_full.astype(wide)
    act_wide, gelu_pull = jax.vjp(exact_gelu, pre_act)
    act_low = act_wide.astype(lowtype)
    ffn_out = matmul_rows(act_low, down_full) + down_bias.astype(wide)
    whole_down = contract_rows(act_low, layer_cot)
    act_grad = contract_cols(layer_cot, down_full)
    pre_grad = gelu_pull(act_grad)[0].astype(lowtype)
    whole_up_bias = column_sum(pre_grad)
    whole_up = contract_rows(hidden_in, pre_grad)
    hidden_grad = contract_cols(pre_grad, up_full)
    grad_up_weight, grad_up_bias, grad_down_weight = (
        lax.psum_scatter(
            whole_up.astype(jnp.bfloat16), "mp", scatter_dimension=1, tiled=True
        ).astype(jnp.float32),
        lax.psum_scatter(
            whole_up_bias.astype(jnp.bfloat16), "mp", scatter_dimension=0, tiled=True
        ).astype(jnp.float32),
        lax.psum_scatter(
            whole_down.astype(jnp.bfloat16), "mp", scatter_dimension=0, tiled=True
        ).astype(jnp.float32),
    )
    layer_out = (middle + ffn_out).astype(lowtype)
    grad_down_bias = column_sum(layer_cot)
    middle_part, grad_gain_two, grad_shift_two = mlp_pull(hidden_grad)
    middle_grad = cot_wide + middle_part
    attn_grad = middle_grad.astype(lowtype)
    grad_out_bias = column_sum(attn_grad)
    grad_out_weight = lax.psum_scatter(
        contract_rows(context_tok, attn_grad).astype(jnp.bfloat16),
        "mp",
        scatter_dimension=0,
        tiled=True,
    ).astype(jnp.float32)
    context_grad_tok = contract_cols(attn_grad, out_full).astype(lowtype)
    context_grad = lax.all_to_all(
        context_grad_tok, "mp", split_axis=1, concat_axis=0, tiled=True
    ).reshape(shape_four)
    probs_grad = jnp.einsum("pqhd,pkhd->phqk", context_grad, value_blk, preferred_element_type=wide)
    value_grad = jnp.einsum("phqk,pqhd->pkhd", probs_low, context_grad, preferred_element_type=wide)
    value_grad = value_grad.astype(lowtype).reshape(group_total, local_width)
    score_grad = (probs * (probs_grad - jnp.sum(probs * probs_grad, -1, keepdims=True))).astype(
        lowtype
    )
    query_grad = (
        jnp.einsum("phqk,pkhd->pqhd", score_grad, key_blk, preferred_element_type=wide) * SCALE
    )
    query_grad = query_grad.astype(lowtype).reshape(group_total, local_width)
    key_grad = (
        jnp.einsum("phqk,pqhd->pkhd", score_grad, query_blk, preferred_element_type=wide) * SCALE
    )
    key_grad = key_grad.astype(lowtype).reshape(group_total, local_width)
    grad_query_weight = contract_rows(group_rows, query_grad)
    grad_key_weight = contract_rows(group_rows, key_grad)
    grad_value_weight = contract_rows(group_rows, value_grad)
    grad_query_bias = column_sum(query_grad)
    grad_value_bias = column_sum(value_grad)
    total = contract_cols(query_grad, query_weight)
    total = total + contract_cols(key_grad, key_weight)
    normed_grad = lax.psum_scatter(
        (total + contract_cols(value_grad, value_weight)).astype(jnp.bfloat16),
        "mp",
        scatter_dimension=0,
        tiled=True,
    ).astype(jnp.float32)
    input_part, grad_gain_one, grad_shift_one = norm_pull(normed_grad)
    grad_in = (middle_grad + input_part).astype(lowtype)
    (
        grad_query_weight,
        grad_query_bias,
        grad_key_weight,
        grad_value_weight,
        grad_value_bias,
        grad_out_weight,
        grad_up_weight,
        grad_up_bias,
        grad_down_weight,
    ) = (
        lax.psum(grad_query_weight.astype(jnp.bfloat16), "dp").astype(jnp.float32),
        lax.psum(grad_query_bias.astype(jnp.bfloat16), "dp").astype(jnp.float32),
        lax.psum(grad_key_weight.astype(jnp.bfloat16), "dp").astype(jnp.float32),
        lax.psum(grad_value_weight.astype(jnp.bfloat16), "dp").astype(jnp.float32),
        lax.psum(grad_value_bias.astype(jnp.bfloat16), "dp").astype(jnp.float32),
        lax.psum(grad_out_weight.astype(jnp.bfloat16), "dp").astype(jnp.float32),
        lax.psum(grad_up_weight.astype(jnp.bfloat16), "dp").astype(jnp.float32),
        lax.psum(grad_up_bias.astype(jnp.bfloat16), "dp").astype(jnp.float32),
        lax.psum(grad_down_weight.astype(jnp.bfloat16), "dp").astype(jnp.float32),
    )
    grad_gain_one, grad_shift_one, grad_out_bias, grad_gain_two, grad_shift_two, grad_down_bias = (
        lax.psum(
            (
                grad_gain_one,
                grad_shift_one,
                grad_out_bias,
                grad_gain_two,
                grad_shift_two,
                grad_down_bias,
            ),
            ("dp", "mp"),
        )
    )
    return (
        layer_out,
        grad_in,
        grad_gain_one,
        grad_shift_one,
        grad_query_weight,
        grad_query_bias,
        grad_key_weight,
        grad_value_weight,
        grad_value_bias,
        grad_out_weight,
        grad_out_bias,
        grad_gain_two,
        grad_shift_two,
        grad_up_weight,
        grad_up_bias,
        grad_down_weight,
        grad_down_bias,
    )


def flip(value, axis, bit, size):
    return lax.ppermute(value, axis, [(i, i ^ bit) for i in range(size)])


CORE, XBIT, ZLOW, ZHIGH = 1, 2, 4, 8


def pick(value, index, width, axis):
    return lax.dynamic_slice_in_dim(value, index * width, width, axis)


def attend(query, key, value, valid):
    wide = jnp.float32
    scores = jnp.einsum("pqhd,pkhd->phqk", query, key, preferred_element_type=wide) * SCALE
    scores = jnp.where(valid[:, None, None, :], scores, NEGATIVE)
    probs = jax.nn.softmax(scores, axis=-1)
    context = jnp.einsum(
        "phqk,pkhd->pqhd", probs.astype(jnp.bfloat16), value, preferred_element_type=wide
    )
    return probs, context.astype(jnp.bfloat16)


def attend_back(query, key, value, probs, cot):
    wide = jnp.float32
    low = jnp.bfloat16
    probs_grad = jnp.einsum("pqhd,pkhd->phqk", cot, value, preferred_element_type=wide)
    value_grad = jnp.einsum(
        "phqk,pqhd->pkhd", probs.astype(low), cot, preferred_element_type=wide
    ).astype(low)
    score_grad = (probs * (probs_grad - jnp.sum(probs * probs_grad, -1, keepdims=True))).astype(low)
    query_grad = (
        jnp.einsum("phqk,pkhd->pqhd", score_grad, key, preferred_element_type=wide) * SCALE
    ).astype(low)
    key_grad = (
        jnp.einsum("phqk,pqhd->pkhd", score_grad, query, preferred_element_type=wide) * SCALE
    ).astype(low)
    return query_grad, key_grad, value_grad


def paired_body(
    layer_in,
    patch_count,
    attn_gain,
    attn_shift,
    query_weight,
    query_bias,
    key_weight,
    value_weight,
    value_bias,
    out_weight,
    out_bias,
    mlp_gain,
    mlp_shift,
    up_weight,
    up_bias,
    down_weight,
    down_bias,
    layer_cot,
):
    low = jnp.bfloat16
    wide = jnp.float32
    groups = lax.axis_size("dp")
    rank = lax.axis_index("dp")
    half_id = lax.axis_index("mp")
    core_id, x_id, zlow_id, zhigh_id = rank & 1, (rank >> 1) & 1, (rank >> 2) & 1, (rank >> 3) & 1
    part = core_id * 2 + x_id
    spot = part * 4 + zlow_id * 2 + zhigh_id

    def swap(value, bit):
        return flip(value, "dp", bit, groups)

    def across(value):
        return flip(value, "mp", 1, 2)

    def fetch(piece):
        near = across(piece)
        pair = jnp.stack([near, swap(near, XBIT)])
        far = swap(pair, CORE)
        return [pair[0], pair[1], far[0], far[1]]

    width = query_weight.shape[1]
    hidden = up_weight.shape[1]
    quarter = width // 4
    block = hidden // 4

    bias_other = across(jnp.concatenate([query_bias, value_bias, up_bias]))
    small = lambda vec: [pick(vec, part ^ r, vec.shape[0] // 4, 0) for r in range(4)]
    other_query_bias = jnp.concatenate(small(bias_other[:width]))
    other_value_bias = jnp.concatenate(small(bias_other[width : 2 * width]))
    other_up_bias = jnp.concatenate(small(bias_other[2 * width :]))

    qkv_pieces = fetch(
        jnp.stack([pick(w, part, quarter, 1) for w in (query_weight, key_weight, value_weight)])
    )
    other_query, other_key, other_value = (
        jnp.concatenate([piece[i] for piece in qkv_pieces], 1) for i in range(3)
    )
    other_out = jnp.concatenate(fetch(pick(out_weight, part, quarter, 0)), 0)
    other_up = jnp.concatenate(fetch(pick(up_weight, part, block, 1)), 1)
    other_down = jnp.concatenate(fetch(pick(down_weight, part, block, 0)), 0)

    rows_in = layer_in.astype(wide)
    gain_one = attn_gain.astype(wide)
    shift_one = attn_shift.astype(wide)
    gain_two = mlp_gain.astype(wide)
    shift_two = mlp_shift.astype(wide)
    normed_wide, norm_pull = jax.vjp(layer_norm, rows_in, gain_one, shift_one)
    normed = normed_wide.astype(low)
    rows = layer_in.shape[0]
    pairs = rows // SEQ
    counts = pick(patch_count, half_id, pairs, 0)
    valid = jnp.arange(SEQ)[None, :] < (TEXT + counts)[:, None]
    shape_four = (pairs, SEQ, width // HEAD_DIM, HEAD_DIM)

    halves = (
        (query_weight, query_bias, key_weight, value_weight, value_bias, out_weight),
        (other_query, other_query_bias, other_key, other_value, other_value_bias, other_out),
    )
    kept = []
    attended = out_bias.astype(wide)
    for wq, bq, wk, wv, bv, wo in halves:
        query = (matmul_rows(normed, wq) + bq.astype(wide)).astype(low).reshape(shape_four)
        key = matmul_rows(normed, wk).astype(low).reshape(shape_four)
        value = (matmul_rows(normed, wv) + bv.astype(wide)).astype(low).reshape(shape_four)
        probs, context = attend(query, key, value, valid)
        context = context.reshape(rows, width)
        attended = attended + matmul_rows(context, wo)
        kept.append((query, key, value, probs, context))
    middle = rows_in + attended
    hidden_wide, mlp_pull = jax.vjp(layer_norm, middle, gain_two, shift_two)
    hidden_in = hidden_wide.astype(low)
    cot_wide = layer_cot.astype(wide)

    ffn_out = down_bias.astype(wide)
    hidden_grad = 0.0
    up_grads, down_grads, up_bias_grads = [], [], []
    for wu, bu, wd in ((up_weight, up_bias, down_weight), (other_up, other_up_bias, other_down)):
        pre_act = matmul_rows(hidden_in, wu) + bu.astype(wide)
        act_wide, gelu_pull = jax.vjp(exact_gelu, pre_act)
        act_low = act_wide.astype(low)
        ffn_out = ffn_out + matmul_rows(act_low, wd)
        act_grad = contract_cols(layer_cot, wd)
        pre_grad = gelu_pull(act_grad)[0].astype(low)
        hidden_grad = hidden_grad + contract_cols(pre_grad, wu)
        down_grads.append(contract_rows(act_low, layer_cot).astype(low))
        up_grads.append(contract_rows(hidden_in, pre_grad).astype(low))
        up_bias_grads.append(column_sum(pre_grad))
    layer_out = (middle + ffn_out).astype(low)
    grad_down_bias = column_sum(layer_cot)

    def relative(own, axis):
        return [pick(own, part ^ r, own.shape[axis] // 4, axis) for r in range(4)]

    def split(other, axis):
        return jnp.split(other, 4, axis)

    def reduce(own, other):
        total = lambda a, b: (a.astype(wide) + b.astype(wide)).astype(low)
        arrived = swap(jnp.stack(other[2:]), CORE)
        outbound = total(jnp.stack(other[:2]), arrived)
        arrived = swap(jnp.stack(own[2:]), CORE)
        beyond = across(outbound)
        mine = (
            jnp.stack(own[:2]).astype(wide) + arrived.astype(wide) + beyond.astype(wide)
        ).astype(low)
        one = total(mine[0], swap(mine[1], XBIT))
        four = one.reshape((2, 2, one.shape[0] // 4) + one.shape[1:])
        two = total(
            pick(four, zlow_id, 1, 0)[0], swap(pick(four, zlow_id ^ 1, 1, 0)[0], ZLOW)
        )
        last = total(pick(two, zhigh_id, 1, 0), swap(pick(two, zhigh_id ^ 1, 1, 0), ZHIGH))
        for bit in (ZHIGH, ZLOW, XBIT):
            last = jnp.concatenate([last, swap(last, bit)])
        return last, swap(last, CORE)

    def natural(both):
        rel = jnp.concatenate(both)
        return rel[jnp.arange(16) ^ spot].astype(wide)

    def columns(both):
        full = natural(both)
        full = full.reshape((4, 4) + full.shape[1:])
        return full.transpose(1, 2, 0, 3).reshape(full.shape[1] * full.shape[2], -1)

    def rows_of(both):
        full = natural(both)
        return full.reshape(-1, full.shape[-1])

    grad_up_weight = columns(reduce(relative(up_grads[0], 1), split(up_grads[1], 1)))
    grad_down_weight = rows_of(reduce(relative(down_grads[0], 0), split(down_grads[1], 0)))

    middle_part, grad_gain_two, grad_shift_two = mlp_pull(hidden_grad)
    middle_grad = cot_wide + middle_part
    attn_grad = middle_grad.astype(low)
    grad_out_bias = column_sum(attn_grad)

    normed_grad = 0.0
    grads = []
    for (wq, bq, wk, wv, bv, wo), (query, key, value, probs, context) in zip(halves, kept):
        grad_wo = contract_rows(context, attn_grad).astype(low)
        context_grad = contract_cols(attn_grad, wo).astype(low).reshape(shape_four)
        parts = attend_back(query, key, value, probs, context_grad)
        flat = [item.reshape(rows, width) for item in parts]
        weights = [contract_rows(normed, item).astype(low) for item in flat]
        for item, weight in zip(flat, (wq, wk, wv)):
            normed_grad = normed_grad + contract_cols(item, weight)
        grads.append((weights, grad_wo, column_sum(flat[0]), column_sum(flat[2])))
    grad_query_weight, grad_key_weight, grad_value_weight = (
        columns(reduce(relative(grads[0][0][i], 1), split(grads[1][0][i], 1))) for i in range(3)
    )
    grad_out_weight = rows_of(reduce(relative(grads[0][1], 0), split(grads[1][1], 0)))
    input_part, grad_gain_one, grad_shift_one = norm_pull(normed_grad)
    grad_in = (middle_grad + input_part).astype(low)

    def back_to_place(vec):
        return vec.reshape(4, -1)[jnp.arange(4) ^ part].reshape(-1)

    def total_over(vec, bits):
        for bit in bits:
            vec = vec + swap(vec, bit)
        return vec

    own_small = jnp.concatenate([grads[0][2], grads[0][3], up_bias_grads[0]])
    other_small = jnp.concatenate(
        [back_to_place(grads[1][2]), back_to_place(grads[1][3]), back_to_place(up_bias_grads[1])]
    )
    shared = jnp.concatenate(
        [grad_gain_one, grad_shift_one, grad_out_bias, grad_gain_two, grad_shift_two, grad_down_bias]
    )
    far = across(jnp.concatenate([other_small, shared]))
    vec = jnp.concatenate([own_small, shared]) + far
    vec = total_over(vec, (CORE, XBIT, ZLOW, ZHIGH))
    grad_query_bias = vec[:width]
    grad_value_bias = vec[width : 2 * width]
    grad_up_bias = vec[2 * width : 2 * width + hidden]
    (
        grad_gain_one,
        grad_shift_one,
        grad_out_bias,
        grad_gain_two,
        grad_shift_two,
        grad_down_bias,
    ) = jnp.split(vec[2 * width + hidden :], 6)
    return (
        layer_out,
        grad_in,
        grad_gain_one,
        grad_shift_one,
        grad_query_weight,
        grad_query_bias,
        grad_key_weight,
        grad_value_weight,
        grad_value_bias,
        grad_out_weight,
        grad_out_bias,
        grad_gain_two,
        grad_shift_two,
        grad_up_weight,
        grad_up_bias,
        grad_down_weight,
        grad_down_bias,
    )


def solution(mesh):
    paired = mesh.shape["mp"] == 2 and mesh.shape["dp"] == 16
    body = paired_body if paired else general_body
    placed = (
        P(("dp", "mp"), None),
        P("dp"),
        P(),
        P(),
        P(None, "mp"),
        P("mp"),
        P(None, "mp"),
        P(None, "mp"),
        P("mp"),
        P("mp", None),
        P(),
        P(),
        P(),
        P(None, "mp"),
        P("mp"),
        P("mp", None),
        P(),
        P(("dp", "mp"), None),
    )
    return jax.shard_map(
        body,
        mesh=mesh,
        in_specs=placed,
        out_specs=(
            P(("dp", "mp"), None),
            P(("dp", "mp"), None),
            P(),
            P(),
            P(None, "mp"),
            P("mp"),
            P(None, "mp"),
            P(None, "mp"),
            P("mp"),
            P("mp", None),
            P(),
            P(),
            P(),
            P(None, "mp"),
            P("mp"),
            P("mp", None),
            P(),
        ),
        check_vma=False,
    )
```

```python
import functools

import jax
import jax.numpy as jnp
from jax import lax
from jax.experimental import pallas as pl
from jax.experimental.pallas import tpu as pltpu
from jax.sharding import PartitionSpec as P

HEAD_DIM = 64
TEXT = 40
SEQ = 280


EPS = 1e-05
SCALE = 0.125
NEGATIVE = -1e30


def layer_norm(values, gain, shift):
    center = values - jnp.mean(values, -1, keepdims=True)
    spread = jnp.mean(center * center, -1, keepdims=True)
    return center * lax.rsqrt(spread + EPS) * gain + shift


def exact_gelu(values):
    return jax.nn.gelu(values, approximate=False)


def matmul_rows(left, right):
    return jnp.dot(left, right, preferred_element_type=jnp.float32)


def contract_rows(left, right):
    return lax.dot_general(
        left, right, (((0,), (0,)), ((), ())), preferred_element_type=jnp.float32
    )


def contract_cols(left, right):
    return lax.dot_general(
        left, right, (((1,), (1,)), ((), ())), preferred_element_type=jnp.float32
    )


def column_sum(values):
    return jnp.sum(values.astype(jnp.float32), 0)


def general_body(
    layer_in,
    patch_count,
    attn_gain,
    attn_shift,
    query_weight,
    query_bias,
    key_weight,
    value_weight,
    value_bias,
    out_weight,
    out_bias,
    mlp_gain,
    mlp_shift,
    up_weight,
    up_bias,
    down_weight,
    down_bias,
    layer_cot,
):
    lowtype = jnp.bfloat16
    wide = jnp.float32
    rows_in = layer_in.astype(wide)
    gain_one = attn_gain.astype(wide)
    shift_one = attn_shift.astype(wide)
    gain_two = mlp_gain.astype(wide)
    shift_two = mlp_shift.astype(wide)
    normed_tok, norm_pull = jax.vjp(layer_norm, rows_in, gain_one, shift_one)
    group_rows = lax.all_gather(normed_tok.astype(lowtype), "mp", axis=0, tiled=True)
    query_rows = (matmul_rows(group_rows, query_weight) + query_bias.astype(wide)).astype(lowtype)
    key_rows = matmul_rows(group_rows, key_weight).astype(lowtype)
    value_rows = (matmul_rows(group_rows, value_weight) + value_bias.astype(wide)).astype(lowtype)
    pairs = patch_count.shape[0]
    local_width = query_weight.shape[1]
    local_heads = local_width // HEAD_DIM
    group_total = group_rows.shape[0]
    shape_four = (pairs, SEQ, local_heads, HEAD_DIM)
    query_blk = query_rows.reshape(shape_four)
    key_blk = key_rows.reshape(shape_four)
    value_blk = value_rows.reshape(shape_four)
    scores = jnp.einsum("pqhd,pkhd->phqk", query_blk, key_blk, preferred_element_type=wide) * SCALE
    valid = jnp.arange(SEQ)[None, :] < (TEXT + patch_count)[:, None]
    scores = jnp.where(valid[:, None, None, :], scores, NEGATIVE)
    probs = jax.nn.softmax(scores, axis=-1)
    probs_low = probs.astype(lowtype)
    context = jnp.einsum("phqk,pkhd->pqhd", probs_low, value_blk, preferred_element_type=wide)
    context = context.astype(lowtype).reshape(group_total, local_width)
    context_tok = lax.all_to_all(context, "mp", split_axis=0, concat_axis=1, tiled=True)
    out_full = lax.all_gather(out_weight, "mp", axis=0, tiled=True)
    attended = matmul_rows(context_tok, out_full) + out_bias.astype(wide)
    middle = rows_in + attended
    hidden_wide, mlp_pull = jax.vjp(layer_norm, middle, gain_two, shift_two)
    hidden_in = hidden_wide.astype(lowtype)
    cot_wide = layer_cot.astype(wide)
    up_full, bias_full, down_full = (
        lax.all_gather(up_weight, "mp", axis=1, tiled=True),
        lax.all_gather(up_bias, "mp", axis=0, tiled=True),
        lax.all_gather(down_weight, "mp", axis=0, tiled=True),
    )
    pre_act = matmul_rows(hidden_in, up_full) + bias_full.astype(wide)
    act_wide, gelu_pull = jax.vjp(exact_gelu, pre_act)
    act_low = act_wide.astype(lowtype)
    ffn_out = matmul_rows(act_low, down_full) + down_bias.astype(wide)
    whole_down = contract_rows(act_low, layer_cot)
    act_grad = contract_cols(layer_cot, down_full)
    pre_grad = gelu_pull(act_grad)[0].astype(lowtype)
    whole_up_bias = column_sum(pre_grad)
    whole_up = contract_rows(hidden_in, pre_grad)
    hidden_grad = contract_cols(pre_grad, up_full)
    grad_up_weight, grad_up_bias, grad_down_weight = (
        lax.psum_scatter(
            whole_up.astype(jnp.bfloat16), "mp", scatter_dimension=1, tiled=True
        ).astype(jnp.float32),
        lax.psum_scatter(
            whole_up_bias.astype(jnp.bfloat16), "mp", scatter_dimension=0, tiled=True
        ).astype(jnp.float32),
        lax.psum_scatter(
            whole_down.astype(jnp.bfloat16), "mp", scatter_dimension=0, tiled=True
        ).astype(jnp.float32),
    )
    layer_out = (middle + ffn_out).astype(lowtype)
    grad_down_bias = column_sum(layer_cot)
    middle_part, grad_gain_two, grad_shift_two = mlp_pull(hidden_grad)
    middle_grad = cot_wide + middle_part
    attn_grad = middle_grad.astype(lowtype)
    grad_out_bias = column_sum(attn_grad)
    grad_out_weight = lax.psum_scatter(
        contract_rows(context_tok, attn_grad).astype(jnp.bfloat16),
        "mp",
        scatter_dimension=0,
        tiled=True,
    ).astype(jnp.float32)
    context_grad_tok = contract_cols(attn_grad, out_full).astype(lowtype)
    context_grad = lax.all_to_all(
        context_grad_tok, "mp", split_axis=1, concat_axis=0, tiled=True
    ).reshape(shape_four)
    probs_grad = jnp.einsum("pqhd,pkhd->phqk", context_grad, value_blk, preferred_element_type=wide)
    value_grad = jnp.einsum("phqk,pqhd->pkhd", probs_low, context_grad, preferred_element_type=wide)
    value_grad = value_grad.astype(lowtype).reshape(group_total, local_width)
    score_grad = (probs * (probs_grad - jnp.sum(probs * probs_grad, -1, keepdims=True))).astype(
        lowtype
    )
    query_grad = (
        jnp.einsum("phqk,pkhd->pqhd", score_grad, key_blk, preferred_element_type=wide) * SCALE
    )
    query_grad = query_grad.astype(lowtype).reshape(group_total, local_width)
    key_grad = (
        jnp.einsum("phqk,pqhd->pkhd", score_grad, query_blk, preferred_element_type=wide) * SCALE
    )
    key_grad = key_grad.astype(lowtype).reshape(group_total, local_width)
    grad_query_weight = contract_rows(group_rows, query_grad)
    grad_key_weight = contract_rows(group_rows, key_grad)
    grad_value_weight = contract_rows(group_rows, value_grad)
    grad_query_bias = column_sum(query_grad)
    grad_value_bias = column_sum(value_grad)
    total = contract_cols(query_grad, query_weight)
    total = total + contract_cols(key_grad, key_weight)
    normed_grad = lax.psum_scatter(
        (total + contract_cols(value_grad, value_weight)).astype(jnp.bfloat16),
        "mp",
        scatter_dimension=0,
        tiled=True,
    ).astype(jnp.float32)
    input_part, grad_gain_one, grad_shift_one = norm_pull(normed_grad)
    grad_in = (middle_grad + input_part).astype(lowtype)
    (
        grad_query_weight,
        grad_query_bias,
        grad_key_weight,
        grad_value_weight,
        grad_value_bias,
        grad_out_weight,
        grad_up_weight,
        grad_up_bias,
        grad_down_weight,
    ) = (
        lax.psum(grad_query_weight.astype(jnp.bfloat16), "dp").astype(jnp.float32),
        lax.psum(grad_query_bias.astype(jnp.bfloat16), "dp").astype(jnp.float32),
        lax.psum(grad_key_weight.astype(jnp.bfloat16), "dp").astype(jnp.float32),
        lax.psum(grad_value_weight.astype(jnp.bfloat16), "dp").astype(jnp.float32),
        lax.psum(grad_value_bias.astype(jnp.bfloat16), "dp").astype(jnp.float32),
        lax.psum(grad_out_weight.astype(jnp.bfloat16), "dp").astype(jnp.float32),
        lax.psum(grad_up_weight.astype(jnp.bfloat16), "dp").astype(jnp.float32),
        lax.psum(grad_up_bias.astype(jnp.bfloat16), "dp").astype(jnp.float32),
        lax.psum(grad_down_weight.astype(jnp.bfloat16), "dp").astype(jnp.float32),
    )
    grad_gain_one, grad_shift_one, grad_out_bias, grad_gain_two, grad_shift_two, grad_down_bias = (
        lax.psum(
            (
                grad_gain_one,
                grad_shift_one,
                grad_out_bias,
                grad_gain_two,
                grad_shift_two,
                grad_down_bias,
            ),
            ("dp", "mp"),
        )
    )
    return (
        layer_out,
        grad_in,
        grad_gain_one,
        grad_shift_one,
        grad_query_weight,
        grad_query_bias,
        grad_key_weight,
        grad_value_weight,
        grad_value_bias,
        grad_out_weight,
        grad_out_bias,
        grad_gain_two,
        grad_shift_two,
        grad_up_weight,
        grad_up_bias,
        grad_down_weight,
        grad_down_bias,
    )


WIDE = jnp.float32
LOW = jnp.bfloat16
LANES = 128
ROOT_HALF = 0.7071067811865476
NORMAL = 0.3989422804014327
CORE, XBIT, ZLOW, ZHIGH = 1, 2, 4, 8


def dot(left, right, left_dim, right_dim):
    return lax.dot_general(
        left, right, (((left_dim,), (right_dim,)), ((), ())), preferred_element_type=WIDE
    )


def flip(value, axis, bit, size):
    return lax.ppermute(value, axis, [(i, i ^ bit) for i in range(size)])


def pick(value, index, width, axis):
    return lax.dynamic_slice_in_dim(value, index * width, width, axis)


def after(value, *others):
    return lax.optimization_barrier((value,) + others)[0]


def total(*items):
    result = items[0].astype(WIDE)
    for item in items[1:]:
        result = result + item.astype(WIDE)
    return result.astype(LOW)


def resident(shape):
    return pl.BlockSpec(shape, lambda *_: (0,) * len(shape), pipeline_mode=pl.Buffered(1))


ANYWHERE = pl.BlockSpec(memory_space=pl.ANY)


def attend_kernel(spot_ref, count_ref, rows_ref, *refs):
    weights, biases, outs = refs[:6], refs[6:10], refs[10:12]
    qkv_ref, context_ref, weight_ref, out_ref, bias_ref = refs[-5:]
    pair = pl.program_id(0)

    @pl.when(pair == 0)
    def _():
        for i in range(6):
            weight_ref[0, :, i * LANES : (i + 1) * LANES] = weights[i][...]
        bias_ref[...] = jnp.zeros_like(bias_ref)
        for i in range(2):
            out_ref[0, i * LANES : (i + 1) * LANES, :] = outs[i][...]
            bias_ref[:, i * LANES : (i + 1) * LANES] = biases[i][...].astype(WIDE)
            bias_ref[:, (4 + i) * LANES : (5 + i) * LANES] = biases[2 + i][...].astype(WIDE)

    qkv = (dot(rows_ref[0], weight_ref[0], 1, 0) + bias_ref[...]).astype(LOW)
    qkv_ref[0, 0] = qkv
    length = TEXT + count_ref[pair]
    lane = lax.broadcasted_iota(jnp.int32, (SEQ, LANES), 1)
    padding = lax.broadcasted_iota(jnp.int32, (SEQ, SEQ), 1) >= length
    for tile in range(2):
        query, key, value = (
            qkv[:, i * 256 + tile * LANES : i * 256 + (tile + 1) * LANES] for i in range(3)
        )
        heads = []
        for side in range(2):
            mine = (lane < HEAD_DIM) if side == 0 else (lane >= HEAD_DIM)
            scores = dot(jnp.where(mine, query, jnp.zeros_like(query)), key, 1, 1) * SCALE
            scores = jnp.where(padding, NEGATIVE, scores)
            power = jnp.exp(scores - jnp.max(scores, -1, keepdims=True))
            probs = power * (1.0 / jnp.sum(power, -1, keepdims=True))
            heads.append(dot(probs.astype(LOW), value, 1, 0))
        context_ref[0, 0, :, tile * LANES : (tile + 1) * LANES] = jnp.where(
            lane < HEAD_DIM, heads[0], heads[1]
        ).astype(LOW)


def attend(slot, spots, counts, rows, weights, biases, outs, buffers):
    pairs, seq, width = rows.shape
    shapes = [
        ((4, pairs, seq, 768), (1, 1, seq, 768), lambda p, *_: (slot, p, 0, 0)),
        ((4, pairs, seq, 256), (1, 1, seq, 256), lambda p, *_: (slot, p, 0, 0)),
        ((4, width, 768), (1, width, 768), lambda p, *_: (slot, 0, 0)),
        ((4, 256, width), (1, 256, width), lambda p, *_: (slot, 0, 0)),
    ]
    operands = list(weights) + list(biases) + list(outs)
    aliases = {}
    if buffers:
        aliases = {3 + len(operands) + i: i for i in range(4)}
    return pl.pallas_call(
        attend_kernel,
        grid_spec=pltpu.PrefetchScalarGridSpec(
            num_scalar_prefetch=2,
            grid=(pairs,),
            in_specs=[pl.BlockSpec((1, seq, width), lambda p, *_: (p, 0, 0))]
            + [spec for _, spec in operands]
            + [ANYWHERE] * len(buffers),
            out_specs=[pl.BlockSpec(block, index) for _, block, index in shapes],
            scratch_shapes=[pltpu.VMEM((1, 768), WIDE)],
        ),
        out_shape=[jax.ShapeDtypeStruct(shape, LOW) for shape, _, _ in shapes],
        input_output_aliases=aliases,
        name="attend",
        compiler_params=pltpu.CompilerParams(vmem_limit_bytes=56 * 1024 * 1024),
    )(spots, counts, rows, *[array for array, _ in operands], *buffers)


def attend_back_kernel(count_ref, rows_ref, cot_ref, qkv_ref, context_ref, weight_ref, out_ref, *refs):
    near_ref, bias_ref, qkv_grad_ref, grad_buf, context_buf = refs[-5:]
    pair = pl.program_id(0)
    at = pl.ds(pl.multiple_of(pair * SEQ, 8), SEQ)
    cot = cot_ref[at, :].astype(LOW)
    context_grad = dot(cot, out_ref[0], 1, 1).astype(LOW)
    qkv = qkv_ref[0, 0]
    context_buf[at, :] = context_ref[0, 0].astype(WIDE)
    length = TEXT + count_ref[pair]
    lane = lax.broadcasted_iota(jnp.int32, (SEQ, LANES), 1)
    padding = lax.broadcasted_iota(jnp.int32, (SEQ, SEQ), 0) >= length
    grads = [[], [], []]
    for tile in range(2):
        query, key, value = (
            qkv[:, i * 256 + tile * LANES : i * 256 + (tile + 1) * LANES] for i in range(3)
        )
        outer = context_grad[:, tile * LANES : (tile + 1) * LANES]
        heads = [[], [], []]
        for side in range(2):
            mine = (lane < HEAD_DIM) if side == 0 else (lane >= HEAD_DIM)
            scores = dot(jnp.where(mine, key, jnp.zeros_like(key)), query, 1, 1) * SCALE
            scores = jnp.where(padding, NEGATIVE, scores)
            power = jnp.exp(scores - jnp.max(scores, 0, keepdims=True))
            probs = power * (1.0 / jnp.sum(power, 0, keepdims=True))
            probs_grad = dot(jnp.where(mine, value, jnp.zeros_like(value)), outer, 1, 1)
            both = probs * probs_grad
            score_grad = (both - probs * jnp.sum(both, 0, keepdims=True)).astype(LOW)
            heads[0].append(dot(score_grad, key, 0, 0))
            heads[1].append(dot(score_grad, query, 1, 0))
            heads[2].append(dot(probs.astype(LOW), outer, 1, 0))
        for i, scale in enumerate((SCALE, SCALE, 1.0)):
            grads[i].append((jnp.where(lane < HEAD_DIM, *heads[i]) * scale).astype(LOW))
    joined = jnp.concatenate(grads[0] + grads[1] + grads[2], 1)
    qkv_grad_ref[0, 0] = joined
    grad_buf[at, :] = joined.astype(WIDE)

    @pl.when(pair == pl.num_programs(0) - 1)
    def _():
        stacked = dot(grad_buf[...].astype(LOW), rows_ref[...], 0, 0).astype(LOW)
        near_ref[:3] = stacked.reshape(3, 2, LANES, -1)
        outs = dot(context_buf[...].astype(LOW), cot_ref[...].astype(LOW), 0, 0).astype(LOW)
        near_ref[3] = outs.reshape(2, LANES, -1)
        bias_ref[...] = jnp.sum(grad_buf[...], 0, keepdims=True)


def attend_back(slot, counts, rows, cot, kept, buffers):
    qkv, context, weights, outs = kept
    _, pairs, seq, _ = qkv.shape
    width = rows.shape[1]
    return pl.pallas_call(
        attend_back_kernel,
        grid_spec=pltpu.PrefetchScalarGridSpec(
            num_scalar_prefetch=1,
            grid=(pairs,),
            in_specs=[
                resident(rows.shape),
                resident(cot.shape),
                pl.BlockSpec((1, 1, seq, 768), lambda p, *_: (slot, p, 0, 0)),
                pl.BlockSpec((1, 1, seq, 256), lambda p, *_: (slot, p, 0, 0)),
                pl.BlockSpec((1, width, 768), lambda p, *_: (slot, 0, 0)),
                pl.BlockSpec((1, 256, width), lambda p, *_: (slot, 0, 0)),
            ]
            + [ANYWHERE] * len(buffers),
            out_specs=[
                pl.BlockSpec((4, 2, LANES, width), lambda p, *_: (0, 0, 0, 0)),
                pl.BlockSpec((1, 768), lambda p, *_: (0, 0)),
                pl.BlockSpec((1, 1, seq, 768), lambda p, *_: (slot, p, 0, 0)),
            ],
            scratch_shapes=[
                pltpu.VMEM((pairs * seq, 768), WIDE),
                pltpu.VMEM((pairs * seq, 256), WIDE),
            ],
        ),
        out_shape=[
            jax.ShapeDtypeStruct((4, 2, LANES, width), LOW),
            jax.ShapeDtypeStruct((1, 768), WIDE),
            jax.ShapeDtypeStruct(qkv.shape, LOW),
        ],
        input_output_aliases={7: 2} if buffers else {},
        name="attend_back",
        compiler_params=pltpu.CompilerParams(vmem_limit_bytes=56 * 1024 * 1024),
    )(counts, rows, cot, qkv, context, weights, outs, *buffers)


def middle_kernel(rows_ref, context_ref, out_ref, bias_ref, gain_ref, shift_ref, middle_ref, hidden_ref):
    context = jnp.concatenate([context_ref[i, 0] for i in range(4)], 1)
    attended = dot(context, out_ref[...].reshape(-1, out_ref.shape[2]), 1, 0)
    middle = rows_ref[0].astype(WIDE) + attended + bias_ref[...].astype(WIDE)
    middle_ref[0] = middle
    center = middle - jnp.mean(middle, -1, keepdims=True)
    spread = jnp.mean(center * center, -1, keepdims=True)
    hidden = center * lax.rsqrt(spread + EPS) * gain_ref[...].astype(WIDE)
    hidden_ref[0] = (hidden + shift_ref[...].astype(WIDE)).astype(LOW)


def middle_step(rows, context, outs, bias, gain, shift):
    pairs, seq, width = rows.shape
    block = lambda: pl.BlockSpec((1, seq, width), lambda p: (p, 0, 0))
    return pl.pallas_call(
        middle_kernel,
        grid=(pairs,),
        in_specs=[
            block(),
            pl.BlockSpec((4, 1, seq, 256), lambda p: (0, p, 0, 0)),
            resident(outs.shape),
        ]
        + [resident((1, width))] * 3,
        out_specs=[block(), block()],
        out_shape=[
            jax.ShapeDtypeStruct(rows.shape, WIDE),
            jax.ShapeDtypeStruct(rows.shape, LOW),
        ],
        name="middle",
        compiler_params=pltpu.CompilerParams(vmem_limit_bytes=56 * 1024 * 1024),
    )(rows, context, outs, bias, gain, shift)


def mlp_kernel(step, spot_ref, hidden_ref, cot_ref, *refs):
    ups, downs, biases = refs[:4], refs[4:8], refs[8:12]
    near_a, far_a, near_b, far_b, bias_out, act_ref, pre_ref, up_ref, down_ref, bias_ref = refs[-10:]
    rows = hidden_ref.shape[0]
    for r in range(4):
        span = slice(r * LANES, (r + 1) * LANES)
        up_ref[0, :, span] = ups[r][...]
        down_ref[0, span, :] = downs[r][...]
        bias_ref[:, span] = biases[r][...].astype(WIDE)

    def one(i, carry):
        at = pl.ds(pl.multiple_of(i * step, step), step)
        pre_act = dot(hidden_ref[at, :], up_ref[0], 1, 0) + bias_ref[...]
        act_grad = dot(cot_ref[at, :], down_ref[0], 1, 1)
        chance = 0.5 + 0.5 * lax.erf(pre_act * ROOT_HALF)
        act_ref[0, at, :] = (pre_act * chance).astype(LOW)
        slope = chance + pre_act * (NORMAL * jnp.exp(-0.5 * pre_act * pre_act))
        pre_ref[0, at, :] = (act_grad * slope).astype(LOW)
        return carry

    lax.fori_loop(0, rows // step, one, 0)
    up_grad = dot(pre_ref[0], hidden_ref[...], 0, 0).astype(LOW).reshape(4, LANES, -1)
    down_grad = dot(act_ref[0], cot_ref[...], 0, 0).astype(LOW).reshape(4, LANES, -1)
    bias_out[0] = jnp.sum(pre_ref[0].astype(WIDE), 0, keepdims=True)
    for j, (near, far) in enumerate(((near_a, far_a), (near_b, far_b))):

        @pl.when(pl.program_id(0) == j)
        def _(near=near, far=far):
            near[0] = up_grad[:2]
            near[1] = down_grad[:2]
            far[0] = up_grad[2:]
            far[1] = down_grad[2:]


def mlp(first, spots, hidden, cot, ups, downs, biases, buffers):
    rows, width = hidden.shape
    operands = list(ups) + list(downs) + list(biases)
    tile = 4 * LANES
    grad = jax.ShapeDtypeStruct((2, 2, LANES, width), LOW)
    return pl.pallas_call(
        functools.partial(mlp_kernel, rows // 2),
        grid_spec=pltpu.PrefetchScalarGridSpec(
            num_scalar_prefetch=1,
            grid=(2,),
            in_specs=[resident(hidden.shape), resident(cot.shape)]
            + [spec for _, spec in operands]
            + [ANYWHERE] * len(buffers),
            out_specs=[resident(grad.shape)] * 4
            + [
                pl.BlockSpec((1, 1, tile), lambda j, *_: (j, 0, 0)),
                pl.BlockSpec((1, rows, tile), lambda j, *_: (first + j, 0, 0)),
                pl.BlockSpec((1, rows, tile), lambda j, *_: (first + j, 0, 0)),
                pl.BlockSpec((1, width, tile), lambda j, *_: (first + j, 0, 0)),
                pl.BlockSpec((1, tile, width), lambda j, *_: (first + j, 0, 0)),
            ],
            scratch_shapes=[pltpu.VMEM((1, tile), WIDE)],
        ),
        out_shape=[grad] * 4
        + [
            jax.ShapeDtypeStruct((2, 1, tile), WIDE),
            jax.ShapeDtypeStruct((8, rows, tile), LOW),
            jax.ShapeDtypeStruct((8, rows, tile), LOW),
            jax.ShapeDtypeStruct((8, width, tile), LOW),
            jax.ShapeDtypeStruct((8, tile, width), LOW),
        ],
        input_output_aliases={3 + len(operands) + i: 5 + i for i in range(len(buffers))},
        name="mlp",
        compiler_params=pltpu.CompilerParams(vmem_limit_bytes=56 * 1024 * 1024),
    )(spots, hidden, cot, *[array for array, _ in operands], *buffers)


def norm_back(values, gain, grad):
    center = values - jnp.mean(values, -1, keepdims=True)
    scale = lax.rsqrt(jnp.mean(center * center, -1, keepdims=True) + EPS)
    unit = center * scale
    inner = grad * gain
    pulled = scale * (
        inner
        - jnp.mean(inner, -1, keepdims=True)
        - unit * jnp.mean(inner * unit, -1, keepdims=True)
    )
    return pulled, jnp.sum(grad * unit, 0, keepdims=True), jnp.sum(grad, 0, keepdims=True)


def mlp_back_kernel(pre_ref, up_ref, middle_ref, cot_ref, gain_ref, grad_ref, sums_ref, sum_buf):
    step = pl.program_id(0)

    @pl.when(step == 0)
    def _():
        sum_buf[...] = dot(pre_ref[0], up_ref[0], 1, 1)

    @pl.when(step > 0)
    def _():
        sum_buf[...] += dot(pre_ref[0], up_ref[0], 1, 1)

    @pl.when(step == pl.num_programs(0) - 1)
    def _():
        sums_ref[...] = jnp.zeros_like(sums_ref)
        chunk = 224

        def one(i, carry):
            at = pl.ds(pl.multiple_of(i * chunk, chunk), chunk)
            cot = cot_ref[at, :].astype(WIDE)
            pulled, gain_grad, shift_grad = norm_back(
                middle_ref[at, :], gain_ref[...].astype(WIDE), sum_buf[at, :]
            )
            grad = cot + pulled
            grad_ref[at, :] = grad
            sums_ref[0:1, :] += gain_grad
            sums_ref[1:2, :] += shift_grad
            sums_ref[2:3, :] += jnp.sum(grad.astype(LOW).astype(WIDE), 0, keepdims=True)
            sums_ref[3:4, :] += jnp.sum(cot, 0, keepdims=True)
            return carry

        lax.fori_loop(0, grad_ref.shape[0] // chunk, one, 0)


def mlp_back(pre_grads, ups, middle, cot, gain):
    tiles, rows, tile = pre_grads.shape
    width = cot.shape[1]
    return pl.pallas_call(
        mlp_back_kernel,
        grid=(tiles,),
        in_specs=[
            pl.BlockSpec((1, rows, tile), lambda j: (j, 0, 0)),
            pl.BlockSpec((1, width, tile), lambda j: (j, 0, 0)),
            resident(middle.shape),
            resident(cot.shape),
            resident((1, width)),
        ],
        out_specs=[resident((rows, width)), resident((8, width))],
        out_shape=[
            jax.ShapeDtypeStruct((rows, width), WIDE),
            jax.ShapeDtypeStruct((8, width), WIDE),
        ],
        scratch_shapes=[pltpu.VMEM((rows, width), WIDE)],
        name="mlp_back",
        compiler_params=pltpu.CompilerParams(vmem_limit_bytes=56 * 1024 * 1024),
    )(pre_grads, ups, middle, cot, gain)


def mlp_out_kernel(act_ref, down_ref, middle_ref, bias_ref, out_ref, sum_buf):
    step = pl.program_id(0)

    @pl.when(step == 0)
    def _():
        sum_buf[...] = middle_ref[...] + bias_ref[...].astype(WIDE)

    sum_buf[...] += dot(act_ref[0], down_ref[0], 1, 0)

    @pl.when(step == pl.num_programs(0) - 1)
    def _():
        out_ref[...] = sum_buf[...].astype(LOW)


def mlp_out(acts, downs, middle, bias):
    tiles, rows, tile = acts.shape
    width = middle.shape[1]
    return pl.pallas_call(
        mlp_out_kernel,
        grid=(tiles,),
        in_specs=[
            pl.BlockSpec((1, rows, tile), lambda j: (j, 0, 0)),
            pl.BlockSpec((1, tile, width), lambda j: (j, 0, 0)),
            resident(middle.shape),
            resident((1, width)),
        ],
        out_specs=resident((rows, width)),
        out_shape=jax.ShapeDtypeStruct((rows, width), LOW),
        scratch_shapes=[pltpu.VMEM((rows, width), WIDE)],
        name="mlp_out",
        compiler_params=pltpu.CompilerParams(vmem_limit_bytes=56 * 1024 * 1024),
    )(acts, downs, middle, bias)


def input_kernel(grad_ref, weight_ref, rows_ref, above_ref, gain_ref, out_ref, sums_ref):
    pulled_sum = dot(grad_ref[0, 0], weight_ref[0], 1, 1)
    for i in range(1, 4):
        pulled_sum = pulled_sum + dot(grad_ref[i, 0], weight_ref[i], 1, 1)
    pulled, gain_grad, shift_grad = norm_back(
        rows_ref[0].astype(WIDE), gain_ref[...].astype(WIDE), pulled_sum
    )
    out_ref[0] = (above_ref[0] + pulled).astype(LOW)

    @pl.when(pl.program_id(0) == 0)
    def _():
        sums_ref[...] = jnp.zeros_like(sums_ref)

    sums_ref[0:1, :] += gain_grad
    sums_ref[1:2, :] += shift_grad


def input_step(grads, weights, rows, above, gain):
    pairs, seq, width = rows.shape
    block = lambda: pl.BlockSpec((1, seq, width), lambda p: (p, 0, 0))
    return pl.pallas_call(
        input_kernel,
        grid=(pairs,),
        in_specs=[
            pl.BlockSpec((4, 1, seq, 768), lambda p: (0, p, 0, 0)),
            resident(weights.shape),
            block(),
            block(),
            resident((1, width)),
        ],
        out_specs=[block(), resident((8, width))],
        out_shape=[
            jax.ShapeDtypeStruct(rows.shape, LOW),
            jax.ShapeDtypeStruct((8, width), WIDE),
        ],
        name="input_grad",
        compiler_params=pltpu.CompilerParams(vmem_limit_bytes=56 * 1024 * 1024),
    )(grads, weights, rows, above, gain)


def place_kernel(turned, spot_ref, near_ref, far_ref, *refs):
    outs = refs[-len(turned) :]
    core = pl.program_id(1) ^ spot_ref[0]
    for i, turn in enumerate(turned):
        parts = []
        for z in range(4):
            at = z ^ spot_ref[2]
            parts.append(
                jnp.where(core == 0, near_ref[at, i].astype(WIDE), far_ref[at, i].astype(WIDE))
            )
        block = jnp.concatenate(parts, 0)
        outs[i][...] = block.T if turn else block


def place(turned, chunk, chunks, spots, near, far, shapes, buffers):
    _, kinds, rows, width = near.shape
    source = lambda: pl.BlockSpec(
        (4, kinds, rows, width), lambda x, c, spot: (x ^ spot[1], 0, 0, 0)
    )
    specs = [
        pl.BlockSpec((width, LANES), lambda x, c, spot: (0, (c * 2 + x) * chunks + chunk))
        if turn
        else pl.BlockSpec((LANES, width), lambda x, c, spot: ((c * 2 + x) * chunks + chunk, 0))
        for turn in turned
    ]
    return pl.pallas_call(
        functools.partial(place_kernel, turned),
        grid_spec=pltpu.PrefetchScalarGridSpec(
            num_scalar_prefetch=1,
            grid=(2, 2),
            in_specs=[source(), source()] + [ANYWHERE] * len(buffers),
            out_specs=specs,
        ),
        out_shape=[jax.ShapeDtypeStruct(shape, WIDE) for shape in shapes],
        input_output_aliases={3 + i: i for i in range(len(buffers))},
        name="place",
        compiler_params=pltpu.CompilerParams(vmem_limit_bytes=56 * 1024 * 1024),
    )(spots, near, far, *buffers)


def paired_body(
    layer_in,
    patch_count,
    attn_gain,
    attn_shift,
    query_weight,
    query_bias,
    key_weight,
    value_weight,
    value_bias,
    out_weight,
    out_bias,
    mlp_gain,
    mlp_shift,
    up_weight,
    up_bias,
    down_weight,
    down_bias,
    layer_cot,
):
    groups = lax.axis_size("dp")
    rank = lax.axis_index("dp")
    half_id = lax.axis_index("mp")
    core_id, x_id, zlow_id, zhigh_id = rank & 1, (rank >> 1) & 1, (rank >> 2) & 1, (rank >> 3) & 1
    part = core_id * 2 + x_id
    spots = jnp.stack([part, part ^ 1, part ^ 2, part ^ 3]).astype(jnp.int32)
    sides = jnp.stack([x_id, x_id ^ 1, x_id, x_id ^ 1]).astype(jnp.int32)
    place_spots = jnp.stack([core_id, x_id, zlow_id * 2 + zhigh_id]).astype(jnp.int32)

    swap = lambda value, bit: flip(value, "dp", bit, groups)
    across = lambda value: flip(value, "mp", 1, 2)

    rows, width = layer_in.shape
    heads_width = query_weight.shape[1]
    hidden_width = up_weight.shape[1]
    block = hidden_width // 4
    pairs = rows // SEQ
    counts = pick(patch_count, half_id, pairs, 0)
    row_vec = lambda vec: vec.reshape(1, -1)

    near_qkv = across(
        jnp.stack([pick(w, core_id, heads_width // 2, 1) for w in (query_weight, key_weight, value_weight)])
    )
    bias_other = across(jnp.concatenate([query_bias, value_bias, up_bias]))
    query_bias_other = row_vec(bias_other[:heads_width])
    value_bias_other = row_vec(bias_other[heads_width : 2 * heads_width])
    up_bias_other = row_vec(bias_other[2 * heads_width :])

    rows_in = layer_in.astype(WIDE)
    normed = layer_norm(
        rows_in, attn_gain.astype(WIDE), attn_shift.astype(WIDE)
    ).astype(LOW)
    shape_three = (pairs, SEQ, width)
    normed_three = normed.reshape(shape_three)

    def own_inputs(group):
        weights = [
            (w, pl.BlockSpec((width, LANES), lambda p, spot, count, i=i: (0, spot[2 * group + i])))
            for w in (query_weight, key_weight, value_weight)
            for i in range(2)
        ]
        biases = [
            (row_vec(b), pl.BlockSpec((1, LANES), lambda p, spot, count, i=i: (0, spot[2 * group + i])))
            for b in (query_bias, value_bias)
            for i in range(2)
        ]
        outs = [
            (out_weight, pl.BlockSpec((LANES, width), lambda p, spot, count, i=i: (spot[2 * group + i], 0)))
            for i in range(2)
        ]
        return weights, biases, outs

    kept = attend(0, spots, counts, normed_three, *own_inputs(0), [])
    kept = attend(1, spots, counts, normed_three, *own_inputs(1), kept)

    far_qkv = swap(near_qkv, CORE)
    out_near = across(after(pick(out_weight, part, heads_width // 4, 0), near_qkv))
    half = block // 2
    eighth = part * 2 + zlow_id
    up_near = across(after(pick(up_weight, eighth, half, 1), near_qkv))
    down_near = across(after(pick(down_weight, eighth, half, 0), near_qkv))
    out_side = swap(out_near, XBIT)
    out_pieces = [out_near, out_side, swap(out_near, CORE), swap(out_side, CORE)]

    def other_inputs(group):
        source = (near_qkv, far_qkv)[group]
        weights = [
            (source, pl.BlockSpec((None, width, LANES), lambda p, side, count, k=k, i=i: (k, 0, side[i])))
            for k in range(3)
            for i in range(2)
        ]
        biases = [
            (b, pl.BlockSpec((1, LANES), lambda p, side, count, i=i: (0, side[4 + 2 * group + i])))
            for b in (query_bias_other, value_bias_other)
            for i in range(2)
        ]
        outs = [(out_pieces[2 * group + i], pl.BlockSpec((LANES, width), lambda p, side, count: (0, 0))) for i in range(2)]
        return weights, biases, outs

    other_spots = jnp.concatenate([sides, spots])
    kept = attend(2, other_spots, counts, normed_three, *other_inputs(0), kept)

    def pair_up(mine, axis):
        theirs = swap(mine, ZLOW)
        low_first = zlow_id == 0
        return jnp.concatenate(
            [jnp.where(low_first, mine, theirs), jnp.where(low_first, theirs, mine)], axis
        )

    up_mine, down_mine = pair_up(up_near, 1), pair_up(down_near, 0)
    kept = attend(3, other_spots, counts, normed_three, *other_inputs(1), kept)
    up_side, down_side = swap(up_mine, XBIT), swap(down_mine, XBIT)
    up_pieces = [up_mine, up_side, swap(up_mine, CORE), swap(up_side, CORE)]
    down_pieces = [down_mine, down_side, swap(down_mine, CORE), swap(down_side, CORE)]

    middle, hidden = middle_step(
        layer_in.reshape(shape_three),
        kept[1],
        kept[3],
        row_vec(out_bias),
        row_vec(mlp_gain),
        row_vec(mlp_shift),
    )
    middle = middle.reshape(rows, width)
    hidden = hidden.reshape(rows, width)
    subs = block // LANES

    def own_mlp(first):
        ups = [
            (up_weight, pl.BlockSpec((width, LANES), lambda j, spot, r=r: (0, spot[r] * subs + first + j)))
            for r in range(4)
        ]
        downs = [
            (down_weight, pl.BlockSpec((LANES, width), lambda j, spot, r=r: (spot[r] * subs + first + j, 0)))
            for r in range(4)
        ]
        biases = [
            (row_vec(up_bias), pl.BlockSpec((1, LANES), lambda j, spot, r=r: (0, spot[r] * subs + first + j)))
            for r in range(4)
        ]
        return ups, downs, biases

    def other_mlp(first):
        ups = [(piece, pl.BlockSpec((width, LANES), lambda j, spot: (0, first + j))) for piece in up_pieces]
        downs = [(piece, pl.BlockSpec((LANES, width), lambda j, spot: (first + j, 0))) for piece in down_pieces]
        biases = [
            (up_bias_other, pl.BlockSpec((1, LANES), lambda j, spot, r=r: (0, spot[r] * subs + first + j)))
            for r in range(4)
        ]
        return ups, downs, biases

    own_a = mlp(0, spots, hidden, layer_cot, *own_mlp(0), [])
    other_a = mlp(2, spots, hidden, layer_cot, *other_mlp(0), own_a[5:])
    own_b = mlp(4, spots, hidden, layer_cot, *own_mlp(2), other_a[5:])
    other_b = mlp(6, spots, hidden, layer_cot, *other_mlp(2), own_b[5:])
    acts, pre_grads, ups_all, downs_all = other_b[5:]

    def chain(other_near, other_far, own_near, own_far):
        outbound = total(other_near, swap(other_far, CORE))
        parts = (own_near, swap(own_far, CORE), across(outbound))

        def reduce():
            side = swap(total(*[item[:, 1] for item in parts]), XBIT)
            kinds, lanes, cols = side.shape
            cut = lambda item, index: pick(item.reshape(kinds, 2, lanes // 2, cols), index, 1, 1)[:, 0]
            items = [item[:, 0] for item in parts] + [side]
            sent = swap(total(*[cut(item, zlow_id ^ 1) for item in items]), ZLOW)
            two = total(*[cut(item, zlow_id) for item in items], sent)
            cut_two = lambda index: pick(two.reshape(kinds, 2, lanes // 4, cols), index, 1, 1)[:, 0]
            one = total(cut_two(zhigh_id), swap(cut_two(zhigh_id ^ 1), ZHIGH))
            have = one[None]
            for bit in (ZHIGH, ZLOW, XBIT):
                have = jnp.concatenate([have, swap(have, bit)])
            return have, swap(have, CORE)

        return reduce

    chains = [
        chain(other_a[0], other_a[1], own_a[0], own_a[1]),
        chain(other_a[2], other_a[3], own_a[2], own_a[3]),
        chain(other_b[0], other_b[1], own_b[0], own_b[1]),
        chain(other_b[2], other_b[3], own_b[2], own_b[3]),
    ]
    middle_grad, sums_two = mlp_back(pre_grads, ups_all, middle, layer_cot, row_vec(mlp_gain))
    other_far, bias_other_far, qkv_grads = attend_back(3, counts, normed, middle_grad, kept, [])
    other_near, bias_other_near, qkv_grads = attend_back(2, counts, normed, middle_grad, kept, [qkv_grads])
    own_far, bias_own_far, qkv_grads = attend_back(1, counts, normed, middle_grad, kept, [qkv_grads])
    own_near, bias_own_near, qkv_grads = attend_back(0, counts, normed, middle_grad, kept, [qkv_grads])
    late = [
        chain(other_near[i : i + 2], other_far[i : i + 2], own_near[i : i + 2], own_far[i : i + 2])
        for i in (0, 2)
    ]
    layer_out = mlp_out(acts, downs_all, middle, row_vec(down_bias))
    grad_in, sums_one = input_step(
        qkv_grads,
        kept[2],
        layer_in.reshape(shape_three),
        middle_grad.reshape(shape_three),
        row_vec(attn_gain),
    )
    up_shape, down_shape = up_weight.shape, down_weight.shape
    placed = []
    for i, finish in enumerate(chains):
        placed = place((True, False), i, subs, place_spots, *finish(), (up_shape, down_shape), placed)
    grad_up_weight, grad_down_weight = placed
    grad_query_weight, grad_key_weight = place(
        (True, True), 0, 1, place_spots, *late[0](), (query_weight.shape,) * 2, []
    )
    grad_value_weight, grad_out_weight = place(
        (True, False), 0, 1, place_spots, *late[1](), (value_weight.shape, out_weight.shape), []
    )

    def back_to_place(near, far):
        return jnp.concatenate([near, far]).reshape(4, -1)[jnp.arange(4) ^ part].reshape(-1)

    def up_bias_grad(first, second):
        sums = jnp.concatenate([first[4], second[4]]).reshape(4, 4, LANES).transpose(1, 0, 2)
        return sums[jnp.arange(4) ^ part].reshape(-1)

    def small(near, far, first, second):
        return jnp.concatenate(
            [
                back_to_place(near[0, :256], far[0, :256]),
                back_to_place(near[0, 512:], far[0, 512:]),
                up_bias_grad(first, second),
            ]
        )

    own_small = small(bias_own_near, bias_own_far, own_a, own_b)
    other_small = small(bias_other_near, bias_other_far, other_a, other_b)
    shared = jnp.concatenate([sums_one[0], sums_one[1], sums_two[2], sums_two[0], sums_two[1], sums_two[3]])
    vec = jnp.concatenate([own_small, shared]) + across(jnp.concatenate([other_small, shared]))
    for bit in (CORE, XBIT, ZLOW, ZHIGH):
        vec = vec + swap(vec, bit)
    grad_query_bias = vec[:heads_width]
    grad_value_bias = vec[heads_width : 2 * heads_width]
    grad_up_bias = vec[2 * heads_width : 2 * heads_width + hidden_width]
    (
        grad_attn_gain,
        grad_attn_shift,
        grad_out_bias,
        grad_mlp_gain,
        grad_mlp_shift,
        grad_down_bias,
    ) = jnp.split(vec[2 * heads_width + hidden_width :], 6)
    return (
        layer_out,
        grad_in.reshape(rows, width),
        grad_attn_gain,
        grad_attn_shift,
        grad_query_weight,
        grad_query_bias,
        grad_key_weight,
        grad_value_weight,
        grad_value_bias,
        grad_out_weight,
        grad_out_bias,
        grad_mlp_gain,
        grad_mlp_shift,
        grad_up_weight,
        grad_up_bias,
        grad_down_weight,
        grad_down_bias,
    )


def solution(mesh):
    paired = mesh.shape["mp"] == 2 and mesh.shape["dp"] == 16
    body = paired_body if paired else general_body
    placed = (
        P(("dp", "mp"), None),
        P("dp"),
        P(),
        P(),
        P(None, "mp"),
        P("mp"),
        P(None, "mp"),
        P(None, "mp"),
        P("mp"),
        P("mp", None),
        P(),
        P(),
        P(),
        P(None, "mp"),
        P("mp"),
        P("mp", None),
        P(),
        P(("dp", "mp"), None),
    )
    return jax.shard_map(
        body,
        mesh=mesh,
        in_specs=placed,
        out_specs=(
            P(("dp", "mp"), None),
            P(("dp", "mp"), None),
            P(),
            P(),
            P(None, "mp"),
            P("mp"),
            P(None, "mp"),
            P(None, "mp"),
            P("mp"),
            P("mp", None),
            P(),
            P(),
            P(),
            P(None, "mp"),
            P("mp"),
            P("mp", None),
            P(),
        ),
        check_vma=False,
    )
```

```python
import functools

import jax
import jax.numpy as jnp
from jax import lax
from jax.experimental import pallas as pl
from jax.experimental.pallas import tpu as pltpu
from jax.sharding import PartitionSpec as P

HEAD_DIM = 64
TEXT = 40
SEQ = 280


EPS = 1e-05
SCALE = 0.125
NEGATIVE = -1e30


def layer_norm(values, gain, shift):
    center = values - jnp.mean(values, -1, keepdims=True)
    spread = jnp.mean(center * center, -1, keepdims=True)
    return center * lax.rsqrt(spread + EPS) * gain + shift


def exact_gelu(values):
    return jax.nn.gelu(values, approximate=False)


def matmul_rows(left, right):
    return jnp.dot(left, right, preferred_element_type=jnp.float32)


def contract_rows(left, right):
    return lax.dot_general(
        left, right, (((0,), (0,)), ((), ())), preferred_element_type=jnp.float32
    )


def contract_cols(left, right):
    return lax.dot_general(
        left, right, (((1,), (1,)), ((), ())), preferred_element_type=jnp.float32
    )


def column_sum(values):
    return jnp.sum(values.astype(jnp.float32), 0)


def general_body(
    layer_in,
    patch_count,
    attn_gain,
    attn_shift,
    query_weight,
    query_bias,
    key_weight,
    value_weight,
    value_bias,
    out_weight,
    out_bias,
    mlp_gain,
    mlp_shift,
    up_weight,
    up_bias,
    down_weight,
    down_bias,
    layer_cot,
):
    lowtype = jnp.bfloat16
    wide = jnp.float32
    rows_in = layer_in.astype(wide)
    gain_one = attn_gain.astype(wide)
    shift_one = attn_shift.astype(wide)
    gain_two = mlp_gain.astype(wide)
    shift_two = mlp_shift.astype(wide)
    normed_tok, norm_pull = jax.vjp(layer_norm, rows_in, gain_one, shift_one)
    group_rows = lax.all_gather(normed_tok.astype(lowtype), "mp", axis=0, tiled=True)
    query_rows = (matmul_rows(group_rows, query_weight) + query_bias.astype(wide)).astype(lowtype)
    key_rows = matmul_rows(group_rows, key_weight).astype(lowtype)
    value_rows = (matmul_rows(group_rows, value_weight) + value_bias.astype(wide)).astype(lowtype)
    pairs = patch_count.shape[0]
    local_width = query_weight.shape[1]
    local_heads = local_width // HEAD_DIM
    group_total = group_rows.shape[0]
    shape_four = (pairs, SEQ, local_heads, HEAD_DIM)
    query_blk = query_rows.reshape(shape_four)
    key_blk = key_rows.reshape(shape_four)
    value_blk = value_rows.reshape(shape_four)
    scores = jnp.einsum("pqhd,pkhd->phqk", query_blk, key_blk, preferred_element_type=wide) * SCALE
    valid = jnp.arange(SEQ)[None, :] < (TEXT + patch_count)[:, None]
    scores = jnp.where(valid[:, None, None, :], scores, NEGATIVE)
    probs = jax.nn.softmax(scores, axis=-1)
    probs_low = probs.astype(lowtype)
    context = jnp.einsum("phqk,pkhd->pqhd", probs_low, value_blk, preferred_element_type=wide)
    context = context.astype(lowtype).reshape(group_total, local_width)
    context_tok = lax.all_to_all(context, "mp", split_axis=0, concat_axis=1, tiled=True)
    out_full = lax.all_gather(out_weight, "mp", axis=0, tiled=True)
    attended = matmul_rows(context_tok, out_full) + out_bias.astype(wide)
    middle = rows_in + attended
    hidden_wide, mlp_pull = jax.vjp(layer_norm, middle, gain_two, shift_two)
    hidden_in = hidden_wide.astype(lowtype)
    cot_wide = layer_cot.astype(wide)
    up_full, bias_full, down_full = (
        lax.all_gather(up_weight, "mp", axis=1, tiled=True),
        lax.all_gather(up_bias, "mp", axis=0, tiled=True),
        lax.all_gather(down_weight, "mp", axis=0, tiled=True),
    )
    pre_act = matmul_rows(hidden_in, up_full) + bias_full.astype(wide)
    act_wide, gelu_pull = jax.vjp(exact_gelu, pre_act)
    act_low = act_wide.astype(lowtype)
    ffn_out = matmul_rows(act_low, down_full) + down_bias.astype(wide)
    whole_down = contract_rows(act_low, layer_cot)
    act_grad = contract_cols(layer_cot, down_full)
    pre_grad = gelu_pull(act_grad)[0].astype(lowtype)
    whole_up_bias = column_sum(pre_grad)
    whole_up = contract_rows(hidden_in, pre_grad)
    hidden_grad = contract_cols(pre_grad, up_full)
    grad_up_weight, grad_up_bias, grad_down_weight = (
        lax.psum_scatter(
            whole_up.astype(jnp.bfloat16), "mp", scatter_dimension=1, tiled=True
        ).astype(jnp.float32),
        lax.psum_scatter(
            whole_up_bias.astype(jnp.bfloat16), "mp", scatter_dimension=0, tiled=True
        ).astype(jnp.float32),
        lax.psum_scatter(
            whole_down.astype(jnp.bfloat16), "mp", scatter_dimension=0, tiled=True
        ).astype(jnp.float32),
    )
    layer_out = (middle + ffn_out).astype(lowtype)
    grad_down_bias = column_sum(layer_cot)
    middle_part, grad_gain_two, grad_shift_two = mlp_pull(hidden_grad)
    middle_grad = cot_wide + middle_part
    attn_grad = middle_grad.astype(lowtype)
    grad_out_bias = column_sum(attn_grad)
    grad_out_weight = lax.psum_scatter(
        contract_rows(context_tok, attn_grad).astype(jnp.bfloat16),
        "mp",
        scatter_dimension=0,
        tiled=True,
    ).astype(jnp.float32)
    context_grad_tok = contract_cols(attn_grad, out_full).astype(lowtype)
    context_grad = lax.all_to_all(
        context_grad_tok, "mp", split_axis=1, concat_axis=0, tiled=True
    ).reshape(shape_four)
    probs_grad = jnp.einsum("pqhd,pkhd->phqk", context_grad, value_blk, preferred_element_type=wide)
    value_grad = jnp.einsum("phqk,pqhd->pkhd", probs_low, context_grad, preferred_element_type=wide)
    value_grad = value_grad.astype(lowtype).reshape(group_total, local_width)
    score_grad = (probs * (probs_grad - jnp.sum(probs * probs_grad, -1, keepdims=True))).astype(
        lowtype
    )
    query_grad = (
        jnp.einsum("phqk,pkhd->pqhd", score_grad, key_blk, preferred_element_type=wide) * SCALE
    )
    query_grad = query_grad.astype(lowtype).reshape(group_total, local_width)
    key_grad = (
        jnp.einsum("phqk,pqhd->pkhd", score_grad, query_blk, preferred_element_type=wide) * SCALE
    )
    key_grad = key_grad.astype(lowtype).reshape(group_total, local_width)
    grad_query_weight = contract_rows(group_rows, query_grad)
    grad_key_weight = contract_rows(group_rows, key_grad)
    grad_value_weight = contract_rows(group_rows, value_grad)
    grad_query_bias = column_sum(query_grad)
    grad_value_bias = column_sum(value_grad)
    total = contract_cols(query_grad, query_weight)
    total = total + contract_cols(key_grad, key_weight)
    normed_grad = lax.psum_scatter(
        (total + contract_cols(value_grad, value_weight)).astype(jnp.bfloat16),
        "mp",
        scatter_dimension=0,
        tiled=True,
    ).astype(jnp.float32)
    input_part, grad_gain_one, grad_shift_one = norm_pull(normed_grad)
    grad_in = (middle_grad + input_part).astype(lowtype)
    (
        grad_query_weight,
        grad_query_bias,
        grad_key_weight,
        grad_value_weight,
        grad_value_bias,
        grad_out_weight,
        grad_up_weight,
        grad_up_bias,
        grad_down_weight,
    ) = (
        lax.psum(grad_query_weight.astype(jnp.bfloat16), "dp").astype(jnp.float32),
        lax.psum(grad_query_bias.astype(jnp.bfloat16), "dp").astype(jnp.float32),
        lax.psum(grad_key_weight.astype(jnp.bfloat16), "dp").astype(jnp.float32),
        lax.psum(grad_value_weight.astype(jnp.bfloat16), "dp").astype(jnp.float32),
        lax.psum(grad_value_bias.astype(jnp.bfloat16), "dp").astype(jnp.float32),
        lax.psum(grad_out_weight.astype(jnp.bfloat16), "dp").astype(jnp.float32),
        lax.psum(grad_up_weight.astype(jnp.bfloat16), "dp").astype(jnp.float32),
        lax.psum(grad_up_bias.astype(jnp.bfloat16), "dp").astype(jnp.float32),
        lax.psum(grad_down_weight.astype(jnp.bfloat16), "dp").astype(jnp.float32),
    )
    grad_gain_one, grad_shift_one, grad_out_bias, grad_gain_two, grad_shift_two, grad_down_bias = (
        lax.psum(
            (
                grad_gain_one,
                grad_shift_one,
                grad_out_bias,
                grad_gain_two,
                grad_shift_two,
                grad_down_bias,
            ),
            ("dp", "mp"),
        )
    )
    return (
        layer_out,
        grad_in,
        grad_gain_one,
        grad_shift_one,
        grad_query_weight,
        grad_query_bias,
        grad_key_weight,
        grad_value_weight,
        grad_value_bias,
        grad_out_weight,
        grad_out_bias,
        grad_gain_two,
        grad_shift_two,
        grad_up_weight,
        grad_up_bias,
        grad_down_weight,
        grad_down_bias,
    )


WIDE = jnp.float32
LOW = jnp.bfloat16
LANES = 128
ROOT_HALF = 0.7071067811865476
NORMAL = 0.3989422804014327
CORE, XBIT, ZLOW, ZHIGH = 1, 2, 4, 8


def dot(left, right, left_dim, right_dim):
    return lax.dot_general(
        left, right, (((left_dim,), (right_dim,)), ((), ())), preferred_element_type=WIDE
    )


def flip(value, axis, bit, size):
    return lax.ppermute(value, axis, [(i, i ^ bit) for i in range(size)])


def pick(value, index, width, axis):
    return lax.dynamic_slice_in_dim(value, index * width, width, axis)


def after(value, *others):
    return lax.optimization_barrier((value,) + others)[0]


def total(*items):
    result = items[0].astype(WIDE)
    for item in items[1:]:
        result = result + item.astype(WIDE)
    return result.astype(LOW)


def resident(shape):
    return pl.BlockSpec(shape, lambda *_: (0,) * len(shape), pipeline_mode=pl.Buffered(1))


ANYWHERE = pl.BlockSpec(memory_space=pl.ANY)


def attend_kernel(spot_ref, count_ref, rows_ref, *refs):
    weights, biases = refs[:6], refs[6:10]
    qkv_ref, context_ref, weight_ref, bias_ref = refs[-4:]
    pair = pl.program_id(1)

    @pl.when(pair == 0)
    def _():
        for i in range(6):
            weight_ref[0, :, i * LANES : (i + 1) * LANES] = weights[i][...]
        bias_ref[...] = jnp.zeros_like(bias_ref)
        for i in range(2):
            bias_ref[:, i * LANES : (i + 1) * LANES] = biases[i][...].astype(WIDE)
            bias_ref[:, (4 + i) * LANES : (5 + i) * LANES] = biases[2 + i][...].astype(WIDE)

    qkv = (dot(rows_ref[0], weight_ref[0], 1, 0) + bias_ref[...]).astype(LOW)
    qkv_ref[0, 0] = qkv
    length = TEXT + count_ref[pair]
    lane = lax.broadcasted_iota(jnp.int32, (SEQ, LANES), 1)
    padding = lax.broadcasted_iota(jnp.int32, (SEQ, SEQ), 1) >= length
    for tile in range(2):
        query, key, value = (
            qkv[:, i * 256 + tile * LANES : i * 256 + (tile + 1) * LANES] for i in range(3)
        )
        heads = []
        for side in range(2):
            mine = (lane < HEAD_DIM) if side == 0 else (lane >= HEAD_DIM)
            scores = dot(jnp.where(mine, query, jnp.zeros_like(query)), key, 1, 1) * SCALE
            scores = jnp.where(padding, NEGATIVE, scores)
            power = jnp.exp(scores - jnp.max(scores, -1, keepdims=True))
            probs = power * (1.0 / jnp.sum(power, -1, keepdims=True))
            heads.append(dot(probs.astype(LOW), value, 1, 0))
        context_ref[0, 0, :, tile * LANES : (tile + 1) * LANES] = jnp.where(
            lane < HEAD_DIM, heads[0], heads[1]
        ).astype(LOW)


def attend(slot, groups, spots, counts, rows, weights, biases, buffers):
    pairs, seq, width = rows.shape
    shapes = [
        ((4, pairs, seq, 768), (1, 1, seq, 768), lambda g, p, *_: (slot + g, p, 0, 0)),
        ((4, pairs, seq, 256), (1, 1, seq, 256), lambda g, p, *_: (slot + g, p, 0, 0)),
        ((4, width, 768), (1, width, 768), lambda g, p, *_: (slot + g, 0, 0)),
    ]
    operands = list(weights) + list(biases)
    aliases = {3 + len(operands) + i: i for i in range(len(buffers))}
    return pl.pallas_call(
        attend_kernel,
        grid_spec=pltpu.PrefetchScalarGridSpec(
            num_scalar_prefetch=2,
            grid=(groups, pairs),
            in_specs=[pl.BlockSpec((1, seq, width), lambda g, p, *_: (p, 0, 0))]
            + [spec for _, spec in operands]
            + [ANYWHERE] * len(buffers),
            out_specs=[pl.BlockSpec(block, index) for _, block, index in shapes],
            scratch_shapes=[pltpu.VMEM((1, 768), WIDE)],
        ),
        out_shape=[jax.ShapeDtypeStruct(shape, LOW) for shape, _, _ in shapes],
        input_output_aliases=aliases,
        name="attend",
        compiler_params=pltpu.CompilerParams(vmem_limit_bytes=56 * 1024 * 1024),
    )(spots, counts, rows, *[array for array, _ in operands], *buffers)


def attend_back_kernel(count_ref, rows_ref, cot_ref, qkv_ref, context_ref, weight_ref, out_ref, *refs):
    near_ref, bias_ref, qkv_grad_ref, grad_buf, context_buf = refs[-5:]
    pair = pl.program_id(0)
    at = pl.ds(pl.multiple_of(pair * SEQ, 8), SEQ)
    cot = cot_ref[at, :].astype(LOW)
    context_grad = dot(cot, out_ref[0], 1, 1).astype(LOW)
    qkv = qkv_ref[0, 0]
    context_buf[at, :] = context_ref[0, 0].astype(WIDE)
    length = TEXT + count_ref[pair]
    lane = lax.broadcasted_iota(jnp.int32, (SEQ, LANES), 1)
    padding = lax.broadcasted_iota(jnp.int32, (SEQ, SEQ), 0) >= length
    grads = [[], [], []]
    for tile in range(2):
        query, key, value = (
            qkv[:, i * 256 + tile * LANES : i * 256 + (tile + 1) * LANES] for i in range(3)
        )
        outer = context_grad[:, tile * LANES : (tile + 1) * LANES]
        heads = [[], [], []]
        for side in range(2):
            mine = (lane < HEAD_DIM) if side == 0 else (lane >= HEAD_DIM)
            scores = dot(jnp.where(mine, key, jnp.zeros_like(key)), query, 1, 1) * SCALE
            scores = jnp.where(padding, NEGATIVE, scores)
            power = jnp.exp(scores - jnp.max(scores, 0, keepdims=True))
            probs = power * (1.0 / jnp.sum(power, 0, keepdims=True))
            probs_grad = dot(jnp.where(mine, value, jnp.zeros_like(value)), outer, 1, 1)
            both = probs * probs_grad
            score_grad = (both - probs * jnp.sum(both, 0, keepdims=True)).astype(LOW)
            heads[0].append(dot(score_grad, key, 0, 0))
            heads[1].append(dot(score_grad, query, 1, 0))
            heads[2].append(dot(probs.astype(LOW), outer, 1, 0))
        for i, scale in enumerate((SCALE, SCALE, 1.0)):
            grads[i].append((jnp.where(lane < HEAD_DIM, *heads[i]) * scale).astype(LOW))
    joined = jnp.concatenate(grads[0] + grads[1] + grads[2], 1)
    qkv_grad_ref[0, 0] = joined
    grad_buf[at, :] = joined.astype(WIDE)

    @pl.when(pair == pl.num_programs(0) - 1)
    def _():
        stacked = dot(grad_buf[...].astype(LOW), rows_ref[...], 0, 0).astype(LOW)
        for i in range(2):
            near_ref[i, :3] = stacked.reshape(3, 2, LANES, -1)[:, i]
        outs = dot(context_buf[...].astype(LOW), cot_ref[...].astype(LOW), 0, 0).astype(LOW)
        for i in range(2):
            near_ref[i, 3] = outs[i * LANES : (i + 1) * LANES]
        bias_ref[...] = jnp.sum(grad_buf[...], 0, keepdims=True)


def attend_back(slot, counts, rows, cot, kept, outs, buffers):
    qkv, context, weights = kept
    _, pairs, seq, _ = qkv.shape
    width = rows.shape[1]
    return pl.pallas_call(
        attend_back_kernel,
        grid_spec=pltpu.PrefetchScalarGridSpec(
            num_scalar_prefetch=1,
            grid=(pairs,),
            in_specs=[
                resident(rows.shape),
                resident(cot.shape),
                pl.BlockSpec((1, 1, seq, 768), lambda p, *_: (slot, p, 0, 0)),
                pl.BlockSpec((1, 1, seq, 256), lambda p, *_: (slot, p, 0, 0)),
                pl.BlockSpec((1, width, 768), lambda p, *_: (slot, 0, 0)),
                pl.BlockSpec((1, 256, width), lambda p, *_: (slot, 0, 0)),
            ]
            + [ANYWHERE] * len(buffers),
            out_specs=[
                pl.BlockSpec((2, 4, LANES, width), lambda p, *_: (0, 0, 0, 0)),
                pl.BlockSpec((1, 768), lambda p, *_: (0, 0)),
                pl.BlockSpec((1, 1, seq, 768), lambda p, *_: (slot, p, 0, 0)),
            ],
            scratch_shapes=[
                pltpu.VMEM((pairs * seq, 768), WIDE),
                pltpu.VMEM((pairs * seq, 256), WIDE),
            ],
        ),
        out_shape=[
            jax.ShapeDtypeStruct((2, 4, LANES, width), LOW),
            jax.ShapeDtypeStruct((1, 768), WIDE),
            jax.ShapeDtypeStruct(qkv.shape, LOW),
        ],
        input_output_aliases={7: 2} if buffers else {},
        name="attend_back",
        compiler_params=pltpu.CompilerParams(vmem_limit_bytes=56 * 1024 * 1024),
    )(counts, rows, cot, qkv, context, weights, outs, *buffers)


def middle_kernel(
    spot_ref, rows_ref, context_ref, own_ref, near_ref, far_ref, bias_ref, gain_ref, shift_ref, *refs
):
    middle_ref, hidden_ref, out_ref = refs

    @pl.when(pl.program_id(0) == 0)
    def _():
        for i in range(8):
            source = own_ref if i < 4 else (near_ref if i < 6 else far_ref)
            start = pl.multiple_of(spot_ref[i] * LANES, LANES)
            out_ref[i // 2, (i % 2) * LANES : (i % 2 + 1) * LANES, :] = source[pl.ds(start, LANES), :]

    context = jnp.concatenate([context_ref[i, 0] for i in range(4)], 1)
    attended = dot(context, out_ref[...].reshape(-1, out_ref.shape[2]), 1, 0)
    middle = rows_ref[0].astype(WIDE) + attended + bias_ref[...].astype(WIDE)
    middle_ref[0] = middle
    center = middle - jnp.mean(middle, -1, keepdims=True)
    spread = jnp.mean(center * center, -1, keepdims=True)
    hidden = center * lax.rsqrt(spread + EPS) * gain_ref[...].astype(WIDE)
    hidden_ref[0] = (hidden + shift_ref[...].astype(WIDE)).astype(LOW)


def middle_step(spots, rows, context, own, near, far, bias, gain, shift):
    pairs, seq, width = rows.shape
    block = lambda: pl.BlockSpec((1, seq, width), lambda p, *_: (p, 0, 0))
    return pl.pallas_call(
        middle_kernel,
        grid_spec=pltpu.PrefetchScalarGridSpec(
            num_scalar_prefetch=1,
            grid=(pairs,),
            in_specs=[
                block(),
                pl.BlockSpec((4, 1, seq, 256), lambda p, *_: (0, p, 0, 0)),
                resident(own.shape),
                resident(near.shape),
                resident(far.shape),
            ]
            + [resident((1, width))] * 3,
            out_specs=[block(), block(), resident((4, 256, width))],
        ),
        out_shape=[
            jax.ShapeDtypeStruct(rows.shape, WIDE),
            jax.ShapeDtypeStruct(rows.shape, LOW),
            jax.ShapeDtypeStruct((4, 256, width), LOW),
        ],
        name="middle",
        compiler_params=pltpu.CompilerParams(vmem_limit_bytes=56 * 1024 * 1024),
    )(spots, rows, context, own, near, far, bias, gain, shift)


def mlp_kernel(step, turned, spot_ref, hidden_ref, cot_ref, *refs):
    ups, downs, biases = refs[:4], refs[4:8], refs[8:12]
    near_ref, far_ref, bias_out, act_ref, pre_ref, up_ref, down_ref, bias_ref = refs[-8:]
    rows = hidden_ref.shape[0]
    for r in range(4):
        span = slice(r * LANES, (r + 1) * LANES)
        if turned:
            up_ref[0, :, span] = ups[r][:, 0].reshape(LANES, -1).T
            down_ref[0, span, :] = downs[r][:, 0].reshape(LANES, -1)
        else:
            up_ref[0, :, span] = ups[r][...]
            down_ref[0, span, :] = downs[r][...]
        bias_ref[:, span] = biases[r][...].astype(WIDE)

    def one(i, carry):
        at = pl.ds(pl.multiple_of(i * step, step), step)
        pre_act = dot(hidden_ref[at, :], up_ref[0], 1, 0) + bias_ref[...]
        act_grad = dot(cot_ref[at, :], down_ref[0], 1, 1)
        chance = 0.5 + 0.5 * lax.erf(pre_act * ROOT_HALF)
        act_ref[0, at, :] = (pre_act * chance).astype(LOW)
        slope = chance + pre_act * (NORMAL * jnp.exp(-0.5 * pre_act * pre_act))
        pre_ref[0, at, :] = (act_grad * slope).astype(LOW)
        return carry

    lax.fori_loop(0, rows // step, one, 0)
    up_grad = dot(pre_ref[0], hidden_ref[...], 0, 0).astype(LOW).reshape(4, LANES, -1)
    down_grad = dot(act_ref[0], cot_ref[...], 0, 0).astype(LOW).reshape(4, LANES, -1)
    bias_out[0] = jnp.sum(pre_ref[0].astype(WIDE), 0, keepdims=True)
    for i in range(2):
        near_ref[i, 0] = up_grad[i]
        near_ref[i, 1] = down_grad[i]
        far_ref[i, 0] = up_grad[2 + i]
        far_ref[i, 1] = down_grad[2 + i]


def mlp(first, turned, spots, hidden, cot, ups, downs, biases, buffers):
    rows, width = hidden.shape
    operands = list(ups) + list(downs) + list(biases)
    tile = 4 * LANES
    grad = jax.ShapeDtypeStruct((2, 4, LANES, width), LOW)
    grad_block = pl.BlockSpec((2, 2, LANES, width), lambda j, *_: (0, j, 0, 0))
    return pl.pallas_call(
        functools.partial(mlp_kernel, rows // 2, turned),
        grid_spec=pltpu.PrefetchScalarGridSpec(
            num_scalar_prefetch=1,
            grid=(2,),
            in_specs=[resident(hidden.shape), resident(cot.shape)]
            + [spec for _, spec in operands]
            + [ANYWHERE] * len(buffers),
            out_specs=[grad_block] * 2
            + [
                pl.BlockSpec((1, 1, tile), lambda j, *_: (j, 0, 0)),
                pl.BlockSpec((1, rows, tile), lambda j, *_: (first + j, 0, 0)),
                pl.BlockSpec((1, rows, tile), lambda j, *_: (first + j, 0, 0)),
                pl.BlockSpec((1, width, tile), lambda j, *_: (first + j, 0, 0)),
                pl.BlockSpec((1, tile, width), lambda j, *_: (first + j, 0, 0)),
            ],
            scratch_shapes=[pltpu.VMEM((1, tile), WIDE)],
        ),
        out_shape=[grad] * 2
        + [
            jax.ShapeDtypeStruct((2, 1, tile), WIDE),
            jax.ShapeDtypeStruct((8, rows, tile), LOW),
            jax.ShapeDtypeStruct((8, rows, tile), LOW),
            jax.ShapeDtypeStruct((8, width, tile), LOW),
            jax.ShapeDtypeStruct((8, tile, width), LOW),
        ],
        input_output_aliases={3 + len(operands) + i: 3 + i for i in range(len(buffers))},
        name="mlp",
        compiler_params=pltpu.CompilerParams(vmem_limit_bytes=56 * 1024 * 1024),
    )(spots, hidden, cot, *[array for array, _ in operands], *buffers)


def norm_back(values, gain, grad):
    center = values - jnp.mean(values, -1, keepdims=True)
    scale = lax.rsqrt(jnp.mean(center * center, -1, keepdims=True) + EPS)
    unit = center * scale
    inner = grad * gain
    pulled = scale * (
        inner
        - jnp.mean(inner, -1, keepdims=True)
        - unit * jnp.mean(inner * unit, -1, keepdims=True)
    )
    return pulled, jnp.sum(grad * unit, 0, keepdims=True), jnp.sum(grad, 0, keepdims=True)


def mlp_back_kernel(pre_ref, up_ref, middle_ref, cot_ref, gain_ref, grad_ref, sums_ref, sum_buf):
    step = pl.program_id(0)

    @pl.when(step == 0)
    def _():
        sum_buf[...] = dot(pre_ref[0], up_ref[0], 1, 1)

    @pl.when(step > 0)
    def _():
        sum_buf[...] += dot(pre_ref[0], up_ref[0], 1, 1)

    @pl.when(step == pl.num_programs(0) - 1)
    def _():
        sums_ref[...] = jnp.zeros_like(sums_ref)
        chunk = 224

        def one(i, carry):
            at = pl.ds(pl.multiple_of(i * chunk, chunk), chunk)
            cot = cot_ref[at, :].astype(WIDE)
            pulled, gain_grad, shift_grad = norm_back(
                middle_ref[at, :], gain_ref[...].astype(WIDE), sum_buf[at, :]
            )
            grad = cot + pulled
            grad_ref[at, :] = grad
            sums_ref[0:1, :] += gain_grad
            sums_ref[1:2, :] += shift_grad
            sums_ref[2:3, :] += jnp.sum(grad.astype(LOW).astype(WIDE), 0, keepdims=True)
            sums_ref[3:4, :] += jnp.sum(cot, 0, keepdims=True)
            return carry

        lax.fori_loop(0, grad_ref.shape[0] // chunk, one, 0)


def mlp_back(pre_grads, ups, middle, cot, gain):
    tiles, rows, tile = pre_grads.shape
    width = cot.shape[1]
    return pl.pallas_call(
        mlp_back_kernel,
        grid=(tiles,),
        in_specs=[
            pl.BlockSpec((1, rows, tile), lambda j: (j, 0, 0)),
            pl.BlockSpec((1, width, tile), lambda j: (j, 0, 0)),
            resident(middle.shape),
            resident(cot.shape),
            resident((1, width)),
        ],
        out_specs=[resident((rows, width)), resident((8, width))],
        out_shape=[
            jax.ShapeDtypeStruct((rows, width), WIDE),
            jax.ShapeDtypeStruct((8, width), WIDE),
        ],
        scratch_shapes=[pltpu.VMEM((rows, width), WIDE)],
        name="mlp_back",
        compiler_params=pltpu.CompilerParams(vmem_limit_bytes=56 * 1024 * 1024),
    )(pre_grads, ups, middle, cot, gain)


def mlp_out_kernel(act_ref, down_ref, middle_ref, bias_ref, out_ref, sum_buf):
    step = pl.program_id(0)

    @pl.when(step == 0)
    def _():
        sum_buf[...] = middle_ref[...] + bias_ref[...].astype(WIDE)

    sum_buf[...] += dot(act_ref[0], down_ref[0], 1, 0)

    @pl.when(step == pl.num_programs(0) - 1)
    def _():
        out_ref[...] = sum_buf[...].astype(LOW)


def mlp_out(acts, downs, middle, bias):
    tiles, rows, tile = acts.shape
    width = middle.shape[1]
    return pl.pallas_call(
        mlp_out_kernel,
        grid=(tiles,),
        in_specs=[
            pl.BlockSpec((1, rows, tile), lambda j: (j, 0, 0)),
            pl.BlockSpec((1, tile, width), lambda j: (j, 0, 0)),
            resident(middle.shape),
            resident((1, width)),
        ],
        out_specs=resident((rows, width)),
        out_shape=jax.ShapeDtypeStruct((rows, width), LOW),
        scratch_shapes=[pltpu.VMEM((rows, width), WIDE)],
        name="mlp_out",
        compiler_params=pltpu.CompilerParams(vmem_limit_bytes=56 * 1024 * 1024),
    )(acts, downs, middle, bias)


def input_kernel(grad_ref, weight_ref, rows_ref, above_ref, gain_ref, out_ref, sums_ref):
    pulled_sum = dot(grad_ref[0, 0], weight_ref[0], 1, 1)
    for i in range(1, 4):
        pulled_sum = pulled_sum + dot(grad_ref[i, 0], weight_ref[i], 1, 1)
    pulled, gain_grad, shift_grad = norm_back(
        rows_ref[0].astype(WIDE), gain_ref[...].astype(WIDE), pulled_sum
    )
    out_ref[0] = (above_ref[0] + pulled).astype(LOW)

    @pl.when(pl.program_id(0) == 0)
    def _():
        sums_ref[...] = jnp.zeros_like(sums_ref)

    sums_ref[0:1, :] += gain_grad
    sums_ref[1:2, :] += shift_grad


def input_step(grads, weights, rows, above, gain):
    pairs, seq, width = rows.shape
    block = lambda: pl.BlockSpec((1, seq, width), lambda p: (p, 0, 0))
    return pl.pallas_call(
        input_kernel,
        grid=(pairs,),
        in_specs=[
            pl.BlockSpec((4, 1, seq, 768), lambda p: (0, p, 0, 0)),
            resident(weights.shape),
            block(),
            block(),
            resident((1, width)),
        ],
        out_specs=[block(), resident((8, width))],
        out_shape=[
            jax.ShapeDtypeStruct(rows.shape, LOW),
            jax.ShapeDtypeStruct((8, width), WIDE),
        ],
        name="input_grad",
        compiler_params=pltpu.CompilerParams(vmem_limit_bytes=56 * 1024 * 1024),
    )(grads, weights, rows, above, gain)


def place_kernel(turned, spot_ref, near_ref, far_ref, *refs):
    outs = refs[-len(turned) :]
    core = pl.program_id(1) ^ spot_ref[0]
    for i, turn in enumerate(turned):
        parts = []
        for z in range(4):
            at = z ^ spot_ref[2]
            parts.append(
                jnp.where(core == 0, near_ref[at, i], far_ref[at, i])
            )
        block = jnp.concatenate(parts, 0)
        outs[i][...] = (block.T if turn else block).astype(WIDE)


def place(turned, chunk, chunks, spots, near, far, shapes, buffers):
    _, kinds, rows, width = near.shape
    source = lambda: pl.BlockSpec(
        (4, kinds, rows, width), lambda x, c, spot: (x ^ spot[1], 0, 0, 0)
    )
    specs = [
        pl.BlockSpec((width, LANES), lambda x, c, spot: (0, (c * 2 + x) * chunks + chunk))
        if turn
        else pl.BlockSpec((LANES, width), lambda x, c, spot: ((c * 2 + x) * chunks + chunk, 0))
        for turn in turned
    ]
    return pl.pallas_call(
        functools.partial(place_kernel, turned),
        grid_spec=pltpu.PrefetchScalarGridSpec(
            num_scalar_prefetch=1,
            grid=(2, 2),
            in_specs=[source(), source()] + [ANYWHERE] * len(buffers),
            out_specs=specs,
        ),
        out_shape=[jax.ShapeDtypeStruct(shape, WIDE) for shape in shapes],
        input_output_aliases={3 + i: i for i in range(len(buffers))},
        name="place",
        compiler_params=pltpu.CompilerParams(vmem_limit_bytes=56 * 1024 * 1024),
    )(spots, near, far, *buffers)


def gathered_kernel(source_ref, *refs):
    up_ref, down_ref = refs[-2:]
    rows = [[source_ref[high, low, 0, 0] for high in range(2)] for low in range(2)]
    for kind, out_ref in enumerate((up_ref, down_ref)):
        parts = []
        for sub in range(2):
            for low in range(2):
                for high in range(2):
                    parts.append(rows[low][high][2 * sub + kind])
        block = jnp.concatenate(parts, 0)
        out_ref[...] = (block.T if kind == 0 else block).astype(WIDE)


def gathered(chunk, chunks, source, shapes, buffers):
    kinds, rows, width = source.shape[1:]
    source = source.reshape((2, 2, 2, 2, kinds, rows, width))
    span = 2 * LANES
    return pl.pallas_call(
        gathered_kernel,
        grid=(2, 2),
        in_specs=[
            pl.BlockSpec((2, 2, 1, 1, kinds, rows, width), lambda c, x: (0, 0, x, c, 0, 0, 0))
        ]
        + [ANYWHERE] * len(buffers),
        out_specs=[
            pl.BlockSpec((width, span), lambda c, x: (0, (c * 2 + x) * chunks + chunk)),
            pl.BlockSpec((span, width), lambda c, x: ((c * 2 + x) * chunks + chunk, 0)),
        ],
        out_shape=[jax.ShapeDtypeStruct(shape, WIDE) for shape in shapes],
        input_output_aliases={1 + i: i for i in range(len(buffers))},
        name="gathered",
        compiler_params=pltpu.CompilerParams(vmem_limit_bytes=56 * 1024 * 1024),
    )(source, *buffers)


def paired_body(
    layer_in,
    patch_count,
    attn_gain,
    attn_shift,
    query_weight,
    query_bias,
    key_weight,
    value_weight,
    value_bias,
    out_weight,
    out_bias,
    mlp_gain,
    mlp_shift,
    up_weight,
    up_bias,
    down_weight,
    down_bias,
    layer_cot,
):
    groups = lax.axis_size("dp")
    rank = lax.axis_index("dp")
    half_id = lax.axis_index("mp")
    core_id, x_id, zlow_id, zhigh_id = rank & 1, (rank >> 1) & 1, (rank >> 2) & 1, (rank >> 3) & 1
    part = core_id * 2 + x_id
    spots = jnp.stack([part, part ^ 1, part ^ 2, part ^ 3]).astype(jnp.int32)
    sides = jnp.stack([x_id, x_id ^ 1, x_id, x_id ^ 1]).astype(jnp.int32)
    place_spots = jnp.stack([core_id, x_id, zlow_id * 2 + zhigh_id]).astype(jnp.int32)

    swap = lambda value, bit: flip(value, "dp", bit, groups)
    across = lambda value: flip(value, "mp", 1, 2)

    rows, width = layer_in.shape
    heads_width = query_weight.shape[1]
    hidden_width = up_weight.shape[1]
    block = hidden_width // 4
    pairs = rows // SEQ
    counts = pick(patch_count, half_id, pairs, 0)
    row_vec = lambda vec: vec.reshape(1, -1)

    gate = lambda value, *waits: after(value, *waits) if waits else value
    shape_three = (pairs, SEQ, width)
    subs = block // LANES

    slice_rows = LANES // 2
    slice_at = (rank // 4) * 2 * subs + rank % 4
    slices = jnp.stack(
        [
            jnp.stack(
                [
                    pick(up_weight, slice_at + 4 * i, slice_rows, 1).T,
                    pick(down_weight, slice_at + 4 * i, slice_rows, 0),
                ]
            )
            for i in range(2)
        ]
    )
    slices = across(slices)
    sent_qkv = jnp.stack(
        [pick(w, core_id, heads_width // 2, 1) for w in (query_weight, key_weight, value_weight)]
    )
    sent_bias = jnp.concatenate([query_bias, value_bias, up_bias])
    near_qkv = across(sent_qkv)
    bias_other = across(sent_bias)
    rows_in = layer_in.astype(WIDE)
    normed = layer_norm(
        rows_in, attn_gain.astype(WIDE), attn_shift.astype(WIDE)
    ).astype(LOW)
    normed_three = normed.reshape(shape_three)

    def own_inputs():
        weights = [
            (w, pl.BlockSpec((width, LANES), lambda g, p, spot, count, i=i: (0, spot[2 * g + i])))
            for w in (query_weight, key_weight, value_weight)
            for i in range(2)
        ]
        biases = [
            (row_vec(b), pl.BlockSpec((1, LANES), lambda g, p, spot, count, i=i: (0, spot[2 * g + i])))
            for b in (query_bias, value_bias)
            for i in range(2)
        ]
        return weights, biases

    def other_inputs(group, qkv):
        weights = [
            (qkv, pl.BlockSpec((None, width, LANES), lambda g, p, side, count, k=k, i=i: (k, 0, side[i])))
            for k in range(3)
            for i in range(2)
        ]
        biases = [
            (b, pl.BlockSpec((1, LANES), lambda g, p, side, count, i=i: (0, side[4 + 2 * group + i])))
            for b in (query_bias_other, value_bias_other)
            for i in range(2)
        ]
        return weights, biases

    other_spots = jnp.concatenate([sides, spots])
    gathered_weights = [lax.all_gather(slices[0], "dp"), lax.all_gather(slices[1], "dp")]
    kept = attend(
        0, 2, gate(spots, sent_qkv, sent_bias, slices), counts, normed_three, *own_inputs(), []
    )
    near_qkv, bias_other, _ = lax.optimization_barrier((near_qkv, bias_other, kept[1]))
    query_bias_other = row_vec(bias_other[:heads_width])
    value_bias_other = row_vec(bias_other[heads_width : 2 * heads_width])
    up_bias_other = row_vec(bias_other[2 * heads_width :])
    sent_out = after(pick(out_weight, core_id, heads_width // 2, 0), near_qkv)
    near_out = across(sent_out)
    far_qkv = swap(near_qkv, CORE)
    kept = attend(
        2, 1, gate(other_spots, sent_out), counts, normed_three, *other_inputs(0, near_qkv), kept
    )
    near_out = after(near_out, kept[1])
    far_out = swap(near_out, CORE)
    kept = attend(
        3, 1, gate(other_spots, near_out), counts, normed_three, *other_inputs(1, far_qkv), kept
    )
    middle, hidden, outs_all = middle_step(
        jnp.concatenate([spots, sides]),
        layer_in.reshape(shape_three),
        kept[1],
        out_weight,
        near_out,
        far_out,
        row_vec(out_bias),
        row_vec(mlp_gain),
        row_vec(mlp_shift),
    )
    middle = middle.reshape(rows, width)
    hidden = hidden.reshape(rows, width)

    def own_mlp(first):
        ups = [
            (up_weight, pl.BlockSpec((width, LANES), lambda j, spot, r=r: (0, spot[r] * subs + first + j)))
            for r in range(4)
        ]
        downs = [
            (down_weight, pl.BlockSpec((LANES, width), lambda j, spot, r=r: (spot[r] * subs + first + j, 0)))
            for r in range(4)
        ]
        biases = [
            (row_vec(up_bias), pl.BlockSpec((1, LANES), lambda j, spot, r=r: (0, spot[r] * subs + first + j)))
            for r in range(4)
        ]
        return ups, downs, biases

    def other_mlp(first):
        source = gathered_weights[first // 2]
        ups, downs = (
            [
                (source, pl.BlockSpec((2, 1, slice_rows, width), lambda j, spot, r=r, k=k: (spot[r] * 2 + j, k, 0, 0)))
                for r in range(4)
            ]
            for k in range(2)
        )
        biases = [
            (up_bias_other, pl.BlockSpec((1, LANES), lambda j, spot, r=r: (0, spot[r] * subs + first + j)))
            for r in range(4)
        ]
        return ups, downs, biases

    def cut(item, index):
        count, lanes, cols = item.shape
        return pick(item.reshape(count, 2, lanes // 2, cols), index, 1, 1)[:, 0]

    def outbound(near, far, first, last):
        return total(near[:, first:last], far[:, first:last])

    def sideways(near, far, beyond, first, last):
        return total(near[1, first:last], far[1, first:last], beyond[1])

    def collected(near, far, beyond, side, first, last):
        return total(near[0, first:last], far[0, first:last], beyond[0], side)

    def halves(item):
        return cut(item, zlow_id ^ 1), cut(item, zlow_id)

    def quarters(item):
        return cut(item, zhigh_id ^ 1), cut(item, zhigh_id)

    back = lambda slot, wait, qkv_grads: attend_back(
        slot, gate(counts, *wait), normed, middle_grad, kept, outs_all, qkv_grads
    )

    other_a = mlp(2, True, spots, hidden, layer_cot, *other_mlp(0), [])
    far_other_a = swap(other_a[1], CORE)
    own_a = mlp(0, False, spots, hidden, layer_cot, *own_mlp(0), other_a[3:])
    far_own_a = swap(own_a[1], CORE)
    far_other_a = after(far_other_a, own_a[2])
    out_a = [outbound(other_a[0], far_other_a, *span) for span in ((0, 1), (1, 2), (2, 4))]
    own_b = mlp(6, False, gate(spots, *out_a), hidden, layer_cot, *own_mlp(2), own_a[3:])
    beyond_a0 = across(out_a[0])
    far_own_b = swap(own_b[1], CORE)
    far_own_a = after(far_own_a, own_b[2])
    other_b = mlp(
        4, True, gate(spots, beyond_a0, far_own_a), hidden, layer_cot, *other_mlp(2), own_b[3:]
    )
    beyond_a1 = across(after(out_a[1], beyond_a0))
    far_other_b = swap(other_b[1], CORE)
    acts, pre_grads, ups_all, downs_all = other_b[3:]
    beyond_a1 = after(beyond_a1, other_b[2])
    beyond_a01 = jnp.concatenate([beyond_a0, beyond_a1], 1)
    side_a01 = sideways(own_a[0], far_own_a, beyond_a01, 0, 2)
    middle_grad, sums_two = mlp_back(
        pre_grads, ups_all, middle, layer_cot, gate(row_vec(mlp_gain), side_a01, beyond_a01, far_own_b)
    )
    beyond_a23 = after(across(after(out_a[2], beyond_a1)), sums_two)
    arrived_a01 = after(swap(side_a01, XBIT), sums_two)
    far_other_b = after(far_other_b, sums_two)
    side_a23 = sideways(own_a[0], far_own_a, beyond_a23, 2, 4)
    out_b = [outbound(other_b[0], far_other_b, *span) for span in ((0, 2), (2, 4))]
    other_far, bias_other_far, qkv_grads = back(3, (side_a23, arrived_a01, *out_b), [])
    beyond_b01 = after(across(out_b[0]), bias_other_far)
    arrived_a23 = after(swap(side_a23, XBIT), bias_other_far)
    late_other_far = swap(other_far, CORE)
    sum_a = jnp.concatenate(
        [
            collected(own_a[0], far_own_a, beyond_a01, arrived_a01, 0, 2),
            collected(own_a[0], far_own_a, beyond_a23, arrived_a23, 2, 4),
        ]
    )
    low_a, keep_a = halves(sum_a)
    side_b01 = sideways(own_b[0], far_own_b, beyond_b01, 0, 2)
    other_near, bias_other_near, qkv_grads = back(2, (low_a, sum_a, side_b01), [qkv_grads])
    beyond_b23 = after(across(after(out_b[1], beyond_b01)), bias_other_near)
    arrived_b01 = after(swap(side_b01, XBIT), bias_other_near)
    low_a = after(swap(low_a, ZLOW), bias_other_near)
    late_other_far = after(late_other_far, bias_other_near)
    high_a, keep_a = quarters(total(keep_a, low_a))
    side_b23 = sideways(own_b[0], far_own_b, beyond_b23, 2, 4)
    late_out = [outbound(other_near, late_other_far, *span) for span in ((0, 2), (2, 4))]
    own_far, bias_own_far, qkv_grads = back(1, (high_a, side_b23, arrived_b01, *late_out), [qkv_grads])
    late_own_far = swap(own_far, CORE)
    late_beyond0 = after(across(late_out[0]), bias_own_far)
    arrived_b23 = after(swap(side_b23, XBIT), bias_own_far)
    high_a = after(swap(high_a, ZHIGH), bias_own_far)
    one_a = total(keep_a, high_a)
    sum_b = jnp.concatenate(
        [
            collected(own_b[0], far_own_b, beyond_b01, arrived_b01, 0, 2),
            collected(own_b[0], far_own_b, beyond_b23, arrived_b23, 2, 4),
        ]
    )
    low_b, keep_b = halves(sum_b)
    gathered_a = lax.all_gather(one_a, "dp")
    own_near, bias_own_near, qkv_grads = back(0, (one_a, low_b, sum_b, late_beyond0), [qkv_grads])
    late_beyond1 = after(across(after(late_out[1], late_beyond0)), bias_own_near)
    late_own_far = after(late_own_far, bias_own_near)
    low_b = after(swap(low_b, ZLOW), bias_own_near)
    high_b, keep_b = quarters(total(keep_b, low_b))
    late_side0 = sideways(own_near, late_own_far, late_beyond0, 0, 2)
    grad_in, sums_one = input_step(
        qkv_grads,
        kept[2],
        layer_in.reshape(shape_three),
        middle_grad.reshape(shape_three),
        gate(row_vec(attn_gain), high_b, late_side0, late_beyond1),
    )
    high_b = after(swap(high_b, ZHIGH), sums_one)
    one_b = total(keep_b, high_b)
    gathered_b = lax.all_gather(one_b, "dp")
    late_arrived0 = after(swap(late_side0, XBIT), sums_one)
    late_side1 = sideways(own_near, late_own_far, after(late_beyond1, sums_one), 2, 4)
    late_low0, late_keep0 = halves(
        collected(own_near, late_own_far, late_beyond0, late_arrived0, 0, 2)
    )
    layer_out = mlp_out(
        acts, downs_all, middle, gate(row_vec(down_bias), one_b, late_side1, late_low0)
    )
    late_arrived1 = after(swap(late_side1, XBIT), layer_out)
    late_low1, late_keep1 = halves(
        collected(own_near, late_own_far, late_beyond1, late_arrived1, 2, 4)
    )
    late_all = []
    for low, keep in ((after(swap(late_low0, ZLOW), layer_out), late_keep0), (swap(late_low1, ZLOW), late_keep1)):
        high, keep = quarters(total(keep, low))
        have = total(keep, swap(high, ZHIGH))[None]
        for bit in (ZHIGH, ZLOW, XBIT):
            have = jnp.concatenate([have, swap(have, bit)])
        late_all.append((have, swap(have, CORE)))
    up_shape, down_shape = up_weight.shape, down_weight.shape
    placed = gathered(0, 2, gathered_a, (up_shape, down_shape), [])
    grad_up_weight, grad_down_weight = gathered(1, 2, gathered_b, (up_shape, down_shape), placed)
    grad_query_weight, grad_key_weight = place(
        (True, True), 0, 1, place_spots, *late_all[0], (query_weight.shape,) * 2, []
    )
    grad_value_weight, grad_out_weight = place(
        (True, False), 0, 1, place_spots, *late_all[1], (value_weight.shape, out_weight.shape), []
    )

    def back_to_place(near, far):
        return jnp.concatenate([near, far]).reshape(4, -1)[jnp.arange(4) ^ part].reshape(-1)

    def up_bias_grad(first, second):
        sums = jnp.concatenate([first[2], second[2]]).reshape(4, 4, LANES).transpose(1, 0, 2)
        return sums[jnp.arange(4) ^ part].reshape(-1)

    def small(near, far, first, second):
        return jnp.concatenate(
            [
                back_to_place(near[0, :256], far[0, :256]),
                back_to_place(near[0, 512:], far[0, 512:]),
                up_bias_grad(first, second),
            ]
        )

    own_small = small(bias_own_near, bias_own_far, own_a, own_b)
    other_small = small(bias_other_near, bias_other_far, other_a, other_b)
    shared = jnp.concatenate([sums_one[0], sums_one[1], sums_two[2], sums_two[0], sums_two[1], sums_two[3]])
    vec = jnp.concatenate([own_small, shared]) + across(jnp.concatenate([other_small, shared]))
    for bit in (CORE, XBIT, ZLOW, ZHIGH):
        vec = vec + swap(vec, bit)
    grad_query_bias = vec[:heads_width]
    grad_value_bias = vec[heads_width : 2 * heads_width]
    grad_up_bias = vec[2 * heads_width : 2 * heads_width + hidden_width]
    (
        grad_attn_gain,
        grad_attn_shift,
        grad_out_bias,
        grad_mlp_gain,
        grad_mlp_shift,
        grad_down_bias,
    ) = jnp.split(vec[2 * heads_width + hidden_width :], 6)
    return (
        layer_out,
        grad_in.reshape(rows, width),
        grad_attn_gain,
        grad_attn_shift,
        grad_query_weight,
        grad_query_bias,
        grad_key_weight,
        grad_value_weight,
        grad_value_bias,
        grad_out_weight,
        grad_out_bias,
        grad_mlp_gain,
        grad_mlp_shift,
        grad_up_weight,
        grad_up_bias,
        grad_down_weight,
        grad_down_bias,
    )


def solution(mesh):
    paired = mesh.shape["mp"] == 2 and mesh.shape["dp"] == 16
    body = paired_body if paired else general_body
    placed = (
        P(("dp", "mp"), None),
        P("dp"),
        P(),
        P(),
        P(None, "mp"),
        P("mp"),
        P(None, "mp"),
        P(None, "mp"),
        P("mp"),
        P("mp", None),
        P(),
        P(),
        P(),
        P(None, "mp"),
        P("mp"),
        P("mp", None),
        P(),
        P(("dp", "mp"), None),
    )
    return jax.shard_map(
        body,
        mesh=mesh,
        in_specs=placed,
        out_specs=(
            P(("dp", "mp"), None),
            P(("dp", "mp"), None),
            P(),
            P(),
            P(None, "mp"),
            P("mp"),
            P(None, "mp"),
            P(None, "mp"),
            P("mp"),
            P("mp", None),
            P(),
            P(),
            P(),
            P(None, "mp"),
            P("mp"),
            P("mp", None),
            P(),
        ),
        check_vma=False,
    )
```

```python
import functools

import jax
import jax.numpy as jnp
from jax import lax
from jax.experimental import pallas as pl
from jax.experimental.pallas import tpu as pltpu
from jax.sharding import PartitionSpec as P

HEAD_DIM = 64
TEXT = 40
SEQ = 280


EPS = 1e-05
SCALE = 0.125
NEGATIVE = -1e30


def layer_norm(values, gain, shift):
    center = values - jnp.mean(values, -1, keepdims=True)
    spread = jnp.mean(center * center, -1, keepdims=True)
    return center * lax.rsqrt(spread + EPS) * gain + shift


def exact_gelu(values):
    return jax.nn.gelu(values, approximate=False)


def matmul_rows(left, right):
    return jnp.dot(left, right, preferred_element_type=jnp.float32)


def contract_rows(left, right):
    return lax.dot_general(
        left, right, (((0,), (0,)), ((), ())), preferred_element_type=jnp.float32
    )


def contract_cols(left, right):
    return lax.dot_general(
        left, right, (((1,), (1,)), ((), ())), preferred_element_type=jnp.float32
    )


def column_sum(values):
    return jnp.sum(values.astype(jnp.float32), 0)


def general_body(
    layer_in,
    patch_count,
    attn_gain,
    attn_shift,
    query_weight,
    query_bias,
    key_weight,
    value_weight,
    value_bias,
    out_weight,
    out_bias,
    mlp_gain,
    mlp_shift,
    up_weight,
    up_bias,
    down_weight,
    down_bias,
    layer_cot,
):
    lowtype = jnp.bfloat16
    wide = jnp.float32
    rows_in = layer_in.astype(wide)
    gain_one = attn_gain.astype(wide)
    shift_one = attn_shift.astype(wide)
    gain_two = mlp_gain.astype(wide)
    shift_two = mlp_shift.astype(wide)
    normed_tok, norm_pull = jax.vjp(layer_norm, rows_in, gain_one, shift_one)
    group_rows = lax.all_gather(normed_tok.astype(lowtype), "mp", axis=0, tiled=True)
    query_rows = (matmul_rows(group_rows, query_weight) + query_bias.astype(wide)).astype(lowtype)
    key_rows = matmul_rows(group_rows, key_weight).astype(lowtype)
    value_rows = (matmul_rows(group_rows, value_weight) + value_bias.astype(wide)).astype(lowtype)
    pairs = patch_count.shape[0]
    local_width = query_weight.shape[1]
    local_heads = local_width // HEAD_DIM
    group_total = group_rows.shape[0]
    shape_four = (pairs, SEQ, local_heads, HEAD_DIM)
    query_blk = query_rows.reshape(shape_four)
    key_blk = key_rows.reshape(shape_four)
    value_blk = value_rows.reshape(shape_four)
    scores = jnp.einsum("pqhd,pkhd->phqk", query_blk, key_blk, preferred_element_type=wide) * SCALE
    valid = jnp.arange(SEQ)[None, :] < (TEXT + patch_count)[:, None]
    scores = jnp.where(valid[:, None, None, :], scores, NEGATIVE)
    probs = jax.nn.softmax(scores, axis=-1)
    probs_low = probs.astype(lowtype)
    context = jnp.einsum("phqk,pkhd->pqhd", probs_low, value_blk, preferred_element_type=wide)
    context = context.astype(lowtype).reshape(group_total, local_width)
    context_tok = lax.all_to_all(context, "mp", split_axis=0, concat_axis=1, tiled=True)
    out_full = lax.all_gather(out_weight, "mp", axis=0, tiled=True)
    attended = matmul_rows(context_tok, out_full) + out_bias.astype(wide)
    middle = rows_in + attended
    hidden_wide, mlp_pull = jax.vjp(layer_norm, middle, gain_two, shift_two)
    hidden_in = hidden_wide.astype(lowtype)
    cot_wide = layer_cot.astype(wide)
    up_full, bias_full, down_full = (
        lax.all_gather(up_weight, "mp", axis=1, tiled=True),
        lax.all_gather(up_bias, "mp", axis=0, tiled=True),
        lax.all_gather(down_weight, "mp", axis=0, tiled=True),
    )
    pre_act = matmul_rows(hidden_in, up_full) + bias_full.astype(wide)
    act_wide, gelu_pull = jax.vjp(exact_gelu, pre_act)
    act_low = act_wide.astype(lowtype)
    ffn_out = matmul_rows(act_low, down_full) + down_bias.astype(wide)
    whole_down = contract_rows(act_low, layer_cot)
    act_grad = contract_cols(layer_cot, down_full)
    pre_grad = gelu_pull(act_grad)[0].astype(lowtype)
    whole_up_bias = column_sum(pre_grad)
    whole_up = contract_rows(hidden_in, pre_grad)
    hidden_grad = contract_cols(pre_grad, up_full)
    grad_up_weight, grad_up_bias, grad_down_weight = (
        lax.psum_scatter(
            whole_up.astype(jnp.bfloat16), "mp", scatter_dimension=1, tiled=True
        ).astype(jnp.float32),
        lax.psum_scatter(
            whole_up_bias.astype(jnp.bfloat16), "mp", scatter_dimension=0, tiled=True
        ).astype(jnp.float32),
        lax.psum_scatter(
            whole_down.astype(jnp.bfloat16), "mp", scatter_dimension=0, tiled=True
        ).astype(jnp.float32),
    )
    layer_out = (middle + ffn_out).astype(lowtype)
    grad_down_bias = column_sum(layer_cot)
    middle_part, grad_gain_two, grad_shift_two = mlp_pull(hidden_grad)
    middle_grad = cot_wide + middle_part
    attn_grad = middle_grad.astype(lowtype)
    grad_out_bias = column_sum(attn_grad)
    grad_out_weight = lax.psum_scatter(
        contract_rows(context_tok, attn_grad).astype(jnp.bfloat16),
        "mp",
        scatter_dimension=0,
        tiled=True,
    ).astype(jnp.float32)
    context_grad_tok = contract_cols(attn_grad, out_full).astype(lowtype)
    context_grad = lax.all_to_all(
        context_grad_tok, "mp", split_axis=1, concat_axis=0, tiled=True
    ).reshape(shape_four)
    probs_grad = jnp.einsum("pqhd,pkhd->phqk", context_grad, value_blk, preferred_element_type=wide)
    value_grad = jnp.einsum("phqk,pqhd->pkhd", probs_low, context_grad, preferred_element_type=wide)
    value_grad = value_grad.astype(lowtype).reshape(group_total, local_width)
    score_grad = (probs * (probs_grad - jnp.sum(probs * probs_grad, -1, keepdims=True))).astype(
        lowtype
    )
    query_grad = (
        jnp.einsum("phqk,pkhd->pqhd", score_grad, key_blk, preferred_element_type=wide) * SCALE
    )
    query_grad = query_grad.astype(lowtype).reshape(group_total, local_width)
    key_grad = (
        jnp.einsum("phqk,pqhd->pkhd", score_grad, query_blk, preferred_element_type=wide) * SCALE
    )
    key_grad = key_grad.astype(lowtype).reshape(group_total, local_width)
    grad_query_weight = contract_rows(group_rows, query_grad)
    grad_key_weight = contract_rows(group_rows, key_grad)
    grad_value_weight = contract_rows(group_rows, value_grad)
    grad_query_bias = column_sum(query_grad)
    grad_value_bias = column_sum(value_grad)
    total = contract_cols(query_grad, query_weight)
    total = total + contract_cols(key_grad, key_weight)
    normed_grad = lax.psum_scatter(
        (total + contract_cols(value_grad, value_weight)).astype(jnp.bfloat16),
        "mp",
        scatter_dimension=0,
        tiled=True,
    ).astype(jnp.float32)
    input_part, grad_gain_one, grad_shift_one = norm_pull(normed_grad)
    grad_in = (middle_grad + input_part).astype(lowtype)
    (
        grad_query_weight,
        grad_query_bias,
        grad_key_weight,
        grad_value_weight,
        grad_value_bias,
        grad_out_weight,
        grad_up_weight,
        grad_up_bias,
        grad_down_weight,
    ) = (
        lax.psum(grad_query_weight.astype(jnp.bfloat16), "dp").astype(jnp.float32),
        lax.psum(grad_query_bias.astype(jnp.bfloat16), "dp").astype(jnp.float32),
        lax.psum(grad_key_weight.astype(jnp.bfloat16), "dp").astype(jnp.float32),
        lax.psum(grad_value_weight.astype(jnp.bfloat16), "dp").astype(jnp.float32),
        lax.psum(grad_value_bias.astype(jnp.bfloat16), "dp").astype(jnp.float32),
        lax.psum(grad_out_weight.astype(jnp.bfloat16), "dp").astype(jnp.float32),
        lax.psum(grad_up_weight.astype(jnp.bfloat16), "dp").astype(jnp.float32),
        lax.psum(grad_up_bias.astype(jnp.bfloat16), "dp").astype(jnp.float32),
        lax.psum(grad_down_weight.astype(jnp.bfloat16), "dp").astype(jnp.float32),
    )
    grad_gain_one, grad_shift_one, grad_out_bias, grad_gain_two, grad_shift_two, grad_down_bias = (
        lax.psum(
            (
                grad_gain_one,
                grad_shift_one,
                grad_out_bias,
                grad_gain_two,
                grad_shift_two,
                grad_down_bias,
            ),
            ("dp", "mp"),
        )
    )
    return (
        layer_out,
        grad_in,
        grad_gain_one,
        grad_shift_one,
        grad_query_weight,
        grad_query_bias,
        grad_key_weight,
        grad_value_weight,
        grad_value_bias,
        grad_out_weight,
        grad_out_bias,
        grad_gain_two,
        grad_shift_two,
        grad_up_weight,
        grad_up_bias,
        grad_down_weight,
        grad_down_bias,
    )


WIDE = jnp.float32
LOW = jnp.bfloat16
LANES = 128
ROOT_HALF = 0.7071067811865476
NORMAL = 0.3989422804014327
CORE, XBIT, ZLOW, ZHIGH = 1, 2, 4, 8


def dot(left, right, left_dim, right_dim):
    return lax.dot_general(
        left, right, (((left_dim,), (right_dim,)), ((), ())), preferred_element_type=WIDE
    )


def flip(value, axis, bit, size):
    return lax.ppermute(value, axis, [(i, i ^ bit) for i in range(size)])


def pick(value, index, width, axis):
    return lax.dynamic_slice_in_dim(value, index * width, width, axis)


def after(value, *others):
    return lax.optimization_barrier((value,) + others)[0]


def total(*items):
    result = items[0].astype(WIDE)
    for item in items[1:]:
        result = result + item.astype(WIDE)
    return result.astype(LOW)


def resident(shape):
    return pl.BlockSpec(shape, lambda *_: (0,) * len(shape), pipeline_mode=pl.Buffered(1))


ANYWHERE = pl.BlockSpec(memory_space=pl.ANY)


def attend_kernel(spot_ref, count_ref, rows_ref, *refs):
    weights, biases = refs[:6], refs[6:10]
    qkv_ref, context_ref, weight_ref, bias_ref = refs[-4:]
    pair = pl.program_id(1)

    @pl.when(pair == 0)
    def _():
        for i in range(6):
            weight_ref[0, :, i * LANES : (i + 1) * LANES] = weights[i][...]
        bias_ref[...] = jnp.zeros_like(bias_ref)
        for i in range(2):
            bias_ref[:, i * LANES : (i + 1) * LANES] = biases[i][...].astype(WIDE)
            bias_ref[:, (4 + i) * LANES : (5 + i) * LANES] = biases[2 + i][...].astype(WIDE)

    qkv = (dot(rows_ref[0], weight_ref[0], 1, 0) + bias_ref[...]).astype(LOW)
    qkv_ref[0, 0] = qkv
    length = TEXT + count_ref[pair]
    lane = lax.broadcasted_iota(jnp.int32, (SEQ, LANES), 1)
    padding = lax.broadcasted_iota(jnp.int32, (SEQ, SEQ), 1) >= length
    lane_low = lane < HEAD_DIM
    everything = []
    for tile in range(2):
        query, key, value = (
            qkv[:, i * 256 + tile * LANES : i * 256 + (tile + 1) * LANES] for i in range(3)
        )
        query = query * SCALE
        for side in range(2):
            mine = lane_low if side == 0 else jnp.logical_not(lane_low)
            everything.append((dot(jnp.where(mine, query, jnp.zeros_like(query)), key, 1, 1), value))
    heads = []
    for scores, value in everything:
        scores = jnp.where(padding, NEGATIVE, scores)
        power = jnp.exp(scores - jnp.max(scores, -1, keepdims=True))
        inverse = 1.0 / jnp.sum(power, -1, keepdims=True)
        heads.append(dot(power.astype(LOW), value, 1, 0) * inverse)
    for tile in range(2):
        context_ref[0, 0, :, tile * LANES : (tile + 1) * LANES] = jnp.where(
            lane_low, heads[2 * tile], heads[2 * tile + 1]
        ).astype(LOW)


def attend(slot, groups, spots, counts, rows, weights, biases, buffers):
    pairs, seq, width = rows.shape
    shapes = [
        ((4, pairs, seq, 768), (1, 1, seq, 768), lambda g, p, *_: (slot + g, p, 0, 0)),
        ((4, pairs, seq, 256), (1, 1, seq, 256), lambda g, p, *_: (slot + g, p, 0, 0)),
        ((4, width, 768), (1, width, 768), lambda g, p, *_: (slot + g, 0, 0)),
    ]
    operands = list(weights) + list(biases)
    aliases = {3 + len(operands) + i: i for i in range(len(buffers))}
    return pl.pallas_call(
        attend_kernel,
        grid_spec=pltpu.PrefetchScalarGridSpec(
            num_scalar_prefetch=2,
            grid=(groups, pairs),
            in_specs=[pl.BlockSpec((1, seq, width), lambda g, p, *_: (p, 0, 0))]
            + [spec for _, spec in operands]
            + [ANYWHERE] * len(buffers),
            out_specs=[pl.BlockSpec(block, index) for _, block, index in shapes],
            scratch_shapes=[pltpu.VMEM((1, 768), WIDE)],
        ),
        out_shape=[jax.ShapeDtypeStruct(shape, LOW) for shape, _, _ in shapes],
        input_output_aliases=aliases,
        name="attend",
        compiler_params=pltpu.CompilerParams(vmem_limit_bytes=56 * 1024 * 1024),
    )(spots, counts, rows, *[array for array, _ in operands], *buffers)


def attend_back_kernel(count_ref, rows_hbm, cots_hbm, cot_ref, qkv_ref, context_ref, out_ref, *refs):
    near_ref, bias_ref, qkv_grad_ref, grad_buf, context_buf, rows_buf, cots_buf, sems = refs[-8:]
    pair = pl.program_id(0)
    copies = [
        pltpu.make_async_copy(rows_hbm, rows_buf, sems.at[0]),
        pltpu.make_async_copy(cots_hbm, cots_buf, sems.at[1]),
    ]

    @pl.when(pair == 0)
    def _():
        for copy in copies:
            copy.start()

    at = pl.ds(pl.multiple_of(pair * SEQ, 8), SEQ)
    context_grad = dot(cot_ref[0], out_ref[0], 1, 1).astype(LOW)
    qkv = qkv_ref[0, 0]
    context_buf[at, :] = context_ref[0, 0].astype(WIDE)
    length = TEXT + count_ref[pair]
    lane = lax.broadcasted_iota(jnp.int32, (SEQ, LANES), 1)
    padding = lax.broadcasted_iota(jnp.int32, (SEQ, SEQ), 0) >= length
    grads = [[], [], []]
    lane_low = lane < HEAD_DIM
    work = []
    for tile in range(2):
        query, key, value = (
            qkv[:, i * 256 + tile * LANES : i * 256 + (tile + 1) * LANES] for i in range(3)
        )
        query = query * SCALE
        outer = context_grad[:, tile * LANES : (tile + 1) * LANES]
        for side in range(2):
            mine = lane_low if side == 0 else jnp.logical_not(lane_low)
            scores = dot(jnp.where(mine, key, jnp.zeros_like(key)), query, 1, 1)
            probs_grad = dot(jnp.where(mine, value, jnp.zeros_like(value)), outer, 1, 1)
            work.append((scores, probs_grad, query, key, outer))
    heads = []
    for scores, probs_grad, query, key, outer in work:
        scores = jnp.where(padding, NEGATIVE, scores)
        power = jnp.exp(scores - jnp.max(scores, 0, keepdims=True))
        probs = power * (1.0 / jnp.sum(power, 0, keepdims=True))
        both = probs * probs_grad
        score_grad = (both - probs * jnp.sum(both, 0, keepdims=True)).astype(LOW)
        heads.append(
            (dot(score_grad, key, 0, 0), dot(score_grad, query, 1, 0), dot(probs.astype(LOW), outer, 1, 0))
        )
    for tile in range(2):
        for i, scale in enumerate((SCALE, 1.0, 1.0)):
            pair_of = [heads[2 * tile + side][i] for side in range(2)]
            grads[i].append((jnp.where(lane_low, *pair_of) * scale).astype(LOW))
    joined = jnp.concatenate(grads[0] + grads[1] + grads[2], 1)
    qkv_grad_ref[0, 0] = joined
    grad_buf[at, :] = joined.astype(WIDE)

    @pl.when(pair == pl.num_programs(0) - 1)
    def _():
        for copy in copies:
            copy.wait()
        stacked = dot(grad_buf[...].astype(LOW), rows_buf[...], 0, 0).astype(LOW)
        outs = dot(context_buf[...].astype(LOW), cots_buf[...], 0, 0).astype(LOW)
        for i in range(2):
            near_ref[i, :3] = stacked.reshape(3, 2, LANES, -1)[:, i]
            near_ref[i, 3] = outs[i * LANES : (i + 1) * LANES]
        bias_ref[...] = jnp.sum(grad_buf[...], 0, keepdims=True)


def attend_back(slot, counts, rows, cot, kept, outs, buffers):
    qkv, context, _ = kept
    _, pairs, seq, _ = qkv.shape
    width = rows.shape[1]
    return pl.pallas_call(
        attend_back_kernel,
        grid_spec=pltpu.PrefetchScalarGridSpec(
            num_scalar_prefetch=1,
            grid=(pairs,),
            in_specs=[
                ANYWHERE,
                ANYWHERE,
                pl.BlockSpec((1, seq, width), lambda p, *_: (p, 0, 0)),
                pl.BlockSpec((1, 1, seq, 768), lambda p, *_: (slot, p, 0, 0)),
                pl.BlockSpec((1, 1, seq, 256), lambda p, *_: (slot, p, 0, 0)),
                pl.BlockSpec((1, 256, width), lambda p, *_: (slot, 0, 0)),
            ]
            + [ANYWHERE] * len(buffers),
            out_specs=[
                pl.BlockSpec((2, 4, LANES, width), lambda p, *_: (0, 0, 0, 0)),
                pl.BlockSpec((1, 768), lambda p, *_: (0, 0)),
                pl.BlockSpec((1, 1, seq, 768), lambda p, *_: (slot, p, 0, 0)),
            ],
            scratch_shapes=[
                pltpu.VMEM((pairs * seq, 768), WIDE),
                pltpu.VMEM((pairs * seq, 256), WIDE),
                pltpu.VMEM(rows.shape, LOW),
                pltpu.VMEM(cot.shape, LOW),
                pltpu.SemaphoreType.DMA((2,)),
            ],
        ),
        out_shape=[
            jax.ShapeDtypeStruct((2, 4, LANES, width), LOW),
            jax.ShapeDtypeStruct((1, 768), WIDE),
            jax.ShapeDtypeStruct(qkv.shape, LOW),
        ],
        input_output_aliases={7: 2} if buffers else {},
        name="attend_back",
        compiler_params=pltpu.CompilerParams(vmem_limit_bytes=56 * 1024 * 1024),
    )(counts, rows, cot, cot.reshape(pairs, seq, width), qkv, context, outs, *buffers)


def middle_kernel(
    spot_ref, rows_ref, context_ref, own_ref, near_ref, far_ref, bias_ref, gain_ref, shift_ref, *refs
):
    middle_ref, hidden_ref, out_ref = refs

    @pl.when(pl.program_id(0) == 0)
    def _():
        for i in range(8):
            source = own_ref if i < 4 else (near_ref if i < 6 else far_ref)
            start = pl.multiple_of(spot_ref[i] * LANES, LANES)
            out_ref[i // 2, (i % 2) * LANES : (i % 2 + 1) * LANES, :] = source[pl.ds(start, LANES), :]

    context = jnp.concatenate([context_ref[i, 0] for i in range(4)], 1)
    attended = dot(context, out_ref[...].reshape(-1, out_ref.shape[2]), 1, 0)
    middle = rows_ref[0].astype(WIDE) + attended + bias_ref[...].astype(WIDE)
    middle_ref[0] = middle
    center = middle - jnp.mean(middle, -1, keepdims=True)
    spread = jnp.mean(center * center, -1, keepdims=True)
    hidden = center * lax.rsqrt(spread + EPS) * gain_ref[...].astype(WIDE)
    hidden_ref[0] = (hidden + shift_ref[...].astype(WIDE)).astype(LOW)


def middle_step(spots, rows, context, own, near, far, bias, gain, shift):
    pairs, seq, width = rows.shape
    block = lambda: pl.BlockSpec((1, seq, width), lambda p, *_: (p, 0, 0))
    return pl.pallas_call(
        middle_kernel,
        grid_spec=pltpu.PrefetchScalarGridSpec(
            num_scalar_prefetch=1,
            grid=(pairs,),
            in_specs=[
                block(),
                pl.BlockSpec((4, 1, seq, 256), lambda p, *_: (0, p, 0, 0)),
                resident(own.shape),
                resident(near.shape),
                resident(far.shape),
            ]
            + [resident((1, width))] * 3,
            out_specs=[block(), block(), resident((4, 256, width))],
        ),
        out_shape=[
            jax.ShapeDtypeStruct(rows.shape, WIDE),
            jax.ShapeDtypeStruct(rows.shape, LOW),
            jax.ShapeDtypeStruct((4, 256, width), LOW),
        ],
        name="middle",
        compiler_params=pltpu.CompilerParams(vmem_limit_bytes=56 * 1024 * 1024),
    )(spots, rows, context, own, near, far, bias, gain, shift)


def mlp_kernel(step, turned, spot_ref, hidden_ref, cot_ref, *refs):
    ups, downs, biases = refs[:4], refs[4:8], refs[8:12]
    near_ref, far_ref, bias_out, act_ref, pre_ref, up_ref, down_ref, bias_ref = refs[-8:]
    rows = hidden_ref.shape[0]
    for r in range(4):
        span = slice(r * LANES, (r + 1) * LANES)
        if turned:
            up_ref[0, :, span] = ups[r][:, 0].reshape(LANES, -1).T
            down_ref[0, span, :] = downs[r][:, 0].reshape(LANES, -1)
        else:
            up_ref[0, :, span] = ups[r][...]
            down_ref[0, span, :] = downs[r][...]
        bias_ref[:, span] = biases[r][...].astype(WIDE)

    def one(i, carry):
        at = pl.ds(pl.multiple_of(i * step, step), step)
        pre_act = dot(hidden_ref[at, :], up_ref[0], 1, 0) + bias_ref[...]
        act_grad = dot(cot_ref[at, :], down_ref[0], 1, 1)
        chance = 0.5 + 0.5 * lax.erf(pre_act * ROOT_HALF)
        act_ref[0, at, :] = (pre_act * chance).astype(LOW)
        slope = chance + pre_act * (NORMAL * jnp.exp(-0.5 * pre_act * pre_act))
        pre_ref[0, at, :] = (act_grad * slope).astype(LOW)
        return carry

    lax.fori_loop(0, rows // step, one, 0)
    up_grad = dot(pre_ref[0], hidden_ref[...], 0, 0).astype(LOW).reshape(4, LANES, -1)
    down_grad = dot(act_ref[0], cot_ref[...], 0, 0).astype(LOW).reshape(4, LANES, -1)
    bias_out[0] = jnp.sum(pre_ref[0].astype(WIDE), 0, keepdims=True)
    for i in range(2):
        near_ref[i, 0] = up_grad[i]
        near_ref[i, 1] = down_grad[i]
        far_ref[i, 0] = up_grad[2 + i]
        far_ref[i, 1] = down_grad[2 + i]


def mlp(first, turned, spots, hidden, cot, ups, downs, biases, buffers):
    rows, width = hidden.shape
    operands = list(ups) + list(downs) + list(biases)
    tile = 4 * LANES
    grad = jax.ShapeDtypeStruct((2, 4, LANES, width), LOW)
    grad_block = pl.BlockSpec((2, 2, LANES, width), lambda j, *_: (0, j, 0, 0))
    return pl.pallas_call(
        functools.partial(mlp_kernel, rows // 2, turned),
        grid_spec=pltpu.PrefetchScalarGridSpec(
            num_scalar_prefetch=1,
            grid=(2,),
            in_specs=[resident(hidden.shape), resident(cot.shape)]
            + [spec for _, spec in operands]
            + [ANYWHERE] * len(buffers),
            out_specs=[grad_block] * 2
            + [
                pl.BlockSpec((1, 1, tile), lambda j, *_: (j, 0, 0)),
                pl.BlockSpec((1, rows, tile), lambda j, *_: (first // 2, 0, j)),
                pl.BlockSpec((1, rows, tile), lambda j, *_: (first // 2, 0, j)),
                pl.BlockSpec((1, width, tile), lambda j, *_: (first // 2, 0, j)),
                pl.BlockSpec((1, tile, width), lambda j, *_: (first // 2, j, 0)),
            ],
            scratch_shapes=[pltpu.VMEM((1, tile), WIDE)],
        ),
        out_shape=[grad] * 2
        + [
            jax.ShapeDtypeStruct((2, 1, tile), WIDE),
            jax.ShapeDtypeStruct((4, rows, 2 * tile), LOW),
            jax.ShapeDtypeStruct((4, rows, 2 * tile), LOW),
            jax.ShapeDtypeStruct((4, width, 2 * tile), LOW),
            jax.ShapeDtypeStruct((4, 2 * tile, width), LOW),
        ],
        input_output_aliases={3 + len(operands) + i: 3 + i for i in range(len(buffers))},
        name="mlp",
        compiler_params=pltpu.CompilerParams(vmem_limit_bytes=56 * 1024 * 1024),
    )(spots, hidden, cot, *[array for array, _ in operands], *buffers)


def norm_back(values, gain, grad):
    center = values - jnp.mean(values, -1, keepdims=True)
    scale = lax.rsqrt(jnp.mean(center * center, -1, keepdims=True) + EPS)
    unit = center * scale
    inner = grad * gain
    pulled = scale * (
        inner
        - jnp.mean(inner, -1, keepdims=True)
        - unit * jnp.mean(inner * unit, -1, keepdims=True)
    )
    return pulled, jnp.sum(grad * unit, 0, keepdims=True), jnp.sum(grad, 0, keepdims=True)


def mlp_back_kernel(pre_ref, up_ref, middle_hbm, cot_hbm, gain_ref, grad_ref, low_ref, sums_ref, *refs):
    sum_buf, middle_buf, cot_buf, sems = refs
    step = pl.program_id(0)
    copies = [
        pltpu.make_async_copy(middle_hbm, middle_buf, sems.at[0]),
        pltpu.make_async_copy(cot_hbm, cot_buf, sems.at[1]),
    ]
    part = dot(pre_ref[0], up_ref[0], 1, 1)

    @pl.when(step == 0)
    def _():
        for copy in copies:
            copy.start()
        sum_buf[...] = part

    @pl.when(step > 0)
    def _():
        sum_buf[...] += part

    @pl.when(step == pl.num_programs(0) - 1)
    def _():
        for copy in copies:
            copy.wait()
        sums_ref[...] = jnp.zeros_like(sums_ref)
        chunk = 224

        def one(i, carry):
            at = pl.ds(pl.multiple_of(i * chunk, chunk), chunk)
            cot = cot_buf[at, :].astype(WIDE)
            pulled, gain_grad, shift_grad = norm_back(
                middle_buf[at, :], gain_ref[...].astype(WIDE), sum_buf[at, :]
            )
            grad = cot + pulled
            low = grad.astype(LOW)
            grad_ref[at, :] = grad
            low_ref[at, :] = low
            sums_ref[0:1, :] += gain_grad
            sums_ref[1:2, :] += shift_grad
            sums_ref[2:3, :] += jnp.sum(low.astype(WIDE), 0, keepdims=True)
            sums_ref[3:4, :] += jnp.sum(cot, 0, keepdims=True)
            return carry

        lax.fori_loop(0, grad_ref.shape[0] // chunk, one, 0)


def mlp_back(pre_grads, ups, middle, cot, gain):
    tiles, rows, tile = pre_grads.shape
    width = cot.shape[1]
    return pl.pallas_call(
        mlp_back_kernel,
        grid=(tiles,),
        in_specs=[
            pl.BlockSpec((1, rows, tile), lambda j: (j, 0, 0)),
            pl.BlockSpec((1, width, tile), lambda j: (j, 0, 0)),
            ANYWHERE,
            ANYWHERE,
            resident((1, width)),
        ],
        out_specs=[resident((rows, width)), resident((rows, width)), resident((8, width))],
        out_shape=[
            jax.ShapeDtypeStruct((rows, width), WIDE),
            jax.ShapeDtypeStruct((rows, width), LOW),
            jax.ShapeDtypeStruct((8, width), WIDE),
        ],
        scratch_shapes=[
            pltpu.VMEM((rows, width), WIDE),
            pltpu.VMEM((rows, width), WIDE),
            pltpu.VMEM((rows, width), LOW),
            pltpu.SemaphoreType.DMA((2,)),
        ],
        name="mlp_back",
        compiler_params=pltpu.CompilerParams(vmem_limit_bytes=56 * 1024 * 1024),
    )(pre_grads, ups, middle, cot, gain)


def mlp_out_kernel(half, act_ref, down_ref, middle_hbm, bias_ref, *refs):
    out_ref, sum_buf, middle_buf, sem = refs[-4:]
    step = pl.program_id(0)
    rows = out_ref.shape[0]
    copy = pltpu.make_async_copy(middle_hbm.at[pl.ds(half * rows, rows), :], middle_buf, sem)
    part = dot(act_ref[0], down_ref[0], 1, 0)

    @pl.when(step == 0)
    def _():
        copy.start()
        sum_buf[...] = part

    @pl.when(step > 0)
    def _():
        sum_buf[...] += part

    @pl.when(step == pl.num_programs(0) - 1)
    def _():
        copy.wait()
        out_ref[...] = (sum_buf[...] + middle_buf[...] + bias_ref[...].astype(WIDE)).astype(LOW)


def mlp_out(half, acts, downs, middle, bias, buffers):
    tiles, rows, tile = acts.shape
    width = middle.shape[1]
    count = rows // 2
    return pl.pallas_call(
        functools.partial(mlp_out_kernel, half),
        grid=(tiles,),
        in_specs=[
            pl.BlockSpec((1, count, tile), lambda j: (j, half, 0)),
            pl.BlockSpec((1, tile, width), lambda j: (j, 0, 0)),
            ANYWHERE,
            resident((1, width)),
        ]
        + [ANYWHERE] * len(buffers),
        out_specs=pl.BlockSpec((count, width), lambda j: (half, 0)),
        out_shape=jax.ShapeDtypeStruct((rows, width), LOW),
        scratch_shapes=[
            pltpu.VMEM((count, width), WIDE),
            pltpu.VMEM((count, width), WIDE),
            pltpu.SemaphoreType.DMA(()),
        ],
        input_output_aliases={4: 0} if buffers else {},
        name="mlp_out",
        compiler_params=pltpu.CompilerParams(vmem_limit_bytes=56 * 1024 * 1024),
    )(acts, downs, middle, bias, *buffers)


def pack_kernel(spot_ref, *refs):
    out_refs = refs[-2:]
    shared_one, shared_two = refs[8:10]
    for side in range(2):
        near, far, first, second = refs[4 * side : 4 * side + 4]
        out = out_refs[side]
        for r in range(4):
            at = spot_ref[r]
            source = near if r < 2 else far
            lanes = (r % 2) * LANES
            out[pl.ds(at, 1), :] = source[:, lanes : lanes + LANES]
            out[pl.ds(4 + at, 1), :] = source[:, 512 + lanes : 512 + lanes + LANES]
            for j in range(4):
                sums = first if j < 2 else second
                out[pl.ds(8 + at * 4 + j, 1), :] = sums[j % 2, :, r * LANES : (r + 1) * LANES]
        rows = [(shared_one, 0), (shared_one, 1), (shared_two, 2), (shared_two, 0), (shared_two, 1), (shared_two, 3)]
        for k, (source, row) in enumerate(rows):
            for i in range(8):
                at = 24 + 8 * k + i
                out[at : at + 1, :] = source[row : row + 1, i * LANES : (i + 1) * LANES]


def pack(spots, own, other, sums_one, sums_two):
    return pl.pallas_call(
        pack_kernel,
        grid_spec=pltpu.PrefetchScalarGridSpec(
            num_scalar_prefetch=1,
            grid=(1,),
            in_specs=[resident(item.shape) for item in (*own, *other, sums_one, sums_two)],
            out_specs=[resident((72, LANES))] * 2,
        ),
        out_shape=[jax.ShapeDtypeStruct((72, LANES), WIDE)] * 2,
        name="pack",
        compiler_params=pltpu.CompilerParams(vmem_limit_bytes=56 * 1024 * 1024),
    )(spots, *own, *other, sums_one, sums_two)


def input_kernel(grad_ref, weight_ref, rows_ref, above_ref, gain_ref, out_ref, sums_ref):
    pulled_sum = dot(grad_ref[0, 0], weight_ref[0], 1, 1)
    for i in range(1, 4):
        pulled_sum = pulled_sum + dot(grad_ref[i, 0], weight_ref[i], 1, 1)
    pulled, gain_grad, shift_grad = norm_back(
        rows_ref[0].astype(WIDE), gain_ref[...].astype(WIDE), pulled_sum
    )
    out_ref[0] = (above_ref[0] + pulled).astype(LOW)

    @pl.when(pl.program_id(0) == 0)
    def _():
        sums_ref[...] = jnp.zeros_like(sums_ref)

    sums_ref[0:1, :] += gain_grad
    sums_ref[1:2, :] += shift_grad


def input_step(grads, weights, rows, above, gain):
    pairs, seq, width = rows.shape
    block = lambda: pl.BlockSpec((1, seq, width), lambda p: (p, 0, 0))
    return pl.pallas_call(
        input_kernel,
        grid=(pairs,),
        in_specs=[
            pl.BlockSpec((4, 1, seq, 768), lambda p: (0, p, 0, 0)),
            resident(weights.shape),
            block(),
            block(),
            resident((1, width)),
        ],
        out_specs=[block(), resident((8, width))],
        out_shape=[
            jax.ShapeDtypeStruct(rows.shape, LOW),
            jax.ShapeDtypeStruct((8, width), WIDE),
        ],
        name="input_grad",
        compiler_params=pltpu.CompilerParams(vmem_limit_bytes=56 * 1024 * 1024),
    )(grads, weights, rows, above, gain)


def place_kernel(turned, spot_ref, near_ref, far_ref, *refs):
    outs = refs[-len(turned) :]
    core = pl.program_id(1) ^ spot_ref[0]
    for i, turn in enumerate(turned):
        parts = []
        for z in range(4):
            at = z ^ spot_ref[2]
            parts.append(
                jnp.where(core == 0, near_ref[at, i], far_ref[at, i])
            )
        block = jnp.concatenate(parts, 0)
        outs[i][...] = (block.T if turn else block).astype(WIDE)


def place(turned, chunk, chunks, spots, near, far, shapes, buffers):
    _, kinds, rows, width = near.shape
    source = lambda: pl.BlockSpec(
        (4, kinds, rows, width), lambda x, c, spot: (x ^ spot[1], 0, 0, 0)
    )
    specs = [
        pl.BlockSpec((width, LANES), lambda x, c, spot: (0, (c * 2 + x) * chunks + chunk))
        if turn
        else pl.BlockSpec((LANES, width), lambda x, c, spot: ((c * 2 + x) * chunks + chunk, 0))
        for turn in turned
    ]
    return pl.pallas_call(
        functools.partial(place_kernel, turned),
        grid_spec=pltpu.PrefetchScalarGridSpec(
            num_scalar_prefetch=1,
            grid=(2, 2),
            in_specs=[source(), source()] + [ANYWHERE] * len(buffers),
            out_specs=specs,
        ),
        out_shape=[jax.ShapeDtypeStruct(shape, WIDE) for shape in shapes],
        input_output_aliases={3 + i: i for i in range(len(buffers))},
        name="place",
        compiler_params=pltpu.CompilerParams(vmem_limit_bytes=56 * 1024 * 1024),
    )(spots, near, far, *buffers)


def gathered_kernel(source_ref, *refs):
    up_ref, down_ref = refs[-2:]
    rows = [[source_ref[high, low, 0, 0] for high in range(2)] for low in range(2)]
    for kind, out_ref in enumerate((up_ref, down_ref)):
        parts = []
        for sub in range(2):
            for low in range(2):
                for high in range(2):
                    parts.append(rows[low][high][2 * sub + kind])
        block = jnp.concatenate(parts, 0)
        out_ref[...] = (block.T if kind == 0 else block).astype(WIDE)


def gathered(chunk, chunks, source, shapes, buffers):
    kinds, rows, width = source.shape[1:]
    source = source.reshape((2, 2, 2, 2, kinds, rows, width))
    span = 2 * LANES
    return pl.pallas_call(
        gathered_kernel,
        grid=(2, 2),
        in_specs=[
            pl.BlockSpec((2, 2, 1, 1, kinds, rows, width), lambda c, x: (0, 0, x, c, 0, 0, 0))
        ]
        + [ANYWHERE] * len(buffers),
        out_specs=[
            pl.BlockSpec((width, span), lambda c, x: (0, (c * 2 + x) * chunks + chunk)),
            pl.BlockSpec((span, width), lambda c, x: ((c * 2 + x) * chunks + chunk, 0)),
        ],
        out_shape=[jax.ShapeDtypeStruct(shape, WIDE) for shape in shapes],
        input_output_aliases={1 + i: i for i in range(len(buffers))},
        name="gathered",
        compiler_params=pltpu.CompilerParams(vmem_limit_bytes=56 * 1024 * 1024),
    )(source, *buffers)


def paired_body(
    layer_in,
    patch_count,
    attn_gain,
    attn_shift,
    query_weight,
    query_bias,
    key_weight,
    value_weight,
    value_bias,
    out_weight,
    out_bias,
    mlp_gain,
    mlp_shift,
    up_weight,
    up_bias,
    down_weight,
    down_bias,
    layer_cot,
):
    groups = lax.axis_size("dp")
    rank = lax.axis_index("dp")
    half_id = lax.axis_index("mp")
    core_id, x_id, zlow_id, zhigh_id = rank & 1, (rank >> 1) & 1, (rank >> 2) & 1, (rank >> 3) & 1
    part = core_id * 2 + x_id
    spots = jnp.stack([part, part ^ 1, part ^ 2, part ^ 3]).astype(jnp.int32)
    sides = jnp.stack([x_id, x_id ^ 1, x_id, x_id ^ 1]).astype(jnp.int32)
    place_spots = jnp.stack([core_id, x_id, zlow_id * 2 + zhigh_id]).astype(jnp.int32)

    swap = lambda value, bit: flip(value, "dp", bit, groups)
    across = lambda value: flip(value, "mp", 1, 2)

    rows, width = layer_in.shape
    heads_width = query_weight.shape[1]
    hidden_width = up_weight.shape[1]
    block = hidden_width // 4
    pairs = rows // SEQ
    counts = pick(patch_count, half_id, pairs, 0)
    row_vec = lambda vec: vec.reshape(1, -1)

    gate = lambda value, *waits: after(value, *waits) if waits else value
    shape_three = (pairs, SEQ, width)
    subs = block // LANES

    slice_rows = LANES // 2
    slice_at = (rank // 4) * 2 * subs + rank % 4
    slices = jnp.stack(
        [
            jnp.stack(
                [
                    pick(up_weight, slice_at + 4 * i, slice_rows, 1).T,
                    pick(down_weight, slice_at + 4 * i, slice_rows, 0),
                ]
            )
            for i in range(2)
        ]
    )
    slices = across(slices)
    sent_qkv = jnp.stack(
        [pick(w, core_id, heads_width // 2, 1) for w in (query_weight, key_weight, value_weight)]
    )
    sent_bias = jnp.concatenate([query_bias, value_bias, up_bias])
    near_qkv = across(sent_qkv)
    bias_other = across(sent_bias)
    rows_in = layer_in.astype(WIDE)
    normed = layer_norm(
        rows_in, attn_gain.astype(WIDE), attn_shift.astype(WIDE)
    ).astype(LOW)
    normed_three = normed.reshape(shape_three)

    def own_inputs():
        weights = [
            (w, pl.BlockSpec((width, LANES), lambda g, p, spot, count, i=i: (0, spot[2 * g + i])))
            for w in (query_weight, key_weight, value_weight)
            for i in range(2)
        ]
        biases = [
            (row_vec(b), pl.BlockSpec((1, LANES), lambda g, p, spot, count, i=i: (0, spot[2 * g + i])))
            for b in (query_bias, value_bias)
            for i in range(2)
        ]
        return weights, biases

    def other_inputs(group, qkv):
        weights = [
            (qkv, pl.BlockSpec((None, width, LANES), lambda g, p, side, count, k=k, i=i: (k, 0, side[i])))
            for k in range(3)
            for i in range(2)
        ]
        biases = [
            (b, pl.BlockSpec((1, LANES), lambda g, p, side, count, i=i: (0, side[4 + 2 * group + i])))
            for b in (query_bias_other, value_bias_other)
            for i in range(2)
        ]
        return weights, biases

    other_spots = jnp.concatenate([sides, spots])
    slices = after(slices, normed)
    gathered_weights = [lax.all_gather(slices[0], "dp"), lax.all_gather(slices[1], "dp")]
    kept = attend(
        0, 2, gate(spots, sent_qkv, sent_bias, slices), counts, normed_three, *own_inputs(), []
    )
    near_qkv, bias_other, _ = lax.optimization_barrier((near_qkv, bias_other, kept[1]))
    query_bias_other = row_vec(bias_other[:heads_width])
    value_bias_other = row_vec(bias_other[heads_width : 2 * heads_width])
    up_bias_other = row_vec(bias_other[2 * heads_width :])
    sent_out = after(pick(out_weight, core_id, heads_width // 2, 0), near_qkv)
    near_out = across(sent_out)
    far_qkv = swap(near_qkv, CORE)
    kept = attend(
        2, 1, gate(other_spots, sent_out), counts, normed_three, *other_inputs(0, near_qkv), kept
    )
    near_out, far_qkv, _ = lax.optimization_barrier((near_out, far_qkv, kept[1]))
    far_out = swap(near_out, CORE)
    kept = attend(
        3, 1, gate(other_spots, near_out), counts, normed_three, *other_inputs(1, far_qkv), kept
    )
    middle, hidden, outs_all = middle_step(
        jnp.concatenate([spots, sides]),
        layer_in.reshape(shape_three),
        kept[1],
        out_weight,
        near_out,
        far_out,
        row_vec(out_bias),
        row_vec(mlp_gain),
        row_vec(mlp_shift),
    )
    middle = middle.reshape(rows, width)
    hidden = hidden.reshape(rows, width)

    def own_mlp(first):
        ups = [
            (up_weight, pl.BlockSpec((width, LANES), lambda j, spot, r=r: (0, spot[r] * subs + first + j)))
            for r in range(4)
        ]
        downs = [
            (down_weight, pl.BlockSpec((LANES, width), lambda j, spot, r=r: (spot[r] * subs + first + j, 0)))
            for r in range(4)
        ]
        biases = [
            (row_vec(up_bias), pl.BlockSpec((1, LANES), lambda j, spot, r=r: (0, spot[r] * subs + first + j)))
            for r in range(4)
        ]
        return ups, downs, biases

    def other_mlp(first):
        source = gathered_weights[first // 2]
        ups, downs = (
            [
                (source, pl.BlockSpec((2, 1, slice_rows, width), lambda j, spot, r=r, k=k: (spot[r] * 2 + j, k, 0, 0)))
                for r in range(4)
            ]
            for k in range(2)
        )
        biases = [
            (up_bias_other, pl.BlockSpec((1, LANES), lambda j, spot, r=r: (0, spot[r] * subs + first + j)))
            for r in range(4)
        ]
        return ups, downs, biases

    def cut(item, index):
        count, lanes, cols = item.shape
        return pick(item.reshape(count, 2, lanes // 2, cols), index, 1, 1)[:, 0]

    def outbound(near, far, first, last):
        return total(near[:, first:last], far[:, first:last])

    def sideways(near, far, beyond, first, last):
        return total(near[1, first:last], far[1, first:last], beyond[1])

    def collected(near, far, beyond, side, first, last):
        return total(near[0, first:last], far[0, first:last], beyond[0], side)

    def halves(item):
        return cut(item, zlow_id ^ 1), cut(item, zlow_id)

    def quarters(item):
        return cut(item, zhigh_id ^ 1), cut(item, zhigh_id)

    back = lambda slot, wait, qkv_grads: attend_back(
        slot, gate(counts, *wait), normed, attn_grad, kept, outs_all, qkv_grads
    )

    together = lambda *items: lax.optimization_barrier(items)
    other_a = mlp(2, True, spots, hidden, layer_cot, *other_mlp(0), [])
    far_other_a = swap(other_a[1], CORE)
    own_a = mlp(0, False, spots, hidden, layer_cot, *own_mlp(0), other_a[3:])
    far_other_a, far, _ = together(far_other_a, own_a[1], own_a[2])
    far_own_a = swap(far, CORE)
    out_a = [outbound(other_a[0], far_other_a, *span) for span in ((0, 1), (1, 2), (2, 4))]
    own_b = mlp(6, False, gate(spots, *out_a), hidden, layer_cot, *own_mlp(2), own_a[3:])
    beyond_a0, far_own_a, far, _ = together(across(out_a[0]), far_own_a, own_b[1], own_b[2])
    far_own_b = swap(far, CORE)
    other_b = mlp(
        4, True, gate(spots, beyond_a0, far_own_a), hidden, layer_cot, *other_mlp(2), own_b[3:]
    )
    acts, pre_grads, ups_all, downs_all = other_b[3:]
    beyond_a1, far_own_b, far, _ = together(
        across(after(out_a[1], beyond_a0)), far_own_b, other_b[1], other_b[2]
    )
    far_other_b = swap(far, CORE)
    beyond_a01 = jnp.concatenate([beyond_a0, beyond_a1], 1)
    side_a01 = sideways(own_a[0], far_own_a, beyond_a01, 0, 2)
    middle_grad, attn_grad, sums_two = mlp_back(
        pre_grads, ups_all, middle, layer_cot, gate(row_vec(mlp_gain), side_a01, beyond_a01, far_own_b)
    )
    beyond_a23, arrived_a01, far_other_b, _ = together(
        across(after(out_a[2], beyond_a1)), swap(side_a01, XBIT), far_other_b, sums_two
    )
    side_a23 = sideways(own_a[0], far_own_a, beyond_a23, 2, 4)
    out_b = [outbound(other_b[0], far_other_b, *span) for span in ((0, 2), (2, 4))]
    other_far, bias_other_far, qkv_grads = back(3, (side_a23, arrived_a01, *out_b), [])
    beyond_b01, arrived_a23, far, _ = together(
        across(out_b[0]), swap(side_a23, XBIT), other_far, bias_other_far
    )
    late_other_far = swap(far, CORE)
    sum_a = jnp.concatenate(
        [
            collected(own_a[0], far_own_a, beyond_a01, arrived_a01, 0, 2),
            collected(own_a[0], far_own_a, beyond_a23, arrived_a23, 2, 4),
        ]
    )
    low_a, keep_a = halves(sum_a)
    side_b01 = sideways(own_b[0], far_own_b, beyond_b01, 0, 2)
    other_near, bias_other_near, qkv_grads = back(2, (low_a, sum_a, side_b01), [qkv_grads])
    beyond_b23, arrived_b01, low_a, late_other_far, _ = together(
        across(after(out_b[1], beyond_b01)), swap(side_b01, XBIT), swap(low_a, ZLOW), late_other_far, bias_other_near
    )
    high_a, keep_a = quarters(total(keep_a, low_a))
    side_b23 = sideways(own_b[0], far_own_b, beyond_b23, 2, 4)
    late_out = [outbound(other_near, late_other_far, *span) for span in ((0, 2), (2, 4))]
    own_far, bias_own_far, qkv_grads = back(1, (high_a, side_b23, arrived_b01, *late_out), [qkv_grads])
    late_beyond0, arrived_b23, high_a, far, _ = together(
        across(late_out[0]), swap(side_b23, XBIT), swap(high_a, ZHIGH), own_far, bias_own_far
    )
    late_own_far = swap(far, CORE)
    one_a = total(keep_a, high_a)
    sum_b = jnp.concatenate(
        [
            collected(own_b[0], far_own_b, beyond_b01, arrived_b01, 0, 2),
            collected(own_b[0], far_own_b, beyond_b23, arrived_b23, 2, 4),
        ]
    )
    low_b, keep_b = halves(sum_b)
    gathered_a = lax.all_gather(one_a, "dp")
    own_near, bias_own_near, qkv_grads = back(0, (one_a, low_b, sum_b, late_beyond0), [qkv_grads])
    late_beyond1, late_own_far, low_b, _ = together(
        across(after(late_out[1], late_beyond0)), late_own_far, swap(low_b, ZLOW), bias_own_near
    )
    high_b, keep_b = quarters(total(keep_b, low_b))
    late_side0 = sideways(own_near, late_own_far, late_beyond0, 0, 2)
    late_side1 = sideways(own_near, late_own_far, late_beyond1, 2, 4)
    grad_in, sums_one = input_step(
        qkv_grads,
        kept[2],
        layer_in.reshape(shape_three),
        middle_grad.reshape(shape_three),
        gate(row_vec(attn_gain), high_b, late_side0, late_side1),
    )
    high_b, late_arrived0, sums_one = together(swap(high_b, ZHIGH), swap(late_side0, XBIT), sums_one)
    one_b = total(keep_b, high_b)
    gathered_b = lax.all_gather(one_b, "dp")
    quarter_id = zlow_id * 2 + zhigh_id
    z_bits = [None, ZHIGH, ZLOW, ZLOW | ZHIGH]

    def four(item):
        count, lanes, cols = item.shape
        item = item.reshape(count, 4, lanes // 4, cols)
        return [pick(item, quarter_id ^ r, 1, 1)[:, 0] for r in range(4)]

    def send_four(items):
        return [swap(items[r], z_bits[r]) for r in range(1, 4)]

    late_four0 = four(collected(own_near, late_own_far, late_beyond0, late_arrived0, 0, 2))
    own_vec, other_vec = pack(
        spots,
        (bias_own_near, bias_own_far, own_a[2], own_b[2]),
        (bias_other_near, bias_other_far, other_a[2], other_b[2]),
        sums_one,
        sums_two,
    )
    layer_out = mlp_out(
        0, acts, downs_all, middle, gate(row_vec(down_bias), one_b, other_vec, *late_four0), []
    )
    late_arrived1, late_got0, vec_got, mark = together(
        swap(after(late_side1, late_arrived0), XBIT), send_four(late_four0), across(other_vec), layer_out
    )
    late_one0 = total(late_four0[0], *late_got0)
    late_four1 = four(collected(own_near, late_own_far, late_beyond1, late_arrived1, 2, 4))
    vec = own_vec + vec_got
    layer_out = mlp_out(
        1, acts, downs_all, middle, gate(row_vec(down_bias), late_one0, vec, *late_four1), [mark]
    )
    late_got1, late_have0, vec_got, layer_out = together(
        send_four(late_four1), send_four([late_one0] * 4), swap(vec, CORE), layer_out
    )
    late_one1 = total(late_four1[0], *late_got1)
    late_have0 = jnp.stack([late_one0, *late_have0])
    vec = vec + vec_got
    up_shape, down_shape = up_weight.shape, down_weight.shape
    placed = gathered(
        0, 2, gate(gathered_a, late_one1, late_have0, vec), (up_shape, down_shape), []
    )
    late_have1, late_side0, vec_got, *placed = together(
        send_four([late_one1] * 4), swap(late_have0, XBIT), swap(vec, XBIT), *placed
    )
    late_have1 = jnp.stack([late_one1, *late_have1])
    late_have0 = jnp.concatenate([late_have0, late_side0])
    vec = vec + vec_got
    placed = gathered(
        1, 2, gate(gathered_b, late_have1, late_have0, vec), (up_shape, down_shape), placed
    )
    late_side1, late_far0, vec_got, grad_up_weight, grad_down_weight = together(
        swap(late_have1, XBIT), swap(late_have0, CORE), send_four([vec] * 4), *placed
    )
    late_have1 = jnp.concatenate([late_have1, late_side1])
    vec = ((vec + vec_got[0]) + (vec_got[1] + vec_got[2])).reshape(-1)
    grad_query_weight, grad_key_weight = place(
        (True, True), 0, 1, gate(place_spots, late_have1), late_have0, late_far0, (query_weight.shape,) * 2, []
    )
    late_far1, grad_query_weight, grad_key_weight = together(
        swap(late_have1, CORE), grad_query_weight, grad_key_weight
    )
    grad_value_weight, grad_out_weight = place(
        (True, False), 0, 1, place_spots, late_have1, late_far1, (value_weight.shape, out_weight.shape), []
    )
    grad_query_bias = vec[:heads_width]
    grad_value_bias = vec[heads_width : 2 * heads_width]
    grad_up_bias = vec[2 * heads_width : 2 * heads_width + hidden_width]
    (
        grad_attn_gain,
        grad_attn_shift,
        grad_out_bias,
        grad_mlp_gain,
        grad_mlp_shift,
        grad_down_bias,
    ) = jnp.split(vec[2 * heads_width + hidden_width :], 6)
    return (
        layer_out,
        grad_in.reshape(rows, width),
        grad_attn_gain,
        grad_attn_shift,
        grad_query_weight,
        grad_query_bias,
        grad_key_weight,
        grad_value_weight,
        grad_value_bias,
        grad_out_weight,
        grad_out_bias,
        grad_mlp_gain,
        grad_mlp_shift,
        grad_up_weight,
        grad_up_bias,
        grad_down_weight,
        grad_down_bias,
    )


def solution(mesh):
    paired = mesh.shape["mp"] == 2 and mesh.shape["dp"] == 16
    body = paired_body if paired else general_body
    placed = (
        P(("dp", "mp"), None),
        P("dp"),
        P(),
        P(),
        P(None, "mp"),
        P("mp"),
        P(None, "mp"),
        P(None, "mp"),
        P("mp"),
        P("mp", None),
        P(),
        P(),
        P(),
        P(None, "mp"),
        P("mp"),
        P("mp", None),
        P(),
        P(("dp", "mp"), None),
    )
    return jax.shard_map(
        body,
        mesh=mesh,
        in_specs=placed,
        out_specs=(
            P(("dp", "mp"), None),
            P(("dp", "mp"), None),
            P(),
            P(),
            P(None, "mp"),
            P("mp"),
            P(None, "mp"),
            P(None, "mp"),
            P("mp"),
            P("mp", None),
            P(),
            P(),
            P(),
            P(None, "mp"),
            P("mp"),
            P("mp", None),
            P(),
        ),
        check_vma=False,
    )
```

```python
import functools

import jax
import jax.numpy as jnp
from jax import lax
from jax.experimental import pallas as pl
from jax.experimental.pallas import tpu as pltpu
from jax.sharding import PartitionSpec as P

HEAD_DIM = 64
TEXT = 40
SEQ = 280


EPS = 1e-05
SCALE = 0.125
NEGATIVE = -1e30


def layer_norm(values, gain, shift):
    center = values - jnp.mean(values, -1, keepdims=True)
    spread = jnp.mean(center * center, -1, keepdims=True)
    return center * lax.rsqrt(spread + EPS) * gain + shift


def exact_gelu(values):
    return jax.nn.gelu(values, approximate=False)


def matmul_rows(left, right):
    return jnp.dot(left, right, preferred_element_type=jnp.float32)


def contract_rows(left, right):
    return lax.dot_general(
        left, right, (((0,), (0,)), ((), ())), preferred_element_type=jnp.float32
    )


def contract_cols(left, right):
    return lax.dot_general(
        left, right, (((1,), (1,)), ((), ())), preferred_element_type=jnp.float32
    )


def column_sum(values):
    return jnp.sum(values.astype(jnp.float32), 0)


def general_body(
    layer_in,
    patch_count,
    attn_gain,
    attn_shift,
    query_weight,
    query_bias,
    key_weight,
    value_weight,
    value_bias,
    out_weight,
    out_bias,
    mlp_gain,
    mlp_shift,
    up_weight,
    up_bias,
    down_weight,
    down_bias,
    layer_cot,
):
    lowtype = jnp.bfloat16
    wide = jnp.float32
    rows_in = layer_in.astype(wide)
    gain_one = attn_gain.astype(wide)
    shift_one = attn_shift.astype(wide)
    gain_two = mlp_gain.astype(wide)
    shift_two = mlp_shift.astype(wide)
    normed_tok, norm_pull = jax.vjp(layer_norm, rows_in, gain_one, shift_one)
    group_rows = lax.all_gather(normed_tok.astype(lowtype), "mp", axis=0, tiled=True)
    query_rows = (matmul_rows(group_rows, query_weight) + query_bias.astype(wide)).astype(lowtype)
    key_rows = matmul_rows(group_rows, key_weight).astype(lowtype)
    value_rows = (matmul_rows(group_rows, value_weight) + value_bias.astype(wide)).astype(lowtype)
    pairs = patch_count.shape[0]
    local_width = query_weight.shape[1]
    local_heads = local_width // HEAD_DIM
    group_total = group_rows.shape[0]
    shape_four = (pairs, SEQ, local_heads, HEAD_DIM)
    query_blk = query_rows.reshape(shape_four)
    key_blk = key_rows.reshape(shape_four)
    value_blk = value_rows.reshape(shape_four)
    scores = jnp.einsum("pqhd,pkhd->phqk", query_blk, key_blk, preferred_element_type=wide) * SCALE
    valid = jnp.arange(SEQ)[None, :] < (TEXT + patch_count)[:, None]
    scores = jnp.where(valid[:, None, None, :], scores, NEGATIVE)
    probs = jax.nn.softmax(scores, axis=-1)
    probs_low = probs.astype(lowtype)
    context = jnp.einsum("phqk,pkhd->pqhd", probs_low, value_blk, preferred_element_type=wide)
    context = context.astype(lowtype).reshape(group_total, local_width)
    context_tok = lax.all_to_all(context, "mp", split_axis=0, concat_axis=1, tiled=True)
    out_full = lax.all_gather(out_weight, "mp", axis=0, tiled=True)
    attended = matmul_rows(context_tok, out_full) + out_bias.astype(wide)
    middle = rows_in + attended
    hidden_wide, mlp_pull = jax.vjp(layer_norm, middle, gain_two, shift_two)
    hidden_in = hidden_wide.astype(lowtype)
    cot_wide = layer_cot.astype(wide)
    up_full, bias_full, down_full = (
        lax.all_gather(up_weight, "mp", axis=1, tiled=True),
        lax.all_gather(up_bias, "mp", axis=0, tiled=True),
        lax.all_gather(down_weight, "mp", axis=0, tiled=True),
    )
    pre_act = matmul_rows(hidden_in, up_full) + bias_full.astype(wide)
    act_wide, gelu_pull = jax.vjp(exact_gelu, pre_act)
    act_low = act_wide.astype(lowtype)
    ffn_out = matmul_rows(act_low, down_full) + down_bias.astype(wide)
    whole_down = contract_rows(act_low, layer_cot)
    act_grad = contract_cols(layer_cot, down_full)
    pre_grad = gelu_pull(act_grad)[0].astype(lowtype)
    whole_up_bias = column_sum(pre_grad)
    whole_up = contract_rows(hidden_in, pre_grad)
    hidden_grad = contract_cols(pre_grad, up_full)
    grad_up_weight, grad_up_bias, grad_down_weight = (
        lax.psum_scatter(
            whole_up.astype(jnp.bfloat16), "mp", scatter_dimension=1, tiled=True
        ).astype(jnp.float32),
        lax.psum_scatter(
            whole_up_bias.astype(jnp.bfloat16), "mp", scatter_dimension=0, tiled=True
        ).astype(jnp.float32),
        lax.psum_scatter(
            whole_down.astype(jnp.bfloat16), "mp", scatter_dimension=0, tiled=True
        ).astype(jnp.float32),
    )
    layer_out = (middle + ffn_out).astype(lowtype)
    grad_down_bias = column_sum(layer_cot)
    middle_part, grad_gain_two, grad_shift_two = mlp_pull(hidden_grad)
    middle_grad = cot_wide + middle_part
    attn_grad = middle_grad.astype(lowtype)
    grad_out_bias = column_sum(attn_grad)
    grad_out_weight = lax.psum_scatter(
        contract_rows(context_tok, attn_grad).astype(jnp.bfloat16),
        "mp",
        scatter_dimension=0,
        tiled=True,
    ).astype(jnp.float32)
    context_grad_tok = contract_cols(attn_grad, out_full).astype(lowtype)
    context_grad = lax.all_to_all(
        context_grad_tok, "mp", split_axis=1, concat_axis=0, tiled=True
    ).reshape(shape_four)
    probs_grad = jnp.einsum("pqhd,pkhd->phqk", context_grad, value_blk, preferred_element_type=wide)
    value_grad = jnp.einsum("phqk,pqhd->pkhd", probs_low, context_grad, preferred_element_type=wide)
    value_grad = value_grad.astype(lowtype).reshape(group_total, local_width)
    score_grad = (probs * (probs_grad - jnp.sum(probs * probs_grad, -1, keepdims=True))).astype(
        lowtype
    )
    query_grad = (
        jnp.einsum("phqk,pkhd->pqhd", score_grad, key_blk, preferred_element_type=wide) * SCALE
    )
    query_grad = query_grad.astype(lowtype).reshape(group_total, local_width)
    key_grad = (
        jnp.einsum("phqk,pqhd->pkhd", score_grad, query_blk, preferred_element_type=wide) * SCALE
    )
    key_grad = key_grad.astype(lowtype).reshape(group_total, local_width)
    grad_query_weight = contract_rows(group_rows, query_grad)
    grad_key_weight = contract_rows(group_rows, key_grad)
    grad_value_weight = contract_rows(group_rows, value_grad)
    grad_query_bias = column_sum(query_grad)
    grad_value_bias = column_sum(value_grad)
    total = contract_cols(query_grad, query_weight)
    total = total + contract_cols(key_grad, key_weight)
    normed_grad = lax.psum_scatter(
        (total + contract_cols(value_grad, value_weight)).astype(jnp.bfloat16),
        "mp",
        scatter_dimension=0,
        tiled=True,
    ).astype(jnp.float32)
    input_part, grad_gain_one, grad_shift_one = norm_pull(normed_grad)
    grad_in = (middle_grad + input_part).astype(lowtype)
    (
        grad_query_weight,
        grad_query_bias,
        grad_key_weight,
        grad_value_weight,
        grad_value_bias,
        grad_out_weight,
        grad_up_weight,
        grad_up_bias,
        grad_down_weight,
    ) = (
        lax.psum(grad_query_weight.astype(jnp.bfloat16), "dp").astype(jnp.float32),
        lax.psum(grad_query_bias.astype(jnp.bfloat16), "dp").astype(jnp.float32),
        lax.psum(grad_key_weight.astype(jnp.bfloat16), "dp").astype(jnp.float32),
        lax.psum(grad_value_weight.astype(jnp.bfloat16), "dp").astype(jnp.float32),
        lax.psum(grad_value_bias.astype(jnp.bfloat16), "dp").astype(jnp.float32),
        lax.psum(grad_out_weight.astype(jnp.bfloat16), "dp").astype(jnp.float32),
        lax.psum(grad_up_weight.astype(jnp.bfloat16), "dp").astype(jnp.float32),
        lax.psum(grad_up_bias.astype(jnp.bfloat16), "dp").astype(jnp.float32),
        lax.psum(grad_down_weight.astype(jnp.bfloat16), "dp").astype(jnp.float32),
    )
    grad_gain_one, grad_shift_one, grad_out_bias, grad_gain_two, grad_shift_two, grad_down_bias = (
        lax.psum(
            (
                grad_gain_one,
                grad_shift_one,
                grad_out_bias,
                grad_gain_two,
                grad_shift_two,
                grad_down_bias,
            ),
            ("dp", "mp"),
        )
    )
    return (
        layer_out,
        grad_in,
        grad_gain_one,
        grad_shift_one,
        grad_query_weight,
        grad_query_bias,
        grad_key_weight,
        grad_value_weight,
        grad_value_bias,
        grad_out_weight,
        grad_out_bias,
        grad_gain_two,
        grad_shift_two,
        grad_up_weight,
        grad_up_bias,
        grad_down_weight,
        grad_down_bias,
    )


WIDE = jnp.float32
LOW = jnp.bfloat16
LANES = 128
ROOT_HALF = 0.7071067811865476
NORMAL = 0.3989422804014327
CORE, XBIT, ZLOW, ZHIGH = 1, 2, 4, 8


def dot(left, right, left_dim, right_dim):
    return lax.dot_general(
        left, right, (((left_dim,), (right_dim,)), ((), ())), preferred_element_type=WIDE
    )


def flip(value, axis, bit, size):
    return lax.ppermute(value, axis, [(i, i ^ bit) for i in range(size)])


def pick(value, index, width, axis):
    return lax.dynamic_slice_in_dim(value, index * width, width, axis)


def after(value, *others):
    return lax.optimization_barrier((value,) + others)[0]


def total(*items):
    result = items[0].astype(WIDE)
    for item in items[1:]:
        result = result + item.astype(WIDE)
    return result.astype(LOW)


def resident(shape):
    return pl.BlockSpec(shape, lambda *_: (0,) * len(shape), pipeline_mode=pl.Buffered(1))


ANYWHERE = pl.BlockSpec(memory_space=pl.ANY)


def attend_kernel(spot_ref, count_ref, rows_ref, *refs):
    weights, biases = refs[:6], refs[6:10]
    qkv_ref, context_ref, weight_ref, bias_ref = refs[-4:]
    pair = pl.program_id(1)

    @pl.when(pair == 0)
    def _():
        for i in range(6):
            weight_ref[0, :, i * LANES : (i + 1) * LANES] = weights[i][...]
        bias_ref[...] = jnp.zeros_like(bias_ref)
        for i in range(2):
            bias_ref[:, i * LANES : (i + 1) * LANES] = biases[i][...].astype(WIDE)
            bias_ref[:, (4 + i) * LANES : (5 + i) * LANES] = biases[2 + i][...].astype(WIDE)

    qkv = (dot(rows_ref[0], weight_ref[0], 1, 0) + bias_ref[...]).astype(LOW)
    qkv_ref[0, 0] = qkv
    length = TEXT + count_ref[pair]
    lane = lax.broadcasted_iota(jnp.int32, (SEQ, LANES), 1)
    padding = lax.broadcasted_iota(jnp.int32, (SEQ, SEQ), 1) >= length
    lane_low = lane < HEAD_DIM
    everything = []
    for tile in range(2):
        query, key, value = (
            qkv[:, i * 256 + tile * LANES : i * 256 + (tile + 1) * LANES] for i in range(3)
        )
        query = query * SCALE
        for side in range(2):
            mine = lane_low if side == 0 else jnp.logical_not(lane_low)
            everything.append((dot(jnp.where(mine, query, jnp.zeros_like(query)), key, 1, 1), value))
    heads = []
    for scores, value in everything:
        scores = jnp.where(padding, NEGATIVE, scores)
        power = jnp.exp(scores - jnp.max(scores, -1, keepdims=True))
        inverse = 1.0 / jnp.sum(power, -1, keepdims=True)
        heads.append(dot(power.astype(LOW), value, 1, 0) * inverse)
    for tile in range(2):
        context_ref[0, 0, :, tile * LANES : (tile + 1) * LANES] = jnp.where(
            lane_low, heads[2 * tile], heads[2 * tile + 1]
        ).astype(LOW)


def attend(slot, groups, spots, counts, rows, weights, biases, buffers):
    pairs, seq, width = rows.shape
    shapes = [
        ((4, pairs, seq, 768), (1, 1, seq, 768), lambda g, p, *_: (slot + g, p, 0, 0)),
        ((4, pairs, seq, 256), (1, 1, seq, 256), lambda g, p, *_: (slot + g, p, 0, 0)),
        ((4, width, 768), (1, width, 768), lambda g, p, *_: (slot + g, 0, 0)),
    ]
    operands = list(weights) + list(biases)
    aliases = {3 + len(operands) + i: i for i in range(len(buffers))}
    return pl.pallas_call(
        attend_kernel,
        grid_spec=pltpu.PrefetchScalarGridSpec(
            num_scalar_prefetch=2,
            grid=(groups, pairs),
            in_specs=[pl.BlockSpec((1, seq, width), lambda g, p, *_: (p, 0, 0))]
            + [spec for _, spec in operands]
            + [ANYWHERE] * len(buffers),
            out_specs=[pl.BlockSpec(block, index) for _, block, index in shapes],
            scratch_shapes=[pltpu.VMEM((1, 768), WIDE)],
        ),
        out_shape=[jax.ShapeDtypeStruct(shape, LOW) for shape, _, _ in shapes],
        input_output_aliases=aliases,
        name="attend",
        compiler_params=pltpu.CompilerParams(vmem_limit_bytes=56 * 1024 * 1024),
    )(spots, counts, rows, *[array for array, _ in operands], *buffers)


def attend_back_kernel(count_ref, rows_hbm, cots_hbm, cot_ref, qkv_ref, context_ref, out_ref, *refs):
    near_ref, bias_ref, qkv_grad_ref, grad_buf, context_buf, rows_buf, cots_buf, sems = refs[-8:]
    pair = pl.program_id(0)
    copies = [
        pltpu.make_async_copy(rows_hbm, rows_buf, sems.at[0]),
        pltpu.make_async_copy(cots_hbm, cots_buf, sems.at[1]),
    ]

    @pl.when(pair == 0)
    def _():
        for copy in copies:
            copy.start()

    at = pl.ds(pl.multiple_of(pair * SEQ, 8), SEQ)
    context_grad = dot(cot_ref[0], out_ref[0], 1, 1).astype(LOW)
    qkv = qkv_ref[0, 0]
    context_buf[at, :] = context_ref[0, 0].astype(WIDE)
    length = TEXT + count_ref[pair]
    lane = lax.broadcasted_iota(jnp.int32, (SEQ, LANES), 1)
    padding = lax.broadcasted_iota(jnp.int32, (SEQ, SEQ), 0) >= length
    grads = [[], [], []]
    lane_low = lane < HEAD_DIM
    work = []
    for tile in range(2):
        query, key, value = (
            qkv[:, i * 256 + tile * LANES : i * 256 + (tile + 1) * LANES] for i in range(3)
        )
        query = query * SCALE
        outer = context_grad[:, tile * LANES : (tile + 1) * LANES]
        for side in range(2):
            mine = lane_low if side == 0 else jnp.logical_not(lane_low)
            scores = dot(jnp.where(mine, key, jnp.zeros_like(key)), query, 1, 1)
            probs_grad = dot(jnp.where(mine, value, jnp.zeros_like(value)), outer, 1, 1)
            work.append((scores, probs_grad, query, key, outer))
    heads = []
    for scores, probs_grad, query, key, outer in work:
        scores = jnp.where(padding, NEGATIVE, scores)
        power = jnp.exp(scores - jnp.max(scores, 0, keepdims=True))
        probs = power * (1.0 / jnp.sum(power, 0, keepdims=True))
        both = probs * probs_grad
        score_grad = (both - probs * jnp.sum(both, 0, keepdims=True)).astype(LOW)
        heads.append(
            (dot(score_grad, key, 0, 0), dot(score_grad, query, 1, 0), dot(probs.astype(LOW), outer, 1, 0))
        )
    for tile in range(2):
        for i, scale in enumerate((SCALE, 1.0, 1.0)):
            pair_of = [heads[2 * tile + side][i] for side in range(2)]
            grads[i].append((jnp.where(lane_low, *pair_of) * scale).astype(LOW))
    joined = jnp.concatenate(grads[0] + grads[1] + grads[2], 1)
    qkv_grad_ref[0] = joined
    grad_buf[at, :] = joined.astype(WIDE)

    @pl.when(pair == pl.num_programs(0) - 1)
    def _():
        for copy in copies:
            copy.wait()
        stacked = dot(grad_buf[...].astype(LOW), rows_buf[...], 0, 0).astype(LOW)
        outs = dot(context_buf[...].astype(LOW), cots_buf[...], 0, 0).astype(LOW)
        for i in range(2):
            near_ref[i, :3] = stacked.reshape(3, 2, LANES, -1)[:, i]
            near_ref[i, 3] = outs[i * LANES : (i + 1) * LANES]
        bias_ref[...] = jnp.sum(grad_buf[...], 0, keepdims=True)


def attend_back(slot, counts, rows, cot, kept, outs):
    qkv, context, _ = kept
    _, pairs, seq, _ = qkv.shape
    width = rows.shape[1]
    return pl.pallas_call(
        attend_back_kernel,
        grid_spec=pltpu.PrefetchScalarGridSpec(
            num_scalar_prefetch=1,
            grid=(pairs,),
            in_specs=[
                ANYWHERE,
                ANYWHERE,
                pl.BlockSpec((1, seq, width), lambda p, *_: (p, 0, 0)),
                pl.BlockSpec((1, 1, seq, 768), lambda p, *_: (slot, p, 0, 0)),
                pl.BlockSpec((1, 1, seq, 256), lambda p, *_: (slot, p, 0, 0)),
                pl.BlockSpec((1, 256, width), lambda p, *_: (slot, 0, 0)),
            ],
            out_specs=[
                pl.BlockSpec((2, 4, LANES, width), lambda p, *_: (0, 0, 0, 0)),
                pl.BlockSpec((1, 768), lambda p, *_: (0, 0)),
                pl.BlockSpec((1, seq, 768), lambda p, *_: (p, 0, 0)),
            ],
            scratch_shapes=[
                pltpu.VMEM((pairs * seq, 768), WIDE),
                pltpu.VMEM((pairs * seq, 256), WIDE),
                pltpu.VMEM(rows.shape, LOW),
                pltpu.VMEM(cot.shape, LOW),
                pltpu.SemaphoreType.DMA((2,)),
            ],
        ),
        out_shape=[
            jax.ShapeDtypeStruct((2, 4, LANES, width), LOW),
            jax.ShapeDtypeStruct((1, 768), WIDE),
            jax.ShapeDtypeStruct(qkv.shape[1:], LOW),
        ],
        name="attend_back",
        compiler_params=pltpu.CompilerParams(vmem_limit_bytes=56 * 1024 * 1024),
    )(counts, rows, cot, cot.reshape(pairs, seq, width), qkv, context, outs)


def middle_kernel(
    spot_ref, rows_ref, context_ref, own_ref, near_ref, far_ref, bias_ref, gain_ref, shift_ref, *refs
):
    middle_ref, hidden_ref, out_ref = refs

    @pl.when(pl.program_id(0) == 0)
    def _():
        for i in range(8):
            source = own_ref if i < 4 else (near_ref if i < 6 else far_ref)
            start = pl.multiple_of(spot_ref[i] * LANES, LANES)
            out_ref[i // 2, (i % 2) * LANES : (i % 2 + 1) * LANES, :] = source[pl.ds(start, LANES), :]

    context = jnp.concatenate([context_ref[i, 0] for i in range(4)], 1)
    attended = dot(context, out_ref[...].reshape(-1, out_ref.shape[2]), 1, 0)
    middle = rows_ref[0].astype(WIDE) + attended + bias_ref[...].astype(WIDE)
    middle_ref[0] = middle
    center = middle - jnp.mean(middle, -1, keepdims=True)
    spread = jnp.mean(center * center, -1, keepdims=True)
    hidden = center * lax.rsqrt(spread + EPS) * gain_ref[...].astype(WIDE)
    hidden_ref[0] = (hidden + shift_ref[...].astype(WIDE)).astype(LOW)


def middle_step(spots, rows, context, own, near, far, bias, gain, shift):
    pairs, seq, width = rows.shape
    block = lambda: pl.BlockSpec((1, seq, width), lambda p, *_: (p, 0, 0))
    return pl.pallas_call(
        middle_kernel,
        grid_spec=pltpu.PrefetchScalarGridSpec(
            num_scalar_prefetch=1,
            grid=(pairs,),
            in_specs=[
                block(),
                pl.BlockSpec((4, 1, seq, 256), lambda p, *_: (0, p, 0, 0)),
                resident(own.shape),
                resident(near.shape),
                resident(far.shape),
            ]
            + [resident((1, width))] * 3,
            out_specs=[block(), block(), resident((4, 256, width))],
        ),
        out_shape=[
            jax.ShapeDtypeStruct(rows.shape, WIDE),
            jax.ShapeDtypeStruct(rows.shape, LOW),
            jax.ShapeDtypeStruct((4, 256, width), LOW),
        ],
        name="middle",
        compiler_params=pltpu.CompilerParams(vmem_limit_bytes=56 * 1024 * 1024),
    )(spots, rows, context, own, near, far, bias, gain, shift)


def mlp_kernel(step, turned, spot_ref, hidden_ref, cot_ref, *refs):
    ups, downs, biases = refs[:4], refs[4:8], refs[8:12]
    near_ref, far_ref, bias_out, act_ref, pre_ref, up_ref, down_ref, bias_ref = refs[-8:]
    rows = hidden_ref.shape[0]
    for r in range(4):
        span = slice(r * LANES, (r + 1) * LANES)
        if turned:
            up_ref[0, :, span] = ups[r][:, 0].reshape(LANES, -1).T
            down_ref[0, span, :] = downs[r][:, 0].reshape(LANES, -1)
        else:
            up_ref[0, :, span] = ups[r][...]
            down_ref[0, span, :] = downs[r][...]
        bias_ref[:, span] = biases[r][...].astype(WIDE)

    def one(i, carry):
        at = pl.ds(pl.multiple_of(i * step, step), step)
        pre_act = dot(hidden_ref[at, :], up_ref[0], 1, 0) + bias_ref[...]
        act_grad = dot(cot_ref[at, :], down_ref[0], 1, 1)
        chance = 0.5 + 0.5 * lax.erf(pre_act * ROOT_HALF)
        act_ref[0, at, :] = (pre_act * chance).astype(LOW)
        slope = chance + pre_act * (NORMAL * jnp.exp(-0.5 * pre_act * pre_act))
        pre_ref[0, at, :] = (act_grad * slope).astype(LOW)
        return carry

    lax.fori_loop(0, rows // step, one, 0)
    up_grad = dot(pre_ref[0], hidden_ref[...], 0, 0).astype(LOW).reshape(4, LANES, -1)
    down_grad = dot(act_ref[0], cot_ref[...], 0, 0).astype(LOW).reshape(4, LANES, -1)
    bias_out[0] = jnp.sum(pre_ref[0].astype(WIDE), 0, keepdims=True)
    for i in range(2):
        near_ref[i, 0] = up_grad[i]
        near_ref[i, 1] = down_grad[i]
        far_ref[i, 0] = up_grad[2 + i]
        far_ref[i, 1] = down_grad[2 + i]


def mlp(first, turned, spots, hidden, cot, ups, downs, biases, buffers):
    rows, width = hidden.shape
    operands = list(ups) + list(downs) + list(biases)
    tile = 4 * LANES
    grad = jax.ShapeDtypeStruct((2, 4, LANES, width), LOW)
    grad_block = pl.BlockSpec((2, 2, LANES, width), lambda j, *_: (0, j, 0, 0))
    return pl.pallas_call(
        functools.partial(mlp_kernel, rows // 2, turned),
        grid_spec=pltpu.PrefetchScalarGridSpec(
            num_scalar_prefetch=1,
            grid=(2,),
            in_specs=[pl.BlockSpec(memory_space=pltpu.VMEM)] * 2
            + [spec for _, spec in operands]
            + [ANYWHERE] * len(buffers),
            out_specs=[grad_block] * 2
            + [
                pl.BlockSpec((1, 1, tile), lambda j, *_: (j, 0, 0)),
                pl.BlockSpec((1, rows, tile), lambda j, *_: (first // 2, 0, j)),
                pl.BlockSpec((1, rows, tile), lambda j, *_: (first // 2, 0, j)),
                pl.BlockSpec((1, width, tile), lambda j, *_: (first // 2, 0, j)),
                pl.BlockSpec((1, tile, width), lambda j, *_: (first // 2, j, 0)),
            ],
            scratch_shapes=[pltpu.VMEM((1, tile), WIDE)],
        ),
        out_shape=[grad] * 2
        + [
            jax.ShapeDtypeStruct((2, 1, tile), WIDE),
            jax.ShapeDtypeStruct((4, rows, 2 * tile), LOW),
            jax.ShapeDtypeStruct((4, rows, 2 * tile), LOW),
            jax.ShapeDtypeStruct((4, width, 2 * tile), LOW),
            jax.ShapeDtypeStruct((4, 2 * tile, width), LOW),
        ],
        input_output_aliases={3 + len(operands) + i: 3 + i for i in range(len(buffers))},
        name="mlp",
        compiler_params=pltpu.CompilerParams(vmem_limit_bytes=36 * 1024 * 1024),
    )(spots, hidden, cot, *[array for array, _ in operands], *buffers)


def norm_back(values, gain, grad):
    center = values - jnp.mean(values, -1, keepdims=True)
    scale = lax.rsqrt(jnp.mean(center * center, -1, keepdims=True) + EPS)
    unit = center * scale
    inner = grad * gain
    pulled = scale * (
        inner
        - jnp.mean(inner, -1, keepdims=True)
        - unit * jnp.mean(inner * unit, -1, keepdims=True)
    )
    return pulled, jnp.sum(grad * unit, 0, keepdims=True), jnp.sum(grad, 0, keepdims=True)


def mlp_back_kernel(pre_ref, up_ref, middle_hbm, cot_hbm, gain_ref, grad_ref, low_ref, sums_ref, *refs):
    sum_buf, middle_buf, cot_buf, sems = refs
    step = pl.program_id(0)
    copies = [
        pltpu.make_async_copy(middle_hbm, middle_buf, sems.at[0]),
        pltpu.make_async_copy(cot_hbm, cot_buf, sems.at[1]),
    ]
    part = dot(pre_ref[0], up_ref[0], 1, 1)

    @pl.when(step == 0)
    def _():
        for copy in copies:
            copy.start()
        sum_buf[...] = part

    @pl.when(step > 0)
    def _():
        sum_buf[...] += part

    @pl.when(step == pl.num_programs(0) - 1)
    def _():
        for copy in copies:
            copy.wait()
        sums_ref[...] = jnp.zeros_like(sums_ref)
        chunk = 224

        def one(i, carry):
            at = pl.ds(pl.multiple_of(i * chunk, chunk), chunk)
            cot = cot_buf[at, :].astype(WIDE)
            pulled, gain_grad, shift_grad = norm_back(
                middle_buf[at, :], gain_ref[...].astype(WIDE), sum_buf[at, :]
            )
            grad = cot + pulled
            low = grad.astype(LOW)
            grad_ref[at, :] = grad
            low_ref[at, :] = low
            sums_ref[0:1, :] += gain_grad
            sums_ref[1:2, :] += shift_grad
            sums_ref[2:3, :] += jnp.sum(low.astype(WIDE), 0, keepdims=True)
            sums_ref[3:4, :] += jnp.sum(cot, 0, keepdims=True)
            return carry

        lax.fori_loop(0, grad_ref.shape[0] // chunk, one, 0)


def mlp_back(pre_grads, ups, middle, cot, gain):
    tiles, rows, tile = pre_grads.shape
    width = cot.shape[1]
    return pl.pallas_call(
        mlp_back_kernel,
        grid=(tiles,),
        in_specs=[
            pl.BlockSpec((1, rows, tile), lambda j: (j, 0, 0)),
            pl.BlockSpec((1, width, tile), lambda j: (j, 0, 0)),
            ANYWHERE,
            ANYWHERE,
            resident((1, width)),
        ],
        out_specs=[resident((rows, width)), resident((rows, width)), resident((8, width))],
        out_shape=[
            jax.ShapeDtypeStruct((rows, width), WIDE),
            jax.ShapeDtypeStruct((rows, width), LOW),
            jax.ShapeDtypeStruct((8, width), WIDE),
        ],
        scratch_shapes=[
            pltpu.VMEM((rows, width), WIDE),
            pltpu.VMEM((rows, width), WIDE),
            pltpu.VMEM((rows, width), LOW),
            pltpu.SemaphoreType.DMA((2,)),
        ],
        name="mlp_back",
        compiler_params=pltpu.CompilerParams(vmem_limit_bytes=44 * 1024 * 1024),
    )(pre_grads, ups, middle, cot, gain)


def mlp_out_kernel(half, act_ref, down_ref, middle_hbm, bias_ref, *refs):
    out_ref, sum_buf, middle_buf, sem = refs[-4:]
    step = pl.program_id(0)
    rows = out_ref.shape[0]
    copy = pltpu.make_async_copy(middle_hbm.at[pl.ds(half * rows, rows), :], middle_buf, sem)
    part = dot(act_ref[0], down_ref[0], 1, 0)

    @pl.when(step == 0)
    def _():
        copy.start()
        sum_buf[...] = part

    @pl.when(step > 0)
    def _():
        sum_buf[...] += part

    @pl.when(step == pl.num_programs(0) - 1)
    def _():
        copy.wait()
        out_ref[...] = (sum_buf[...] + middle_buf[...] + bias_ref[...].astype(WIDE)).astype(LOW)


def mlp_out(half, acts, downs, middle, bias, buffers):
    tiles, rows, tile = acts.shape
    width = middle.shape[1]
    count = rows // 2
    return pl.pallas_call(
        functools.partial(mlp_out_kernel, half),
        grid=(tiles,),
        in_specs=[
            pl.BlockSpec((1, count, tile), lambda j: (j, half, 0)),
            pl.BlockSpec((1, tile, width), lambda j: (j, 0, 0)),
            ANYWHERE,
            resident((1, width)),
        ]
        + [ANYWHERE] * len(buffers),
        out_specs=pl.BlockSpec((count, width), lambda j: (half, 0)),
        out_shape=jax.ShapeDtypeStruct((rows, width), LOW),
        scratch_shapes=[
            pltpu.VMEM((count, width), WIDE),
            pltpu.VMEM((count, width), WIDE),
            pltpu.SemaphoreType.DMA(()),
        ],
        input_output_aliases={4: 0} if buffers else {},
        name="mlp_out",
        compiler_params=pltpu.CompilerParams(vmem_limit_bytes=56 * 1024 * 1024),
    )(acts, downs, middle, bias, *buffers)


def pack_kernel(spot_ref, *refs):
    out_refs = refs[-2:]
    shared_one, shared_two = refs[8:10]
    for side in range(2):
        near, far, first, second = refs[4 * side : 4 * side + 4]
        out = out_refs[side]
        for r in range(4):
            at = spot_ref[r]
            source = near if r < 2 else far
            lanes = (r % 2) * LANES
            out[pl.ds(at, 1), :] = source[:, lanes : lanes + LANES]
            out[pl.ds(4 + at, 1), :] = source[:, 512 + lanes : 512 + lanes + LANES]
            for j in range(4):
                sums = first if j < 2 else second
                out[pl.ds(8 + at * 4 + j, 1), :] = sums[j % 2, :, r * LANES : (r + 1) * LANES]
        rows = [(shared_one, 0), (shared_one, 1), (shared_two, 2), (shared_two, 0), (shared_two, 1), (shared_two, 3)]
        for k, (source, row) in enumerate(rows):
            for i in range(8):
                at = 24 + 8 * k + i
                out[at : at + 1, :] = source[row : row + 1, i * LANES : (i + 1) * LANES]


def pack(spots, own, other, sums_one, sums_two):
    return pl.pallas_call(
        pack_kernel,
        grid_spec=pltpu.PrefetchScalarGridSpec(
            num_scalar_prefetch=1,
            grid=(1,),
            in_specs=[resident(item.shape) for item in (*own, *other, sums_one, sums_two)],
            out_specs=[resident((72, LANES))] * 2,
        ),
        out_shape=[jax.ShapeDtypeStruct((72, LANES), WIDE)] * 2,
        name="pack",
        compiler_params=pltpu.CompilerParams(vmem_limit_bytes=8 * 1024 * 1024),
    )(spots, *own, *other, sums_one, sums_two)


def input_kernel(zero_ref, one_ref, two_ref, three_ref, weight_ref, rows_ref, above_ref, gain_ref, out_ref, sums_ref):
    pulled_sum = dot(zero_ref[0], weight_ref[0], 1, 1)
    for i, grad_ref in enumerate((one_ref, two_ref, three_ref)):
        pulled_sum = pulled_sum + dot(grad_ref[0], weight_ref[i + 1], 1, 1)
    pulled, gain_grad, shift_grad = norm_back(
        rows_ref[0].astype(WIDE), gain_ref[...].astype(WIDE), pulled_sum
    )
    out_ref[0] = (above_ref[0] + pulled).astype(LOW)

    @pl.when(pl.program_id(0) == 0)
    def _():
        sums_ref[...] = jnp.zeros_like(sums_ref)

    sums_ref[0:1, :] += gain_grad
    sums_ref[1:2, :] += shift_grad


def input_step(grads, weights, rows, above, gain):
    pairs, seq, width = rows.shape
    block = lambda: pl.BlockSpec((1, seq, width), lambda p: (p, 0, 0))
    return pl.pallas_call(
        input_kernel,
        grid=(pairs,),
        in_specs=[
            pl.BlockSpec((1, seq, 768), lambda p: (p, 0, 0)),
            pl.BlockSpec((1, seq, 768), lambda p: (p, 0, 0)),
            pl.BlockSpec((1, seq, 768), lambda p: (p, 0, 0)),
            pl.BlockSpec((1, seq, 768), lambda p: (p, 0, 0)),
            resident(weights.shape),
            block(),
            block(),
            resident((1, width)),
        ],
        out_specs=[block(), resident((8, width))],
        out_shape=[
            jax.ShapeDtypeStruct(rows.shape, LOW),
            jax.ShapeDtypeStruct((8, width), WIDE),
        ],
        name="input_grad",
        compiler_params=pltpu.CompilerParams(vmem_limit_bytes=28 * 1024 * 1024),
    )(*grads, weights, rows, above, gain)


def place_kernel(turned, spot_ref, near_ref, far_ref, *refs):
    outs = refs[-len(turned) :]
    core = pl.program_id(1) ^ spot_ref[0]
    for i, turn in enumerate(turned):
        parts = []
        for z in range(4):
            at = z ^ spot_ref[2]
            parts.append(
                jnp.where(core == 0, near_ref[at, i], far_ref[at, i])
            )
        block = jnp.concatenate(parts, 0)
        outs[i][...] = (block.T if turn else block).astype(WIDE)


def place(turned, chunk, chunks, spots, near, far, shapes, buffers):
    _, kinds, rows, width = near.shape
    source = lambda: pl.BlockSpec(
        (4, kinds, rows, width), lambda x, c, spot: (x ^ spot[1], 0, 0, 0)
    )
    specs = [
        pl.BlockSpec((width, LANES), lambda x, c, spot: (0, (c * 2 + x) * chunks + chunk))
        if turn
        else pl.BlockSpec((LANES, width), lambda x, c, spot: ((c * 2 + x) * chunks + chunk, 0))
        for turn in turned
    ]
    return pl.pallas_call(
        functools.partial(place_kernel, turned),
        grid_spec=pltpu.PrefetchScalarGridSpec(
            num_scalar_prefetch=1,
            grid=(2, 2),
            in_specs=[source(), source()] + [ANYWHERE] * len(buffers),
            out_specs=specs,
        ),
        out_shape=[jax.ShapeDtypeStruct(shape, WIDE) for shape in shapes],
        input_output_aliases={3 + i: i for i in range(len(buffers))},
        name="place",
        compiler_params=pltpu.CompilerParams(vmem_limit_bytes=20 * 1024 * 1024),
    )(spots, near, far, *buffers)


def gathered_kernel(source_ref, *refs):
    up_ref, down_ref = refs[-2:]
    rows = [[source_ref[high, low, 0, 0] for high in range(2)] for low in range(2)]
    for kind, out_ref in enumerate((up_ref, down_ref)):
        parts = []
        for sub in range(2):
            for low in range(2):
                for high in range(2):
                    parts.append(rows[low][high][2 * sub + kind])
        block = jnp.concatenate(parts, 0)
        out_ref[...] = (block.T if kind == 0 else block).astype(WIDE)


def gathered(chunk, chunks, source, shapes, buffers):
    kinds, rows, width = source.shape[1:]
    source = source.reshape((2, 2, 2, 2, kinds, rows, width))
    span = 2 * LANES
    return pl.pallas_call(
        gathered_kernel,
        grid=(2, 2),
        in_specs=[
            pl.BlockSpec((2, 2, 1, 1, kinds, rows, width), lambda c, x: (0, 0, x, c, 0, 0, 0))
        ]
        + [ANYWHERE] * len(buffers),
        out_specs=[
            pl.BlockSpec((width, span), lambda c, x: (0, (c * 2 + x) * chunks + chunk)),
            pl.BlockSpec((span, width), lambda c, x: ((c * 2 + x) * chunks + chunk, 0)),
        ],
        out_shape=[jax.ShapeDtypeStruct(shape, WIDE) for shape in shapes],
        input_output_aliases={1 + i: i for i in range(len(buffers))},
        name="gathered",
        compiler_params=pltpu.CompilerParams(vmem_limit_bytes=24 * 1024 * 1024),
    )(source, *buffers)


def paired_body(
    layer_in,
    patch_count,
    attn_gain,
    attn_shift,
    query_weight,
    query_bias,
    key_weight,
    value_weight,
    value_bias,
    out_weight,
    out_bias,
    mlp_gain,
    mlp_shift,
    up_weight,
    up_bias,
    down_weight,
    down_bias,
    layer_cot,
):
    groups = lax.axis_size("dp")
    rank = lax.axis_index("dp")
    half_id = lax.axis_index("mp")
    core_id, x_id, zlow_id, zhigh_id = rank & 1, (rank >> 1) & 1, (rank >> 2) & 1, (rank >> 3) & 1
    part = core_id * 2 + x_id
    spots = jnp.stack([part, part ^ 1, part ^ 2, part ^ 3]).astype(jnp.int32)
    sides = jnp.stack([x_id, x_id ^ 1, x_id, x_id ^ 1]).astype(jnp.int32)
    place_spots = jnp.stack([core_id, x_id, zlow_id * 2 + zhigh_id]).astype(jnp.int32)

    swap = lambda value, bit: flip(value, "dp", bit, groups)
    across = lambda value: flip(value, "mp", 1, 2)

    rows, width = layer_in.shape
    heads_width = query_weight.shape[1]
    hidden_width = up_weight.shape[1]
    block = hidden_width // 4
    pairs = rows // SEQ
    counts = pick(patch_count, half_id, pairs, 0)
    row_vec = lambda vec: vec.reshape(1, -1)

    gate = lambda value, *waits: after(value, *waits) if waits else value
    shape_three = (pairs, SEQ, width)
    subs = block // LANES

    slice_rows = LANES // 2
    slice_at = (rank // 4) * 2 * subs + rank % 4
    slices = jnp.stack(
        [
            jnp.stack(
                [
                    pick(up_weight, slice_at + 4 * i, slice_rows, 1).T,
                    pick(down_weight, slice_at + 4 * i, slice_rows, 0),
                ]
            )
            for i in range(2)
        ]
    )
    slices = across(slices)
    sent_qk = jnp.stack([pick(w, core_id, heads_width // 2, 1) for w in (query_weight, key_weight)])
    value_near = across(pick(value_weight, part, LANES, 1))
    sent_bias = row_vec(jnp.concatenate([query_bias, value_bias, up_bias]))
    raw_out = pick(out_weight, core_id, heads_width // 2, 0)
    rows_in = layer_in.astype(WIDE)
    normed = layer_norm(
        rows_in, attn_gain.astype(WIDE), attn_shift.astype(WIDE)
    ).astype(LOW)
    normed_three = normed.reshape(shape_three)

    def own_inputs():
        weights = [
            (w, pl.BlockSpec((width, LANES), lambda g, p, spot, count, i=i: (0, spot[2 * g + i])))
            for w in (query_weight, key_weight, value_weight)
            for i in range(2)
        ]
        biases = [
            (row_vec(b), pl.BlockSpec((1, LANES), lambda g, p, spot, count, i=i: (0, spot[2 * g + i])))
            for b in (query_bias, value_bias)
            for i in range(2)
        ]
        return weights, biases

    def other_inputs(group, qk, values):
        weights = [
            (qk, pl.BlockSpec((None, width, LANES), lambda g, p, side, count, k=k, i=i: (k, 0, side[i])))
            for k in range(2)
            for i in range(2)
        ]
        weights += [(item, pl.BlockSpec((width, LANES), lambda g, p, *_: (0, 0))) for item in values]
        biases = [
            (bias_other, pl.BlockSpec((1, LANES), lambda g, p, side, count, k=k, i=i: (0, 4 * k + side[4 + 2 * group + i])))
            for k in range(2)
            for i in range(2)
        ]
        return weights, biases

    other_spots = jnp.concatenate([sides, spots])
    slices, value_near, sent_qk, raw_out, sent_bias, normed, spots, other_spots, counts = lax.optimization_barrier(
        (slices, value_near, sent_qk, raw_out, sent_bias, normed, spots, other_spots, counts)
    )
    normed_three = normed.reshape(shape_three)
    near_qk = across(sent_qk)
    bias_other = across(sent_bias)
    value_side = swap(value_near, XBIT)
    gathered_weights = [lax.all_gather(slices[0], "dp"), lax.all_gather(slices[1], "dp")]
    kept = attend(
        0, 2, spots, counts, normed_three, *own_inputs(), []
    )
    near_qk, bias_other, value_side, _ = lax.optimization_barrier((near_qk, bias_other, value_side, kept[1]))
    sent_out = after(raw_out, near_qk)
    near_out = across(sent_out)
    far_qk, far_values = swap(near_qk, CORE), [swap(value_near, CORE), swap(value_side, CORE)]
    kept = attend(
        2, 1, gate(other_spots, sent_out), counts, normed_three, *other_inputs(0, near_qk, (value_near, value_side)), kept
    )
    near_out, far_qk, far_values, _ = lax.optimization_barrier((near_out, far_qk, far_values, kept[1]))
    far_out = swap(near_out, CORE)
    kept = attend(
        3, 1, gate(other_spots, near_out), counts, normed_three, *other_inputs(1, far_qk, far_values), kept
    )
    middle, hidden, outs_all = middle_step(
        jnp.concatenate([spots, sides]),
        layer_in.reshape(shape_three),
        kept[1],
        out_weight,
        near_out,
        far_out,
        row_vec(out_bias),
        row_vec(mlp_gain),
        row_vec(mlp_shift),
    )
    middle = middle.reshape(rows, width)
    hidden = hidden.reshape(rows, width)

    def own_mlp(first):
        ups = [
            (up_weight, pl.BlockSpec((width, LANES), lambda j, spot, r=r: (0, spot[r] * subs + first + j)))
            for r in range(4)
        ]
        downs = [
            (down_weight, pl.BlockSpec((LANES, width), lambda j, spot, r=r: (spot[r] * subs + first + j, 0)))
            for r in range(4)
        ]
        biases = [
            (row_vec(up_bias), pl.BlockSpec((1, LANES), lambda j, spot, r=r: (0, spot[r] * subs + first + j)))
            for r in range(4)
        ]
        return ups, downs, biases

    def other_mlp(first):
        source = gathered_weights[first // 2]
        ups, downs = (
            [
                (source, pl.BlockSpec((2, 1, slice_rows, width), lambda j, spot, r=r, k=k: (spot[r] * 2 + j, k, 0, 0)))
                for r in range(4)
            ]
            for k in range(2)
        )
        biases = [
            (bias_other, pl.BlockSpec((1, LANES), lambda j, spot, r=r: (0, 8 + spot[r] * subs + first + j)))
            for r in range(4)
        ]
        return ups, downs, biases

    def cut(item, index):
        count, lanes, cols = item.shape
        return pick(item.reshape(count, 2, lanes // 2, cols), index, 1, 1)[:, 0]

    def outbound(near, far, first, last):
        return total(near[:, first:last], far[:, first:last])

    def sideways(near, far, beyond, first, last):
        return total(near[1, first:last], far[1, first:last], beyond[1])

    def collected(near, far, beyond, side, first, last):
        return total(near[0, first:last], far[0, first:last], beyond[0], side)

    def halves(item):
        return cut(item, zlow_id ^ 1), cut(item, zlow_id)

    def quarters(item):
        return cut(item, zhigh_id ^ 1), cut(item, zhigh_id)

    back = lambda slot, *wait: attend_back(
        slot, gate(counts, *wait), normed, attn_grad, kept, outs_all
    )

    together = lambda *items: lax.optimization_barrier(items)
    other_a = mlp(2, True, spots, hidden, layer_cot, *other_mlp(0), [])
    far_other_a = swap(other_a[1], CORE)
    own_a = mlp(0, False, spots, hidden, layer_cot, *own_mlp(0), other_a[3:])
    far_other_a, far, _ = together(far_other_a, own_a[1], own_a[2])
    far_own_a = swap(far, CORE)
    out_a = [outbound(other_a[0], far_other_a, *span) for span in ((0, 1), (1, 2), (2, 4))]
    own_b = mlp(6, False, gate(spots, *out_a), hidden, layer_cot, *own_mlp(2), own_a[3:])
    beyond_a0, far_own_a, far, _ = together(across(out_a[0]), far_own_a, own_b[1], own_b[2])
    far_own_b = swap(far, CORE)
    other_b = mlp(
        4, True, gate(spots, beyond_a0, far_own_a), hidden, layer_cot, *other_mlp(2), own_b[3:]
    )
    acts, pre_grads, ups_all, downs_all = other_b[3:]
    beyond_a1, far_own_b, far, _ = together(
        across(after(out_a[1], beyond_a0)), far_own_b, other_b[1], other_b[2]
    )
    far_other_b = swap(far, CORE)
    beyond_a01 = jnp.concatenate([beyond_a0, beyond_a1], 1)
    side_a01 = sideways(own_a[0], far_own_a, beyond_a01, 0, 2)
    middle_grad, attn_grad, sums_two = mlp_back(
        pre_grads, ups_all, middle, layer_cot, gate(row_vec(mlp_gain), side_a01, beyond_a01, far_own_b)
    )
    beyond_a23, arrived_a01, far_other_b, _ = together(
        across(after(out_a[2], beyond_a1)), swap(side_a01, XBIT), far_other_b, sums_two
    )
    side_a23 = sideways(own_a[0], far_own_a, beyond_a23, 2, 4)
    out_b = [outbound(other_b[0], far_other_b, *span) for span in ((0, 2), (2, 4))]
    other_far, bias_other_far, grads_three = back(3, side_a23, arrived_a01, *out_b)
    beyond_b01, arrived_a23, far, _ = together(
        across(out_b[0]), swap(side_a23, XBIT), other_far, bias_other_far
    )
    late_other_far = swap(far, CORE)
    sum_a = jnp.concatenate(
        [
            collected(own_a[0], far_own_a, beyond_a01, arrived_a01, 0, 2),
            collected(own_a[0], far_own_a, beyond_a23, arrived_a23, 2, 4),
        ]
    )
    low_a, keep_a = halves(sum_a)
    side_b01 = sideways(own_b[0], far_own_b, beyond_b01, 0, 2)
    other_near, bias_other_near, grads_two = back(2, low_a, sum_a, side_b01, grads_three)
    beyond_b23, arrived_b01, low_a, late_other_far, _ = together(
        across(after(out_b[1], beyond_b01)), swap(side_b01, XBIT), swap(low_a, ZLOW), late_other_far, bias_other_near
    )
    high_a, keep_a = quarters(total(keep_a, low_a))
    side_b23 = sideways(own_b[0], far_own_b, beyond_b23, 2, 4)
    late_out = [outbound(other_near, late_other_far, *span) for span in ((0, 2), (2, 4))]
    own_far, bias_own_far, grads_one = back(1, high_a, side_b23, arrived_b01, *late_out, grads_two)
    late_beyond0, arrived_b23, high_a, far, _ = together(
        across(late_out[0]), swap(side_b23, XBIT), swap(high_a, ZHIGH), own_far, bias_own_far
    )
    late_own_far = swap(far, CORE)
    one_a = total(keep_a, high_a)
    sum_b = jnp.concatenate(
        [
            collected(own_b[0], far_own_b, beyond_b01, arrived_b01, 0, 2),
            collected(own_b[0], far_own_b, beyond_b23, arrived_b23, 2, 4),
        ]
    )
    low_b, keep_b = halves(sum_b)
    gathered_a = lax.all_gather(one_a, "dp")
    own_near, bias_own_near, grads_zero = back(0, one_a, low_b, sum_b, late_beyond0, grads_one)
    late_beyond1, late_own_far, low_b, _ = together(
        across(after(late_out[1], late_beyond0)), late_own_far, swap(low_b, ZLOW), bias_own_near
    )
    high_b, keep_b = quarters(total(keep_b, low_b))
    late_side0 = sideways(own_near, late_own_far, late_beyond0, 0, 2)
    late_side1 = sideways(own_near, late_own_far, late_beyond1, 2, 4)
    grad_in, sums_one = input_step(
        (grads_zero, grads_one, grads_two, grads_three),
        kept[2],
        layer_in.reshape(shape_three),
        middle_grad.reshape(shape_three),
        gate(row_vec(attn_gain), high_b, late_side0, late_side1),
    )
    high_b, late_arrived0, sums_one = together(swap(high_b, ZHIGH), swap(late_side0, XBIT), sums_one)
    one_b = total(keep_b, high_b)
    gathered_b = lax.all_gather(one_b, "dp")
    quarter_id = zlow_id * 2 + zhigh_id
    z_bits = [None, ZHIGH, ZLOW, ZLOW | ZHIGH]

    def four(item):
        count, lanes, cols = item.shape
        item = item.reshape(count, 4, lanes // 4, cols)
        return [pick(item, quarter_id ^ r, 1, 1)[:, 0] for r in range(4)]

    def send_four(items):
        return [swap(items[r], z_bits[r]) for r in range(1, 4)]

    late_four0 = four(collected(own_near, late_own_far, late_beyond0, late_arrived0, 0, 2))
    own_vec, other_vec = pack(
        spots,
        (bias_own_near, bias_own_far, own_a[2], own_b[2]),
        (bias_other_near, bias_other_far, other_a[2], other_b[2]),
        sums_one,
        sums_two,
    )
    layer_out = mlp_out(
        0, acts, downs_all, middle, gate(row_vec(down_bias), one_b, other_vec, *late_four0), []
    )
    late_arrived1, late_got0, vec_got, mark = together(
        swap(after(late_side1, late_arrived0), XBIT), send_four(late_four0), across(other_vec), layer_out
    )
    late_one0 = total(late_four0[0], *late_got0)
    late_four1 = four(collected(own_near, late_own_far, late_beyond1, late_arrived1, 2, 4))
    vec = own_vec + vec_got
    layer_out = mlp_out(
        1, acts, downs_all, middle, gate(row_vec(down_bias), late_one0, vec, *late_four1), [mark]
    )
    late_got1, late_have0, vec_got, layer_out = together(
        send_four(late_four1), send_four([late_one0] * 4), swap(vec, CORE), layer_out
    )
    late_one1 = total(late_four1[0], *late_got1)
    late_have0 = jnp.stack([late_one0, *late_have0])
    vec = vec + vec_got
    up_shape, down_shape = up_weight.shape, down_weight.shape
    placed = gathered(
        0, 2, gate(gathered_a, late_one1, late_have0, vec), (up_shape, down_shape), []
    )
    late_have1, late_side0, vec_got, *placed = together(
        send_four([late_one1] * 4), swap(late_have0, XBIT), swap(vec, XBIT), *placed
    )
    late_have1 = jnp.stack([late_one1, *late_have1])
    late_have0 = jnp.concatenate([late_have0, late_side0])
    vec = vec + vec_got
    placed = gathered(
        1, 2, gate(gathered_b, late_have1, late_have0, vec), (up_shape, down_shape), placed
    )
    late_side1, late_far0, vec_got, grad_up_weight, grad_down_weight = together(
        swap(late_have1, XBIT), swap(late_have0, CORE), send_four([vec] * 4), *placed
    )
    late_have1 = jnp.concatenate([late_have1, late_side1])
    vec = ((vec + vec_got[0]) + (vec_got[1] + vec_got[2])).reshape(-1)
    grad_query_weight, grad_key_weight = place(
        (True, True), 0, 1, gate(place_spots, late_have1), late_have0, late_far0, (query_weight.shape,) * 2, []
    )
    late_far1, grad_query_weight, grad_key_weight = together(
        swap(late_have1, CORE), grad_query_weight, grad_key_weight
    )
    grad_value_weight, grad_out_weight = place(
        (True, False), 0, 1, place_spots, late_have1, late_far1, (value_weight.shape, out_weight.shape), []
    )
    grad_query_bias = vec[:heads_width]
    grad_value_bias = vec[heads_width : 2 * heads_width]
    grad_up_bias = vec[2 * heads_width : 2 * heads_width + hidden_width]
    (
        grad_attn_gain,
        grad_attn_shift,
        grad_out_bias,
        grad_mlp_gain,
        grad_mlp_shift,
        grad_down_bias,
    ) = jnp.split(vec[2 * heads_width + hidden_width :], 6)
    return (
        layer_out,
        grad_in.reshape(rows, width),
        grad_attn_gain,
        grad_attn_shift,
        grad_query_weight,
        grad_query_bias,
        grad_key_weight,
        grad_value_weight,
        grad_value_bias,
        grad_out_weight,
        grad_out_bias,
        grad_mlp_gain,
        grad_mlp_shift,
        grad_up_weight,
        grad_up_bias,
        grad_down_weight,
        grad_down_bias,
    )


def solution(mesh):
    paired = mesh.shape["mp"] == 2 and mesh.shape["dp"] == 16
    body = paired_body if paired else general_body
    placed = (
        P(("dp", "mp"), None),
        P("dp"),
        P(),
        P(),
        P(None, "mp"),
        P("mp"),
        P(None, "mp"),
        P(None, "mp"),
        P("mp"),
        P("mp", None),
        P(),
        P(),
        P(),
        P(None, "mp"),
        P("mp"),
        P("mp", None),
        P(),
        P(("dp", "mp"), None),
    )
    return jax.shard_map(
        body,
        mesh=mesh,
        in_specs=placed,
        out_specs=(
            P(("dp", "mp"), None),
            P(("dp", "mp"), None),
            P(),
            P(),
            P(None, "mp"),
            P("mp"),
            P(None, "mp"),
            P(None, "mp"),
            P("mp"),
            P("mp", None),
            P(),
            P(),
            P(),
            P(None, "mp"),
            P("mp"),
            P("mp", None),
            P(),
        ),
        check_vma=False,
    )
```

```python
import functools

import jax
import jax.numpy as jnp
from jax import lax
from jax.experimental import pallas as pl
from jax.experimental.pallas import tpu as pltpu
from jax.sharding import PartitionSpec as P

HEAD_DIM = 64
TEXT = 40
SEQ = 280


EPS = 1e-05
SCALE = 0.125
NEGATIVE = -1e30


def layer_norm(values, gain, shift):
    center = values - jnp.mean(values, -1, keepdims=True)
    spread = jnp.mean(center * center, -1, keepdims=True)
    return center * lax.rsqrt(spread + EPS) * gain + shift


def exact_gelu(values):
    return jax.nn.gelu(values, approximate=False)


def matmul_rows(left, right):
    return jnp.dot(left, right, preferred_element_type=jnp.float32)


def contract_rows(left, right):
    return lax.dot_general(
        left, right, (((0,), (0,)), ((), ())), preferred_element_type=jnp.float32
    )


def contract_cols(left, right):
    return lax.dot_general(
        left, right, (((1,), (1,)), ((), ())), preferred_element_type=jnp.float32
    )


def column_sum(values):
    return jnp.sum(values.astype(jnp.float32), 0)


def general_body(
    layer_in,
    patch_count,
    attn_gain,
    attn_shift,
    query_weight,
    query_bias,
    key_weight,
    value_weight,
    value_bias,
    out_weight,
    out_bias,
    mlp_gain,
    mlp_shift,
    up_weight,
    up_bias,
    down_weight,
    down_bias,
    layer_cot,
):
    lowtype = jnp.bfloat16
    wide = jnp.float32
    rows_in = layer_in.astype(wide)
    gain_one = attn_gain.astype(wide)
    shift_one = attn_shift.astype(wide)
    gain_two = mlp_gain.astype(wide)
    shift_two = mlp_shift.astype(wide)
    normed_tok, norm_pull = jax.vjp(layer_norm, rows_in, gain_one, shift_one)
    group_rows = lax.all_gather(normed_tok.astype(lowtype), "mp", axis=0, tiled=True)
    query_rows = (matmul_rows(group_rows, query_weight) + query_bias.astype(wide)).astype(lowtype)
    key_rows = matmul_rows(group_rows, key_weight).astype(lowtype)
    value_rows = (matmul_rows(group_rows, value_weight) + value_bias.astype(wide)).astype(lowtype)
    pairs = patch_count.shape[0]
    local_width = query_weight.shape[1]
    local_heads = local_width // HEAD_DIM
    group_total = group_rows.shape[0]
    shape_four = (pairs, SEQ, local_heads, HEAD_DIM)
    query_blk = query_rows.reshape(shape_four)
    key_blk = key_rows.reshape(shape_four)
    value_blk = value_rows.reshape(shape_four)
    scores = jnp.einsum("pqhd,pkhd->phqk", query_blk, key_blk, preferred_element_type=wide) * SCALE
    valid = jnp.arange(SEQ)[None, :] < (TEXT + patch_count)[:, None]
    scores = jnp.where(valid[:, None, None, :], scores, NEGATIVE)
    probs = jax.nn.softmax(scores, axis=-1)
    probs_low = probs.astype(lowtype)
    context = jnp.einsum("phqk,pkhd->pqhd", probs_low, value_blk, preferred_element_type=wide)
    context = context.astype(lowtype).reshape(group_total, local_width)
    context_tok = lax.all_to_all(context, "mp", split_axis=0, concat_axis=1, tiled=True)
    out_full = lax.all_gather(out_weight, "mp", axis=0, tiled=True)
    attended = matmul_rows(context_tok, out_full) + out_bias.astype(wide)
    middle = rows_in + attended
    hidden_wide, mlp_pull = jax.vjp(layer_norm, middle, gain_two, shift_two)
    hidden_in = hidden_wide.astype(lowtype)
    cot_wide = layer_cot.astype(wide)
    up_full, bias_full, down_full = (
        lax.all_gather(up_weight, "mp", axis=1, tiled=True),
        lax.all_gather(up_bias, "mp", axis=0, tiled=True),
        lax.all_gather(down_weight, "mp", axis=0, tiled=True),
    )
    pre_act = matmul_rows(hidden_in, up_full) + bias_full.astype(wide)
    act_wide, gelu_pull = jax.vjp(exact_gelu, pre_act)
    act_low = act_wide.astype(lowtype)
    ffn_out = matmul_rows(act_low, down_full) + down_bias.astype(wide)
    whole_down = contract_rows(act_low, layer_cot)
    act_grad = contract_cols(layer_cot, down_full)
    pre_grad = gelu_pull(act_grad)[0].astype(lowtype)
    whole_up_bias = column_sum(pre_grad)
    whole_up = contract_rows(hidden_in, pre_grad)
    hidden_grad = contract_cols(pre_grad, up_full)
    grad_up_weight, grad_up_bias, grad_down_weight = (
        lax.psum_scatter(
            whole_up.astype(jnp.bfloat16), "mp", scatter_dimension=1, tiled=True
        ).astype(jnp.float32),
        lax.psum_scatter(
            whole_up_bias.astype(jnp.bfloat16), "mp", scatter_dimension=0, tiled=True
        ).astype(jnp.float32),
        lax.psum_scatter(
            whole_down.astype(jnp.bfloat16), "mp", scatter_dimension=0, tiled=True
        ).astype(jnp.float32),
    )
    layer_out = (middle + ffn_out).astype(lowtype)
    grad_down_bias = column_sum(layer_cot)
    middle_part, grad_gain_two, grad_shift_two = mlp_pull(hidden_grad)
    middle_grad = cot_wide + middle_part
    attn_grad = middle_grad.astype(lowtype)
    grad_out_bias = column_sum(attn_grad)
    grad_out_weight = lax.psum_scatter(
        contract_rows(context_tok, attn_grad).astype(jnp.bfloat16),
        "mp",
        scatter_dimension=0,
        tiled=True,
    ).astype(jnp.float32)
    context_grad_tok = contract_cols(attn_grad, out_full).astype(lowtype)
    context_grad = lax.all_to_all(
        context_grad_tok, "mp", split_axis=1, concat_axis=0, tiled=True
    ).reshape(shape_four)
    probs_grad = jnp.einsum("pqhd,pkhd->phqk", context_grad, value_blk, preferred_element_type=wide)
    value_grad = jnp.einsum("phqk,pqhd->pkhd", probs_low, context_grad, preferred_element_type=wide)
    value_grad = value_grad.astype(lowtype).reshape(group_total, local_width)
    score_grad = (probs * (probs_grad - jnp.sum(probs * probs_grad, -1, keepdims=True))).astype(
        lowtype
    )
    query_grad = (
        jnp.einsum("phqk,pkhd->pqhd", score_grad, key_blk, preferred_element_type=wide) * SCALE
    )
    query_grad = query_grad.astype(lowtype).reshape(group_total, local_width)
    key_grad = (
        jnp.einsum("phqk,pqhd->pkhd", score_grad, query_blk, preferred_element_type=wide) * SCALE
    )
    key_grad = key_grad.astype(lowtype).reshape(group_total, local_width)
    grad_query_weight = contract_rows(group_rows, query_grad)
    grad_key_weight = contract_rows(group_rows, key_grad)
    grad_value_weight = contract_rows(group_rows, value_grad)
    grad_query_bias = column_sum(query_grad)
    grad_value_bias = column_sum(value_grad)
    total = contract_cols(query_grad, query_weight)
    total = total + contract_cols(key_grad, key_weight)
    normed_grad = lax.psum_scatter(
        (total + contract_cols(value_grad, value_weight)).astype(jnp.bfloat16),
        "mp",
        scatter_dimension=0,
        tiled=True,
    ).astype(jnp.float32)
    input_part, grad_gain_one, grad_shift_one = norm_pull(normed_grad)
    grad_in = (middle_grad + input_part).astype(lowtype)
    (
        grad_query_weight,
        grad_query_bias,
        grad_key_weight,
        grad_value_weight,
        grad_value_bias,
        grad_out_weight,
        grad_up_weight,
        grad_up_bias,
        grad_down_weight,
    ) = (
        lax.psum(grad_query_weight.astype(jnp.bfloat16), "dp").astype(jnp.float32),
        lax.psum(grad_query_bias.astype(jnp.bfloat16), "dp").astype(jnp.float32),
        lax.psum(grad_key_weight.astype(jnp.bfloat16), "dp").astype(jnp.float32),
        lax.psum(grad_value_weight.astype(jnp.bfloat16), "dp").astype(jnp.float32),
        lax.psum(grad_value_bias.astype(jnp.bfloat16), "dp").astype(jnp.float32),
        lax.psum(grad_out_weight.astype(jnp.bfloat16), "dp").astype(jnp.float32),
        lax.psum(grad_up_weight.astype(jnp.bfloat16), "dp").astype(jnp.float32),
        lax.psum(grad_up_bias.astype(jnp.bfloat16), "dp").astype(jnp.float32),
        lax.psum(grad_down_weight.astype(jnp.bfloat16), "dp").astype(jnp.float32),
    )
    grad_gain_one, grad_shift_one, grad_out_bias, grad_gain_two, grad_shift_two, grad_down_bias = (
        lax.psum(
            (
                grad_gain_one,
                grad_shift_one,
                grad_out_bias,
                grad_gain_two,
                grad_shift_two,
                grad_down_bias,
            ),
            ("dp", "mp"),
        )
    )
    return (
        layer_out,
        grad_in,
        grad_gain_one,
        grad_shift_one,
        grad_query_weight,
        grad_query_bias,
        grad_key_weight,
        grad_value_weight,
        grad_value_bias,
        grad_out_weight,
        grad_out_bias,
        grad_gain_two,
        grad_shift_two,
        grad_up_weight,
        grad_up_bias,
        grad_down_weight,
        grad_down_bias,
    )


WIDE = jnp.float32
LOW = jnp.bfloat16
LANES = 128
ROOT_HALF = 0.7071067811865476
NORMAL = 0.3989422804014327
CORE, XBIT, ZLOW, ZHIGH = 1, 2, 4, 8


def dot(left, right, left_dim, right_dim):
    return lax.dot_general(
        left, right, (((left_dim,), (right_dim,)), ((), ())), preferred_element_type=WIDE
    )


def flip(value, axis, bit, size):
    return lax.ppermute(value, axis, [(i, i ^ bit) for i in range(size)])


def pick(value, index, width, axis):
    return lax.dynamic_slice_in_dim(value, index * width, width, axis)


def after(value, *others):
    return lax.optimization_barrier((value,) + others)[0]


def total(*items):
    result = items[0].astype(WIDE)
    for item in items[1:]:
        result = result + item.astype(WIDE)
    return result.astype(LOW)


def resident(shape):
    return pl.BlockSpec(shape, lambda *_: (0,) * len(shape), pipeline_mode=pl.Buffered(1))


ANYWHERE = pl.BlockSpec(memory_space=pl.ANY)


def attend_kernel(spot_ref, count_ref, rows_ref, *refs):
    weights, biases = refs[:6], refs[6:10]
    qkv_ref, context_ref, weight_ref, bias_ref = refs[-4:]
    pair = pl.program_id(1)

    @pl.when(pair == 0)
    def _():
        for i in range(6):
            weight_ref[0, :, i * LANES : (i + 1) * LANES] = weights[i][...]
        bias_ref[...] = jnp.zeros_like(bias_ref)
        for i in range(2):
            bias_ref[:, i * LANES : (i + 1) * LANES] = biases[i][...].astype(WIDE)
            bias_ref[:, (4 + i) * LANES : (5 + i) * LANES] = biases[2 + i][...].astype(WIDE)

    qkv = (dot(rows_ref[0], weight_ref[0], 1, 0) + bias_ref[...]).astype(LOW)
    qkv_ref[0, 0] = qkv
    length = TEXT + count_ref[pair]
    lane = lax.broadcasted_iota(jnp.int32, (SEQ, LANES), 1)
    padding = lax.broadcasted_iota(jnp.int32, (SEQ, SEQ), 1) >= length
    lane_low = lane < HEAD_DIM
    everything = []
    for tile in range(2):
        query, key, value = (
            qkv[:, i * 256 + tile * LANES : i * 256 + (tile + 1) * LANES] for i in range(3)
        )
        query = query * SCALE
        for side in range(2):
            mine = lane_low if side == 0 else jnp.logical_not(lane_low)
            everything.append((dot(jnp.where(mine, query, jnp.zeros_like(query)), key, 1, 1), value))
    heads = []
    for scores, value in everything:
        scores = jnp.where(padding, NEGATIVE, scores)
        power = jnp.exp(scores - jnp.max(scores, -1, keepdims=True))
        inverse = 1.0 / jnp.sum(power, -1, keepdims=True)
        heads.append(dot(power.astype(LOW), value, 1, 0) * inverse)
    for tile in range(2):
        context_ref[0, 0, :, tile * LANES : (tile + 1) * LANES] = jnp.where(
            lane_low, heads[2 * tile], heads[2 * tile + 1]
        ).astype(LOW)


def attend(slot, groups, spots, counts, rows, weights, biases, buffers):
    pairs, seq, width = rows.shape
    shapes = [
        ((4, pairs, seq, 768), (1, 1, seq, 768), lambda g, p, *_: (slot + g, p, 0, 0)),
        ((4, pairs, seq, 256), (1, 1, seq, 256), lambda g, p, *_: (slot + g, p, 0, 0)),
        ((4, width, 768), (1, width, 768), lambda g, p, *_: (slot + g, 0, 0)),
    ]
    operands = list(weights) + list(biases)
    aliases = {3 + len(operands) + i: i for i in range(len(buffers))}
    return pl.pallas_call(
        attend_kernel,
        grid_spec=pltpu.PrefetchScalarGridSpec(
            num_scalar_prefetch=2,
            grid=(groups, pairs),
            in_specs=[pl.BlockSpec((1, seq, width), lambda g, p, *_: (p, 0, 0))]
            + [spec for _, spec in operands]
            + [ANYWHERE] * len(buffers),
            out_specs=[pl.BlockSpec(block, index) for _, block, index in shapes],
            scratch_shapes=[pltpu.VMEM((1, 768), WIDE)],
        ),
        out_shape=[jax.ShapeDtypeStruct(shape, LOW) for shape, _, _ in shapes],
        input_output_aliases=aliases,
        name="attend",
        compiler_params=pltpu.CompilerParams(vmem_limit_bytes=56 * 1024 * 1024),
    )(spots, counts, rows, *[array for array, _ in operands], *buffers)


def attend_back_kernel(
    count_ref, place_ref, rows_hbm, cots_hbm, cot_ref, qkv_ref, context_ref, upper_ref, lower_ref, *refs
):
    near_ref, bias_ref, qkv_grad_ref, grad_buf, context_buf, rows_buf, cots_buf, out_buf, sems = refs[-9:]
    pair = pl.program_id(0)
    copies = [
        pltpu.make_async_copy(rows_hbm, rows_buf, sems.at[0]),
        pltpu.make_async_copy(cots_hbm, cots_buf, sems.at[1]),
    ]

    @pl.when(pair == 0)
    def _():
        for copy in copies:
            copy.start()
        out_buf[:LANES, :] = upper_ref[...]
        out_buf[LANES:, :] = lower_ref[...]

    at = pl.ds(pl.multiple_of(pair * SEQ, 8), SEQ)
    context_grad = dot(cot_ref[0], out_buf[...], 1, 1).astype(LOW)
    qkv = qkv_ref[0, 0]
    context_buf[at, :] = context_ref[0, 0].astype(WIDE)
    length = TEXT + count_ref[pair]
    lane = lax.broadcasted_iota(jnp.int32, (SEQ, LANES), 1)
    padding = lax.broadcasted_iota(jnp.int32, (SEQ, SEQ), 0) >= length
    grads = [[], [], []]
    lane_low = lane < HEAD_DIM
    work = []
    for tile in range(2):
        query, key, value = (
            qkv[:, i * 256 + tile * LANES : i * 256 + (tile + 1) * LANES] for i in range(3)
        )
        query = query * SCALE
        outer = context_grad[:, tile * LANES : (tile + 1) * LANES]
        for side in range(2):
            mine = lane_low if side == 0 else jnp.logical_not(lane_low)
            scores = dot(jnp.where(mine, key, jnp.zeros_like(key)), query, 1, 1)
            probs_grad = dot(jnp.where(mine, value, jnp.zeros_like(value)), outer, 1, 1)
            work.append((scores, probs_grad, query, key, outer))
    heads = []
    for scores, probs_grad, query, key, outer in work:
        scores = jnp.where(padding, NEGATIVE, scores)
        power = jnp.exp(scores - jnp.max(scores, 0, keepdims=True))
        probs = power * (1.0 / jnp.sum(power, 0, keepdims=True))
        both = probs * probs_grad
        score_grad = (both - probs * jnp.sum(both, 0, keepdims=True)).astype(LOW)
        heads.append(
            (dot(score_grad, key, 0, 0), dot(score_grad, query, 1, 0), dot(probs.astype(LOW), outer, 1, 0))
        )
    for tile in range(2):
        for i, scale in enumerate((SCALE, 1.0, 1.0)):
            pair_of = [heads[2 * tile + side][i] for side in range(2)]
            grads[i].append((jnp.where(lane_low, *pair_of) * scale).astype(LOW))
    joined = jnp.concatenate(grads[0] + grads[1] + grads[2], 1)
    qkv_grad_ref[0] = joined
    grad_buf[at, :] = joined.astype(WIDE)

    @pl.when(pair == pl.num_programs(0) - 1)
    def _():
        for copy in copies:
            copy.wait()
        stacked = dot(grad_buf[...].astype(LOW), rows_buf[...], 0, 0).astype(LOW)
        outs = dot(context_buf[...].astype(LOW), cots_buf[...], 0, 0).astype(LOW)
        for i in range(2):
            near_ref[i, :3] = stacked.reshape(3, 2, LANES, -1)[:, i]
            near_ref[i, 3] = outs[i * LANES : (i + 1) * LANES]
        bias_ref[...] = jnp.sum(grad_buf[...], 0, keepdims=True)


def attend_back(slot, first, counts, places, rows, cot, kept, out):
    qkv, context, _ = kept
    _, pairs, seq, _ = qkv.shape
    width = rows.shape[1]
    return pl.pallas_call(
        attend_back_kernel,
        grid_spec=pltpu.PrefetchScalarGridSpec(
            num_scalar_prefetch=2,
            grid=(pairs,),
            in_specs=[
                ANYWHERE,
                ANYWHERE,
                pl.BlockSpec((1, seq, width), lambda p, *_: (p, 0, 0)),
                pl.BlockSpec((1, 1, seq, 768), lambda p, *_: (slot, p, 0, 0)),
                pl.BlockSpec((1, 1, seq, 256), lambda p, *_: (slot, p, 0, 0)),
                pl.BlockSpec((LANES, width), lambda p, count, at: (at[first], 0)),
                pl.BlockSpec((LANES, width), lambda p, count, at: (at[first + 1], 0)),
            ],
            out_specs=[
                pl.BlockSpec((2, 4, LANES, width), lambda p, *_: (0, 0, 0, 0)),
                pl.BlockSpec((1, 768), lambda p, *_: (0, 0)),
                pl.BlockSpec((1, seq, 768), lambda p, *_: (p, 0, 0)),
            ],
            scratch_shapes=[
                pltpu.VMEM((pairs * seq, 768), WIDE),
                pltpu.VMEM((pairs * seq, 256), WIDE),
                pltpu.VMEM(rows.shape, LOW),
                pltpu.VMEM(cot.shape, LOW),
                pltpu.VMEM((2 * LANES, width), LOW),
                pltpu.SemaphoreType.DMA((2,)),
            ],
        ),
        out_shape=[
            jax.ShapeDtypeStruct((2, 4, LANES, width), LOW),
            jax.ShapeDtypeStruct((1, 768), WIDE),
            jax.ShapeDtypeStruct(qkv.shape[1:], LOW),
        ],
        name="attend_back",
        compiler_params=pltpu.CompilerParams(vmem_limit_bytes=56 * 1024 * 1024),
    )(counts, places, rows, cot, cot.reshape(pairs, seq, width), qkv, context, out, out)


def middle_kernel(
    spot_ref, rows_ref, context_ref, own_ref, near_ref, far_ref, bias_ref, gain_ref, shift_ref, *refs
):
    middle_ref, hidden_ref, out_ref = refs

    @pl.when(pl.program_id(0) == 0)
    def _():
        for i in range(8):
            source = own_ref if i < 4 else (near_ref if i < 6 else far_ref)
            start = pl.multiple_of(spot_ref[i] * LANES, LANES)
            out_ref[i * LANES : (i + 1) * LANES, :] = source[pl.ds(start, LANES), :]

    context = jnp.concatenate([context_ref[i, 0] for i in range(4)], 1)
    attended = dot(context, out_ref[...], 1, 0)
    middle = rows_ref[0].astype(WIDE) + attended + bias_ref[...].astype(WIDE)
    middle_ref[0] = middle
    center = middle - jnp.mean(middle, -1, keepdims=True)
    spread = jnp.mean(center * center, -1, keepdims=True)
    hidden = center * lax.rsqrt(spread + EPS) * gain_ref[...].astype(WIDE)
    hidden_ref[0] = (hidden + shift_ref[...].astype(WIDE)).astype(LOW)


def middle_step(spots, rows, context, own, near, far, bias, gain, shift):
    pairs, seq, width = rows.shape
    block = lambda: pl.BlockSpec((1, seq, width), lambda p, *_: (p, 0, 0))
    return pl.pallas_call(
        middle_kernel,
        grid_spec=pltpu.PrefetchScalarGridSpec(
            num_scalar_prefetch=1,
            grid=(pairs,),
            in_specs=[
                block(),
                pl.BlockSpec((4, 1, seq, 256), lambda p, *_: (0, p, 0, 0)),
                resident(own.shape),
                resident(near.shape),
                resident(far.shape),
            ]
            + [resident((1, width))] * 3,
            out_specs=[block(), block()],
            scratch_shapes=[pltpu.VMEM((8 * LANES, width), LOW)],
        ),
        out_shape=[
            jax.ShapeDtypeStruct(rows.shape, WIDE),
            jax.ShapeDtypeStruct(rows.shape, LOW),
        ],
        name="middle",
        compiler_params=pltpu.CompilerParams(vmem_limit_bytes=56 * 1024 * 1024),
    )(spots, rows, context, own, near, far, bias, gain, shift)


def mlp_kernel(step, turned, spot_ref, hidden_ref, cot_ref, *refs):
    ups, downs, biases = refs[:4], refs[4:8], refs[8:12]
    near_ref, far_ref, bias_out, act_ref, pre_ref, up_ref, down_ref, bias_ref = refs[-8:]
    rows = hidden_ref.shape[0]
    for r in range(4):
        span = slice(r * LANES, (r + 1) * LANES)
        if turned:
            up_ref[0, :, span] = ups[r][:, 0].reshape(LANES, -1).T
            down_ref[0, span, :] = downs[r][:, 0].reshape(LANES, -1)
        else:
            up_ref[0, :, span] = ups[r][...]
            down_ref[0, span, :] = downs[r][...]
        bias_ref[:, span] = biases[r][...].astype(WIDE)

    def one(i, carry):
        at = pl.ds(i * step, step)
        pre_act = dot(hidden_ref[at, :], up_ref[0], 1, 0) + bias_ref[...]
        act_grad = dot(cot_ref[at, :], down_ref[0], 1, 1)
        chance = 0.5 + 0.5 * lax.erf(pre_act * ROOT_HALF)
        act_ref[0, at, :] = (pre_act * chance).astype(LOW)
        slope = chance + pre_act * (NORMAL * jnp.exp(-0.5 * pre_act * pre_act))
        pre_ref[0, at, :] = (act_grad * slope).astype(LOW)
        return carry

    for i in range(rows // step):
        one(i, 0)
    up_grad = dot(pre_ref[0], hidden_ref[...], 0, 0).astype(LOW).reshape(4, LANES, -1)
    down_grad = dot(act_ref[0], cot_ref[...], 0, 0).astype(LOW).reshape(4, LANES, -1)
    bias_out[0] = jnp.sum(pre_ref[0].astype(WIDE), 0, keepdims=True)
    for i in range(2):
        near_ref[i, 0] = up_grad[i]
        near_ref[i, 1] = down_grad[i]
        far_ref[i, 0] = up_grad[2 + i]
        far_ref[i, 1] = down_grad[2 + i]


def mlp(first, turned, spots, hidden, cot, ups, downs, biases, buffers):
    rows, width = hidden.shape
    operands = list(ups) + list(downs) + list(biases)
    tile = 4 * LANES
    grad = jax.ShapeDtypeStruct((2, 4, LANES, width), LOW)
    grad_block = pl.BlockSpec((2, 2, LANES, width), lambda j, *_: (0, j, 0, 0))
    return pl.pallas_call(
        functools.partial(mlp_kernel, rows // 2, turned),
        grid_spec=pltpu.PrefetchScalarGridSpec(
            num_scalar_prefetch=1,
            grid=(2,),
            in_specs=[pl.BlockSpec(memory_space=pltpu.VMEM)] * 2
            + [spec for _, spec in operands]
            + [ANYWHERE] * len(buffers),
            out_specs=[grad_block] * 2
            + [
                pl.BlockSpec((1, 1, tile), lambda j, *_: (j, 0, 0)),
                pl.BlockSpec((1, rows, tile), lambda j, *_: (first // 2, 0, j)),
                pl.BlockSpec((1, rows, tile), lambda j, *_: (first // 2, 0, j)),
                pl.BlockSpec((1, width, tile), lambda j, *_: (first // 2, 0, j)),
                pl.BlockSpec((1, tile, width), lambda j, *_: (first // 2, j, 0)),
            ],
            scratch_shapes=[pltpu.VMEM((1, tile), WIDE)],
        ),
        out_shape=[grad] * 2
        + [
            jax.ShapeDtypeStruct((2, 1, tile), WIDE),
            jax.ShapeDtypeStruct((4, rows, 2 * tile), LOW),
            jax.ShapeDtypeStruct((4, rows, 2 * tile), LOW),
            jax.ShapeDtypeStruct((4, width, 2 * tile), LOW),
            jax.ShapeDtypeStruct((4, 2 * tile, width), LOW),
        ],
        input_output_aliases={3 + len(operands) + i: 3 + i for i in range(len(buffers))},
        name="mlp",
        compiler_params=pltpu.CompilerParams(vmem_limit_bytes=36 * 1024 * 1024),
    )(spots, hidden, cot, *[array for array, _ in operands], *buffers)


def norm_back(values, gain, grad):
    center = values - jnp.mean(values, -1, keepdims=True)
    scale = lax.rsqrt(jnp.mean(center * center, -1, keepdims=True) + EPS)
    unit = center * scale
    inner = grad * gain
    pulled = scale * (
        inner
        - jnp.mean(inner, -1, keepdims=True)
        - unit * jnp.mean(inner * unit, -1, keepdims=True)
    )
    return pulled, jnp.sum(grad * unit, 0, keepdims=True), jnp.sum(grad, 0, keepdims=True)


def mlp_back_kernel(pre_ref, up_ref, middle_hbm, cot_hbm, gain_ref, grad_ref, low_ref, sums_ref, *refs):
    sum_buf, middle_buf, cot_buf, sems = refs
    step = pl.program_id(0)
    copies = [
        pltpu.make_async_copy(middle_hbm, middle_buf, sems.at[0]),
        pltpu.make_async_copy(cot_hbm, cot_buf, sems.at[1]),
    ]
    part = dot(pre_ref[0], up_ref[0], 1, 1)

    @pl.when(step == 0)
    def _():
        for copy in copies:
            copy.start()
        sum_buf[...] = part

    @pl.when(step > 0)
    def _():
        sum_buf[...] += part

    @pl.when(step == pl.num_programs(0) - 1)
    def _():
        for copy in copies:
            copy.wait()
        sums_ref[...] = jnp.zeros_like(sums_ref)
        chunk = 224

        def one(i, carry):
            at = pl.ds(pl.multiple_of(i * chunk, chunk), chunk)
            cot = cot_buf[at, :].astype(WIDE)
            pulled, gain_grad, shift_grad = norm_back(
                middle_buf[at, :], gain_ref[...].astype(WIDE), sum_buf[at, :]
            )
            grad = cot + pulled
            low = grad.astype(LOW)
            grad_ref[at, :] = grad
            low_ref[at, :] = low
            sums_ref[0:1, :] += gain_grad
            sums_ref[1:2, :] += shift_grad
            sums_ref[2:3, :] += jnp.sum(low.astype(WIDE), 0, keepdims=True)
            sums_ref[3:4, :] += jnp.sum(cot, 0, keepdims=True)
            return carry

        lax.fori_loop(0, grad_ref.shape[0] // chunk, one, 0)


def mlp_back(pre_grads, ups, middle, cot, gain):
    tiles, rows, tile = pre_grads.shape
    width = cot.shape[1]
    return pl.pallas_call(
        mlp_back_kernel,
        grid=(tiles,),
        in_specs=[
            pl.BlockSpec((1, rows, tile), lambda j: (j, 0, 0)),
            pl.BlockSpec((1, width, tile), lambda j: (j, 0, 0)),
            ANYWHERE,
            ANYWHERE,
            resident((1, width)),
        ],
        out_specs=[resident((rows, width)), resident((rows, width)), resident((8, width))],
        out_shape=[
            jax.ShapeDtypeStruct((rows, width), WIDE),
            jax.ShapeDtypeStruct((rows, width), LOW),
            jax.ShapeDtypeStruct((8, width), WIDE),
        ],
        scratch_shapes=[
            pltpu.VMEM((rows, width), WIDE),
            pltpu.VMEM((rows, width), WIDE),
            pltpu.VMEM((rows, width), LOW),
            pltpu.SemaphoreType.DMA((2,)),
        ],
        name="mlp_back",
        compiler_params=pltpu.CompilerParams(vmem_limit_bytes=44 * 1024 * 1024),
    )(pre_grads, ups, middle, cot, gain)


def mlp_out_kernel(half, act_ref, down_ref, middle_hbm, bias_ref, *refs):
    out_ref, sum_buf, middle_buf, sem = refs[-4:]
    step = pl.program_id(0)
    rows = out_ref.shape[0]
    copy = pltpu.make_async_copy(middle_hbm.at[pl.ds(half * rows, rows), :], middle_buf, sem)
    part = dot(act_ref[0], down_ref[0], 1, 0)

    @pl.when(step == 0)
    def _():
        copy.start()
        sum_buf[...] = part

    @pl.when(step > 0)
    def _():
        sum_buf[...] += part

    @pl.when(step == pl.num_programs(0) - 1)
    def _():
        copy.wait()
        out_ref[...] = (sum_buf[...] + middle_buf[...] + bias_ref[...].astype(WIDE)).astype(LOW)


def mlp_out(half, acts, downs, middle, bias, buffers):
    tiles, rows, tile = acts.shape
    width = middle.shape[1]
    count = rows // 2
    return pl.pallas_call(
        functools.partial(mlp_out_kernel, half),
        grid=(tiles,),
        in_specs=[
            pl.BlockSpec((1, count, tile), lambda j: (j, half, 0)),
            pl.BlockSpec((1, tile, width), lambda j: (j, 0, 0)),
            ANYWHERE,
            resident((1, width)),
        ]
        + [ANYWHERE] * len(buffers),
        out_specs=pl.BlockSpec((count, width), lambda j: (half, 0)),
        out_shape=jax.ShapeDtypeStruct((rows, width), LOW),
        scratch_shapes=[
            pltpu.VMEM((count, width), WIDE),
            pltpu.VMEM((count, width), WIDE),
            pltpu.SemaphoreType.DMA(()),
        ],
        input_output_aliases={4: 0} if buffers else {},
        name="mlp_out",
        compiler_params=pltpu.CompilerParams(vmem_limit_bytes=56 * 1024 * 1024),
    )(acts, downs, middle, bias, *buffers)


def pack_kernel(spot_ref, *refs):
    out_refs = refs[-2:]
    shared_one, shared_two = refs[8:10]
    for side in range(2):
        near, far, first, second = refs[4 * side : 4 * side + 4]
        out = out_refs[side]
        for r in range(4):
            at = spot_ref[r]
            source = near if r < 2 else far
            lanes = (r % 2) * LANES
            out[pl.ds(at, 1), :] = source[:, lanes : lanes + LANES]
            out[pl.ds(4 + at, 1), :] = source[:, 512 + lanes : 512 + lanes + LANES]
            for j in range(4):
                sums = first if j < 2 else second
                out[pl.ds(8 + at * 4 + j, 1), :] = sums[j % 2, :, r * LANES : (r + 1) * LANES]
        rows = [(shared_one, 0), (shared_one, 1), (shared_two, 2), (shared_two, 0), (shared_two, 1), (shared_two, 3)]
        for k, (source, row) in enumerate(rows):
            for i in range(8):
                at = 24 + 8 * k + i
                out[at : at + 1, :] = source[row : row + 1, i * LANES : (i + 1) * LANES]


def pack(spots, own, other, sums_one, sums_two):
    return pl.pallas_call(
        pack_kernel,
        grid_spec=pltpu.PrefetchScalarGridSpec(
            num_scalar_prefetch=1,
            grid=(1,),
            in_specs=[resident(item.shape) for item in (*own, *other, sums_one, sums_two)],
            out_specs=[resident((72, LANES))] * 2,
        ),
        out_shape=[jax.ShapeDtypeStruct((72, LANES), WIDE)] * 2,
        name="pack",
        compiler_params=pltpu.CompilerParams(vmem_limit_bytes=8 * 1024 * 1024),
    )(spots, *own, *other, sums_one, sums_two)


def input_kernel(zero_ref, one_ref, two_ref, three_ref, weight_ref, rows_ref, above_ref, gain_ref, out_ref, sums_ref):
    pulled_sum = dot(zero_ref[0], weight_ref[0], 1, 1)
    for i, grad_ref in enumerate((one_ref, two_ref, three_ref)):
        pulled_sum = pulled_sum + dot(grad_ref[0], weight_ref[i + 1], 1, 1)
    pulled, gain_grad, shift_grad = norm_back(
        rows_ref[0].astype(WIDE), gain_ref[...].astype(WIDE), pulled_sum
    )
    out_ref[0] = (above_ref[0] + pulled).astype(LOW)

    @pl.when(pl.program_id(0) == 0)
    def _():
        sums_ref[...] = jnp.zeros_like(sums_ref)

    sums_ref[0:1, :] += gain_grad
    sums_ref[1:2, :] += shift_grad


def input_step(grads, weights, rows, above, gain):
    pairs, seq, width = rows.shape
    block = lambda: pl.BlockSpec((1, seq, width), lambda p: (p, 0, 0))
    return pl.pallas_call(
        input_kernel,
        grid=(pairs,),
        in_specs=[
            pl.BlockSpec((1, seq, 768), lambda p: (p, 0, 0)),
            pl.BlockSpec((1, seq, 768), lambda p: (p, 0, 0)),
            pl.BlockSpec((1, seq, 768), lambda p: (p, 0, 0)),
            pl.BlockSpec((1, seq, 768), lambda p: (p, 0, 0)),
            resident(weights.shape),
            block(),
            block(),
            resident((1, width)),
        ],
        out_specs=[block(), resident((8, width))],
        out_shape=[
            jax.ShapeDtypeStruct(rows.shape, LOW),
            jax.ShapeDtypeStruct((8, width), WIDE),
        ],
        name="input_grad",
        compiler_params=pltpu.CompilerParams(vmem_limit_bytes=28 * 1024 * 1024),
    )(*grads, weights, rows, above, gain)


def place_kernel(turned, spot_ref, near_ref, far_ref, *refs):
    outs = refs[-len(turned) :]
    core = pl.program_id(1) ^ spot_ref[0]
    for i, turn in enumerate(turned):
        parts = []
        for z in range(4):
            at = z ^ spot_ref[2]
            parts.append(
                jnp.where(core == 0, near_ref[at, i], far_ref[at, i])
            )
        block = jnp.concatenate(parts, 0)
        outs[i][...] = (block.T if turn else block).astype(WIDE)


def place(turned, chunk, chunks, spots, near, far, shapes, buffers):
    _, kinds, rows, width = near.shape
    source = lambda: pl.BlockSpec(
        (4, kinds, rows, width), lambda x, c, spot: (x ^ spot[1], 0, 0, 0)
    )
    specs = [
        pl.BlockSpec((width, LANES), lambda x, c, spot: (0, (c * 2 + x) * chunks + chunk))
        if turn
        else pl.BlockSpec((LANES, width), lambda x, c, spot: ((c * 2 + x) * chunks + chunk, 0))
        for turn in turned
    ]
    return pl.pallas_call(
        functools.partial(place_kernel, turned),
        grid_spec=pltpu.PrefetchScalarGridSpec(
            num_scalar_prefetch=1,
            grid=(2, 2),
            in_specs=[source(), source()] + [ANYWHERE] * len(buffers),
            out_specs=specs,
        ),
        out_shape=[jax.ShapeDtypeStruct(shape, WIDE) for shape in shapes],
        input_output_aliases={3 + i: i for i in range(len(buffers))},
        name="place",
        compiler_params=pltpu.CompilerParams(vmem_limit_bytes=20 * 1024 * 1024),
    )(spots, near, far, *buffers)


def gathered_kernel(source_ref, *refs):
    up_ref, down_ref = refs[-2:]
    rows = [[source_ref[high, low, 0, 0] for high in range(2)] for low in range(2)]
    for kind, out_ref in enumerate((up_ref, down_ref)):
        parts = []
        for sub in range(2):
            for low in range(2):
                for high in range(2):
                    parts.append(rows[low][high][2 * sub + kind])
        block = jnp.concatenate(parts, 0)
        out_ref[...] = (block.T if kind == 0 else block).astype(WIDE)


def gathered(chunk, chunks, source, shapes, buffers):
    kinds, rows, width = source.shape[1:]
    source = source.reshape((2, 2, 2, 2, kinds, rows, width))
    span = 2 * LANES
    return pl.pallas_call(
        gathered_kernel,
        grid=(2, 2),
        in_specs=[
            pl.BlockSpec((2, 2, 1, 1, kinds, rows, width), lambda c, x: (0, 0, x, c, 0, 0, 0))
        ]
        + [ANYWHERE] * len(buffers),
        out_specs=[
            pl.BlockSpec((width, span), lambda c, x: (0, (c * 2 + x) * chunks + chunk)),
            pl.BlockSpec((span, width), lambda c, x: ((c * 2 + x) * chunks + chunk, 0)),
        ],
        out_shape=[jax.ShapeDtypeStruct(shape, WIDE) for shape in shapes],
        input_output_aliases={1 + i: i for i in range(len(buffers))},
        name="gathered",
        compiler_params=pltpu.CompilerParams(vmem_limit_bytes=24 * 1024 * 1024),
    )(source, *buffers)


def paired_body(
    layer_in,
    patch_count,
    attn_gain,
    attn_shift,
    query_weight,
    query_bias,
    key_weight,
    value_weight,
    value_bias,
    out_weight,
    out_bias,
    mlp_gain,
    mlp_shift,
    up_weight,
    up_bias,
    down_weight,
    down_bias,
    layer_cot,
):
    groups = lax.axis_size("dp")
    rank = lax.axis_index("dp")
    half_id = lax.axis_index("mp")
    core_id, x_id, zlow_id, zhigh_id = rank & 1, (rank >> 1) & 1, (rank >> 2) & 1, (rank >> 3) & 1
    part = core_id * 2 + x_id
    spots = jnp.stack([part, part ^ 1, part ^ 2, part ^ 3]).astype(jnp.int32)
    sides = jnp.stack([x_id, x_id ^ 1, x_id, x_id ^ 1]).astype(jnp.int32)
    place_spots = jnp.stack([core_id, x_id, zlow_id * 2 + zhigh_id]).astype(jnp.int32)

    swap = lambda value, bit: flip(value, "dp", bit, groups)
    across = lambda value: flip(value, "mp", 1, 2)

    rows, width = layer_in.shape
    heads_width = query_weight.shape[1]
    hidden_width = up_weight.shape[1]
    block = hidden_width // 4
    pairs = rows // SEQ
    counts = pick(patch_count, half_id, pairs, 0)
    row_vec = lambda vec: vec.reshape(1, -1)

    gate = lambda value, *waits: after(value, *waits) if waits else value
    shape_three = (pairs, SEQ, width)
    subs = block // LANES

    slice_rows = LANES // 2
    slice_at = (rank // 4) * 2 * subs + rank % 4
    slices = jnp.stack(
        [
            jnp.stack(
                [
                    pick(up_weight, slice_at + 4 * i, slice_rows, 1).T,
                    pick(down_weight, slice_at + 4 * i, slice_rows, 0),
                ]
            )
            for i in range(2)
        ]
    )
    slices = across(slices)
    sent_qk = jnp.stack([pick(w, core_id, heads_width // 2, 1) for w in (query_weight, key_weight)])
    value_near = across(pick(value_weight, part, LANES, 1))
    sent_bias = row_vec(jnp.concatenate([query_bias, value_bias, up_bias]))
    raw_out = pick(out_weight, core_id, heads_width // 2, 0)
    rows_in = layer_in.astype(WIDE)
    normed = layer_norm(
        rows_in, attn_gain.astype(WIDE), attn_shift.astype(WIDE)
    ).astype(LOW)
    normed_three = normed.reshape(shape_three)

    def own_inputs():
        weights = [
            (w, pl.BlockSpec((width, LANES), lambda g, p, spot, count, i=i: (0, spot[2 * g + i])))
            for w in (query_weight, key_weight, value_weight)
            for i in range(2)
        ]
        biases = [
            (row_vec(b), pl.BlockSpec((1, LANES), lambda g, p, spot, count, i=i: (0, spot[2 * g + i])))
            for b in (query_bias, value_bias)
            for i in range(2)
        ]
        return weights, biases

    def other_inputs(group, qk, values):
        weights = [
            (qk, pl.BlockSpec((None, width, LANES), lambda g, p, side, count, k=k, i=i: (k, 0, side[i])))
            for k in range(2)
            for i in range(2)
        ]
        weights += [(item, pl.BlockSpec((width, LANES), lambda g, p, *_: (0, 0))) for item in values]
        biases = [
            (bias_other, pl.BlockSpec((1, LANES), lambda g, p, side, count, k=k, i=i: (0, 4 * k + side[4 + 2 * group + i])))
            for k in range(2)
            for i in range(2)
        ]
        return weights, biases

    other_spots = jnp.concatenate([sides, spots])
    slices, value_near, sent_qk, raw_out, sent_bias, normed, spots, other_spots, counts = lax.optimization_barrier(
        (slices, value_near, sent_qk, raw_out, sent_bias, normed, spots, other_spots, counts)
    )
    normed_three = normed.reshape(shape_three)
    near_qk = across(sent_qk)
    bias_other = across(sent_bias)
    value_side = swap(value_near, XBIT)
    gathered_weights = [lax.all_gather(slices[0], "dp"), lax.all_gather(slices[1], "dp")]
    kept = attend(
        0, 2, spots, counts, normed_three, *own_inputs(), []
    )
    near_qk, bias_other, value_side, _ = lax.optimization_barrier((near_qk, bias_other, value_side, kept[1]))
    sent_out = after(raw_out, near_qk)
    near_out = across(sent_out)
    far_qk, far_values = swap(near_qk, CORE), [swap(value_near, CORE), swap(value_side, CORE)]
    kept = attend(
        2, 1, gate(other_spots, sent_out), counts, normed_three, *other_inputs(0, near_qk, (value_near, value_side)), kept
    )
    near_out, far_qk, far_values, _ = lax.optimization_barrier((near_out, far_qk, far_values, kept[1]))
    far_out = swap(near_out, CORE)
    kept = attend(
        3, 1, gate(other_spots, near_out), counts, normed_three, *other_inputs(1, far_qk, far_values), kept
    )
    places = jnp.concatenate([spots, sides])
    middle, hidden = middle_step(
        places,
        layer_in.reshape(shape_three),
        kept[1],
        out_weight,
        near_out,
        far_out,
        row_vec(out_bias),
        row_vec(mlp_gain),
        row_vec(mlp_shift),
    )
    middle = middle.reshape(rows, width)
    hidden = hidden.reshape(rows, width)

    def own_mlp(first):
        ups = [
            (up_weight, pl.BlockSpec((width, LANES), lambda j, spot, r=r: (0, spot[r] * subs + first + j)))
            for r in range(4)
        ]
        downs = [
            (down_weight, pl.BlockSpec((LANES, width), lambda j, spot, r=r: (spot[r] * subs + first + j, 0)))
            for r in range(4)
        ]
        biases = [
            (row_vec(up_bias), pl.BlockSpec((1, LANES), lambda j, spot, r=r: (0, spot[r] * subs + first + j)))
            for r in range(4)
        ]
        return ups, downs, biases

    def other_mlp(first):
        source = gathered_weights[first // 2]
        ups, downs = (
            [
                (source, pl.BlockSpec((2, 1, slice_rows, width), lambda j, spot, r=r, k=k: (spot[r] * 2 + j, k, 0, 0)))
                for r in range(4)
            ]
            for k in range(2)
        )
        biases = [
            (bias_other, pl.BlockSpec((1, LANES), lambda j, spot, r=r: (0, 8 + spot[r] * subs + first + j)))
            for r in range(4)
        ]
        return ups, downs, biases

    def cut(item, index):
        count, lanes, cols = item.shape
        return pick(item.reshape(count, 2, lanes // 2, cols), index, 1, 1)[:, 0]

    def outbound(near, far, first, last):
        return total(near[:, first:last], far[:, first:last])

    def sideways(near, far, beyond, first, last):
        return total(near[1, first:last], far[1, first:last], beyond[1])

    def collected(near, far, beyond, side, first, last):
        return total(near[0, first:last], far[0, first:last], beyond[0], side)

    def halves(item):
        return cut(item, zlow_id ^ 1), cut(item, zlow_id)

    def quarters(item):
        return cut(item, zhigh_id ^ 1), cut(item, zhigh_id)

    back = lambda slot, *wait: attend_back(
        slot,
        2 * slot,
        gate(counts, *wait),
        places,
        normed,
        attn_grad,
        kept,
        (out_weight, out_weight, near_out, far_out)[slot],
    )

    together = lambda *items: lax.optimization_barrier(items)
    other_a = mlp(2, True, spots, hidden, layer_cot, *other_mlp(0), [])
    far_other_a = swap(other_a[1], CORE)
    own_a = mlp(0, False, spots, hidden, layer_cot, *own_mlp(0), other_a[3:])
    far_other_a, far, _ = together(far_other_a, own_a[1], own_a[2])
    far_own_a = swap(far, CORE)
    out_a = [outbound(other_a[0], far_other_a, *span) for span in ((0, 1), (1, 2), (2, 4))]
    own_b = mlp(6, False, gate(spots, *out_a), hidden, layer_cot, *own_mlp(2), own_a[3:])
    beyond_a0, far_own_a, far, _ = together(across(out_a[0]), far_own_a, own_b[1], own_b[2])
    far_own_b = swap(far, CORE)
    other_b = mlp(
        4, True, gate(spots, beyond_a0, far_own_a), hidden, layer_cot, *other_mlp(2), own_b[3:]
    )
    acts, pre_grads, ups_all, downs_all = other_b[3:]
    beyond_a1, far_own_b, far, _ = together(
        across(after(out_a[1], beyond_a0)), far_own_b, other_b[1], other_b[2]
    )
    far_other_b = swap(far, CORE)
    beyond_a01 = jnp.concatenate([beyond_a0, beyond_a1], 1)
    side_a01 = sideways(own_a[0], far_own_a, beyond_a01, 0, 2)
    middle_grad, attn_grad, sums_two = mlp_back(
        pre_grads, ups_all, middle, layer_cot, gate(row_vec(mlp_gain), side_a01, beyond_a01, far_own_b)
    )
    beyond_a23, arrived_a01, far_other_b, _ = together(
        across(after(out_a[2], beyond_a1)), swap(side_a01, XBIT), far_other_b, sums_two
    )
    side_a23 = sideways(own_a[0], far_own_a, beyond_a23, 2, 4)
    out_b = [outbound(other_b[0], far_other_b, *span) for span in ((0, 2), (2, 4))]
    other_far, bias_other_far, grads_three = back(3, side_a23, arrived_a01, *out_b)
    beyond_b01, arrived_a23, far, _ = together(
        across(out_b[0]), swap(side_a23, XBIT), other_far, bias_other_far
    )
    late_other_far = swap(far, CORE)
    sum_a = jnp.concatenate(
        [
            collected(own_a[0], far_own_a, beyond_a01, arrived_a01, 0, 2),
            collected(own_a[0], far_own_a, beyond_a23, arrived_a23, 2, 4),
        ]
    )
    low_a, keep_a = halves(sum_a)
    side_b01 = sideways(own_b[0], far_own_b, beyond_b01, 0, 2)
    other_near, bias_other_near, grads_two = back(2, low_a, sum_a, side_b01, grads_three)
    beyond_b23, arrived_b01, low_a, late_other_far, _ = together(
        across(after(out_b[1], beyond_b01)), swap(side_b01, XBIT), swap(low_a, ZLOW), late_other_far, bias_other_near
    )
    high_a, keep_a = quarters(total(keep_a, low_a))
    side_b23 = sideways(own_b[0], far_own_b, beyond_b23, 2, 4)
    late_out = [outbound(other_near, late_other_far, *span) for span in ((0, 2), (2, 4))]
    own_far, bias_own_far, grads_one = back(1, high_a, side_b23, arrived_b01, *late_out, grads_two)
    late_beyond0, arrived_b23, high_a, far, _ = together(
        across(late_out[0]), swap(side_b23, XBIT), swap(high_a, ZHIGH), own_far, bias_own_far
    )
    late_own_far = swap(far, CORE)
    one_a = total(keep_a, high_a)
    sum_b = jnp.concatenate(
        [
            collected(own_b[0], far_own_b, beyond_b01, arrived_b01, 0, 2),
            collected(own_b[0], far_own_b, beyond_b23, arrived_b23, 2, 4),
        ]
    )
    low_b, keep_b = halves(sum_b)
    gathered_a = lax.all_gather(one_a, "dp")
    own_near, bias_own_near, grads_zero = back(0, one_a, low_b, sum_b, late_beyond0, grads_one)
    late_beyond1, late_own_far, low_b, _ = together(
        across(after(late_out[1], late_beyond0)), late_own_far, swap(low_b, ZLOW), bias_own_near
    )
    high_b, keep_b = quarters(total(keep_b, low_b))
    late_side0 = sideways(own_near, late_own_far, late_beyond0, 0, 2)
    late_side1 = sideways(own_near, late_own_far, late_beyond1, 2, 4)
    grad_in, sums_one = input_step(
        (grads_zero, grads_one, grads_two, grads_three),
        kept[2],
        layer_in.reshape(shape_three),
        middle_grad.reshape(shape_three),
        gate(row_vec(attn_gain), high_b, late_side0, late_side1),
    )
    high_b, late_arrived0, sums_one = together(swap(high_b, ZHIGH), swap(late_side0, XBIT), sums_one)
    one_b = total(keep_b, high_b)
    gathered_b = lax.all_gather(one_b, "dp")
    quarter_id = zlow_id * 2 + zhigh_id
    z_bits = [None, ZHIGH, ZLOW, ZLOW | ZHIGH]

    def four(item):
        count, lanes, cols = item.shape
        item = item.reshape(count, 4, lanes // 4, cols)
        return [pick(item, quarter_id ^ r, 1, 1)[:, 0] for r in range(4)]

    def send_four(items):
        return [swap(items[r], z_bits[r]) for r in range(1, 4)]

    late_four0 = four(collected(own_near, late_own_far, late_beyond0, late_arrived0, 0, 2))
    own_vec, other_vec = pack(
        spots,
        (bias_own_near, bias_own_far, own_a[2], own_b[2]),
        (bias_other_near, bias_other_far, other_a[2], other_b[2]),
        sums_one,
        sums_two,
    )
    layer_out = mlp_out(
        0, acts, downs_all, middle, gate(row_vec(down_bias), one_b, other_vec, *late_four0), []
    )
    late_arrived1, late_got0, vec_got, mark = together(
        swap(after(late_side1, late_arrived0), XBIT), send_four(late_four0), across(other_vec), layer_out
    )
    late_one0 = total(late_four0[0], *late_got0)
    late_four1 = four(collected(own_near, late_own_far, late_beyond1, late_arrived1, 2, 4))
    vec = own_vec + vec_got
    layer_out = mlp_out(
        1, acts, downs_all, middle, gate(row_vec(down_bias), late_one0, vec, *late_four1), [mark]
    )
    late_got1, late_have0, layer_out = together(
        send_four(late_four1), send_four([late_one0] * 4), layer_out
    )
    late_one1 = total(late_four1[0], *late_got1)
    late_have0 = jnp.stack([late_one0, *late_have0])
    up_shape, down_shape = up_weight.shape, down_weight.shape
    placed = gathered(
        0, 2, gate(gathered_a, late_one1, late_have0), (up_shape, down_shape), []
    )
    late_have1, late_side0, vec_got, *placed = together(
        send_four([late_one1] * 4), swap(late_have0, XBIT), swap(vec, CORE), *placed
    )
    late_have1 = jnp.stack([late_one1, *late_have1])
    late_have0 = jnp.concatenate([late_have0, late_side0])
    vec = vec + vec_got
    placed = gathered(
        1, 2, gate(gathered_b, late_have1, late_have0, vec), (up_shape, down_shape), placed
    )
    late_side1, late_far0, vec_got, grad_up_weight, grad_down_weight = together(
        swap(late_have1, XBIT), swap(late_have0, CORE), swap(vec, XBIT), *placed
    )
    late_have1 = jnp.concatenate([late_have1, late_side1])
    vec = vec + vec_got
    grad_query_weight, grad_key_weight = place(
        (True, True), 0, 1, gate(place_spots, late_have1, vec), late_have0, late_far0, (query_weight.shape,) * 2, []
    )
    late_far1, vec_got, grad_query_weight, grad_key_weight = together(
        swap(late_have1, CORE), send_four([vec] * 4), grad_query_weight, grad_key_weight
    )
    vec = ((vec + vec_got[0]) + (vec_got[1] + vec_got[2])).reshape(-1)
    grad_value_weight, grad_out_weight = place(
        (True, False), 0, 1, place_spots, late_have1, late_far1, (value_weight.shape, out_weight.shape), []
    )
    grad_query_bias = vec[:heads_width]
    grad_value_bias = vec[heads_width : 2 * heads_width]
    grad_up_bias = vec[2 * heads_width : 2 * heads_width + hidden_width]
    (
        grad_attn_gain,
        grad_attn_shift,
        grad_out_bias,
        grad_mlp_gain,
        grad_mlp_shift,
        grad_down_bias,
    ) = jnp.split(vec[2 * heads_width + hidden_width :], 6)
    return (
        layer_out,
        grad_in.reshape(rows, width),
        grad_attn_gain,
        grad_attn_shift,
        grad_query_weight,
        grad_query_bias,
        grad_key_weight,
        grad_value_weight,
        grad_value_bias,
        grad_out_weight,
        grad_out_bias,
        grad_mlp_gain,
        grad_mlp_shift,
        grad_up_weight,
        grad_up_bias,
        grad_down_weight,
        grad_down_bias,
    )


def solution(mesh):
    paired = mesh.shape["mp"] == 2 and mesh.shape["dp"] == 16
    body = paired_body if paired else general_body
    placed = (
        P(("dp", "mp"), None),
        P("dp"),
        P(),
        P(),
        P(None, "mp"),
        P("mp"),
        P(None, "mp"),
        P(None, "mp"),
        P("mp"),
        P("mp", None),
        P(),
        P(),
        P(),
        P(None, "mp"),
        P("mp"),
        P("mp", None),
        P(),
        P(("dp", "mp"), None),
    )
    return jax.shard_map(
        body,
        mesh=mesh,
        in_specs=placed,
        out_specs=(
            P(("dp", "mp"), None),
            P(("dp", "mp"), None),
            P(),
            P(),
            P(None, "mp"),
            P("mp"),
            P(None, "mp"),
            P(None, "mp"),
            P("mp"),
            P("mp", None),
            P(),
            P(),
            P(),
            P(None, "mp"),
            P("mp"),
            P("mp", None),
            P(),
        ),
        check_vma=False,
    )
```

```python
import functools

import jax
import jax.numpy as jnp
from jax import lax
from jax.experimental import pallas as pl
from jax.experimental.pallas import tpu as pltpu
from jax.sharding import PartitionSpec as P

HEAD_DIM = 64
TEXT = 40
SEQ = 280


EPS = 1e-05
SCALE = 0.125
NEGATIVE = -1e30


def layer_norm(values, gain, shift):
    center = values - jnp.mean(values, -1, keepdims=True)
    spread = jnp.mean(center * center, -1, keepdims=True)
    return center * lax.rsqrt(spread + EPS) * gain + shift


def exact_gelu(values):
    return jax.nn.gelu(values, approximate=False)


def matmul_rows(left, right):
    return jnp.dot(left, right, preferred_element_type=jnp.float32)


def contract_rows(left, right):
    return lax.dot_general(
        left, right, (((0,), (0,)), ((), ())), preferred_element_type=jnp.float32
    )


def contract_cols(left, right):
    return lax.dot_general(
        left, right, (((1,), (1,)), ((), ())), preferred_element_type=jnp.float32
    )


def column_sum(values):
    return jnp.sum(values.astype(jnp.float32), 0)


def general_body(
    layer_in,
    patch_count,
    attn_gain,
    attn_shift,
    query_weight,
    query_bias,
    key_weight,
    value_weight,
    value_bias,
    out_weight,
    out_bias,
    mlp_gain,
    mlp_shift,
    up_weight,
    up_bias,
    down_weight,
    down_bias,
    layer_cot,
):
    lowtype = jnp.bfloat16
    wide = jnp.float32
    rows_in = layer_in.astype(wide)
    gain_one = attn_gain.astype(wide)
    shift_one = attn_shift.astype(wide)
    gain_two = mlp_gain.astype(wide)
    shift_two = mlp_shift.astype(wide)
    normed_tok, norm_pull = jax.vjp(layer_norm, rows_in, gain_one, shift_one)
    group_rows = lax.all_gather(normed_tok.astype(lowtype), "mp", axis=0, tiled=True)
    query_rows = (matmul_rows(group_rows, query_weight) + query_bias.astype(wide)).astype(lowtype)
    key_rows = matmul_rows(group_rows, key_weight).astype(lowtype)
    value_rows = (matmul_rows(group_rows, value_weight) + value_bias.astype(wide)).astype(lowtype)
    pairs = patch_count.shape[0]
    local_width = query_weight.shape[1]
    local_heads = local_width // HEAD_DIM
    group_total = group_rows.shape[0]
    shape_four = (pairs, SEQ, local_heads, HEAD_DIM)
    query_blk = query_rows.reshape(shape_four)
    key_blk = key_rows.reshape(shape_four)
    value_blk = value_rows.reshape(shape_four)
    scores = jnp.einsum("pqhd,pkhd->phqk", query_blk, key_blk, preferred_element_type=wide) * SCALE
    valid = jnp.arange(SEQ)[None, :] < (TEXT + patch_count)[:, None]
    scores = jnp.where(valid[:, None, None, :], scores, NEGATIVE)
    probs = jax.nn.softmax(scores, axis=-1)
    probs_low = probs.astype(lowtype)
    context = jnp.einsum("phqk,pkhd->pqhd", probs_low, value_blk, preferred_element_type=wide)
    context = context.astype(lowtype).reshape(group_total, local_width)
    context_tok = lax.all_to_all(context, "mp", split_axis=0, concat_axis=1, tiled=True)
    out_full = lax.all_gather(out_weight, "mp", axis=0, tiled=True)
    attended = matmul_rows(context_tok, out_full) + out_bias.astype(wide)
    middle = rows_in + attended
    hidden_wide, mlp_pull = jax.vjp(layer_norm, middle, gain_two, shift_two)
    hidden_in = hidden_wide.astype(lowtype)
    cot_wide = layer_cot.astype(wide)
    up_full, bias_full, down_full = (
        lax.all_gather(up_weight, "mp", axis=1, tiled=True),
        lax.all_gather(up_bias, "mp", axis=0, tiled=True),
        lax.all_gather(down_weight, "mp", axis=0, tiled=True),
    )
    pre_act = matmul_rows(hidden_in, up_full) + bias_full.astype(wide)
    act_wide, gelu_pull = jax.vjp(exact_gelu, pre_act)
    act_low = act_wide.astype(lowtype)
    ffn_out = matmul_rows(act_low, down_full) + down_bias.astype(wide)
    whole_down = contract_rows(act_low, layer_cot)
    act_grad = contract_cols(layer_cot, down_full)
    pre_grad = gelu_pull(act_grad)[0].astype(lowtype)
    whole_up_bias = column_sum(pre_grad)
    whole_up = contract_rows(hidden_in, pre_grad)
    hidden_grad = contract_cols(pre_grad, up_full)
    grad_up_weight, grad_up_bias, grad_down_weight = (
        lax.psum_scatter(
            whole_up.astype(jnp.bfloat16), "mp", scatter_dimension=1, tiled=True
        ).astype(jnp.float32),
        lax.psum_scatter(
            whole_up_bias.astype(jnp.bfloat16), "mp", scatter_dimension=0, tiled=True
        ).astype(jnp.float32),
        lax.psum_scatter(
            whole_down.astype(jnp.bfloat16), "mp", scatter_dimension=0, tiled=True
        ).astype(jnp.float32),
    )
    layer_out = (middle + ffn_out).astype(lowtype)
    grad_down_bias = column_sum(layer_cot)
    middle_part, grad_gain_two, grad_shift_two = mlp_pull(hidden_grad)
    middle_grad = cot_wide + middle_part
    attn_grad = middle_grad.astype(lowtype)
    grad_out_bias = column_sum(attn_grad)
    grad_out_weight = lax.psum_scatter(
        contract_rows(context_tok, attn_grad).astype(jnp.bfloat16),
        "mp",
        scatter_dimension=0,
        tiled=True,
    ).astype(jnp.float32)
    context_grad_tok = contract_cols(attn_grad, out_full).astype(lowtype)
    context_grad = lax.all_to_all(
        context_grad_tok, "mp", split_axis=1, concat_axis=0, tiled=True
    ).reshape(shape_four)
    probs_grad = jnp.einsum("pqhd,pkhd->phqk", context_grad, value_blk, preferred_element_type=wide)
    value_grad = jnp.einsum("phqk,pqhd->pkhd", probs_low, context_grad, preferred_element_type=wide)
    value_grad = value_grad.astype(lowtype).reshape(group_total, local_width)
    score_grad = (probs * (probs_grad - jnp.sum(probs * probs_grad, -1, keepdims=True))).astype(
        lowtype
    )
    query_grad = (
        jnp.einsum("phqk,pkhd->pqhd", score_grad, key_blk, preferred_element_type=wide) * SCALE
    )
    query_grad = query_grad.astype(lowtype).reshape(group_total, local_width)
    key_grad = (
        jnp.einsum("phqk,pqhd->pkhd", score_grad, query_blk, preferred_element_type=wide) * SCALE
    )
    key_grad = key_grad.astype(lowtype).reshape(group_total, local_width)
    grad_query_weight = contract_rows(group_rows, query_grad)
    grad_key_weight = contract_rows(group_rows, key_grad)
    grad_value_weight = contract_rows(group_rows, value_grad)
    grad_query_bias = column_sum(query_grad)
    grad_value_bias = column_sum(value_grad)
    total = contract_cols(query_grad, query_weight)
    total = total + contract_cols(key_grad, key_weight)
    normed_grad = lax.psum_scatter(
        (total + contract_cols(value_grad, value_weight)).astype(jnp.bfloat16),
        "mp",
        scatter_dimension=0,
        tiled=True,
    ).astype(jnp.float32)
    input_part, grad_gain_one, grad_shift_one = norm_pull(normed_grad)
    grad_in = (middle_grad + input_part).astype(lowtype)
    (
        grad_query_weight,
        grad_query_bias,
        grad_key_weight,
        grad_value_weight,
        grad_value_bias,
        grad_out_weight,
        grad_up_weight,
        grad_up_bias,
        grad_down_weight,
    ) = (
        lax.psum(grad_query_weight.astype(jnp.bfloat16), "dp").astype(jnp.float32),
        lax.psum(grad_query_bias.astype(jnp.bfloat16), "dp").astype(jnp.float32),
        lax.psum(grad_key_weight.astype(jnp.bfloat16), "dp").astype(jnp.float32),
        lax.psum(grad_value_weight.astype(jnp.bfloat16), "dp").astype(jnp.float32),
        lax.psum(grad_value_bias.astype(jnp.bfloat16), "dp").astype(jnp.float32),
        lax.psum(grad_out_weight.astype(jnp.bfloat16), "dp").astype(jnp.float32),
        lax.psum(grad_up_weight.astype(jnp.bfloat16), "dp").astype(jnp.float32),
        lax.psum(grad_up_bias.astype(jnp.bfloat16), "dp").astype(jnp.float32),
        lax.psum(grad_down_weight.astype(jnp.bfloat16), "dp").astype(jnp.float32),
    )
    grad_gain_one, grad_shift_one, grad_out_bias, grad_gain_two, grad_shift_two, grad_down_bias = (
        lax.psum(
            (
                grad_gain_one,
                grad_shift_one,
                grad_out_bias,
                grad_gain_two,
                grad_shift_two,
                grad_down_bias,
            ),
            ("dp", "mp"),
        )
    )
    return (
        layer_out,
        grad_in,
        grad_gain_one,
        grad_shift_one,
        grad_query_weight,
        grad_query_bias,
        grad_key_weight,
        grad_value_weight,
        grad_value_bias,
        grad_out_weight,
        grad_out_bias,
        grad_gain_two,
        grad_shift_two,
        grad_up_weight,
        grad_up_bias,
        grad_down_weight,
        grad_down_bias,
    )


WIDE = jnp.float32
LOW = jnp.bfloat16
LANES = 128
ROOT_HALF = 0.7071067811865476
NORMAL = 0.3989422804014327
CORE, XBIT, ZLOW, ZHIGH = 1, 2, 4, 8


def dot(left, right, left_dim, right_dim):
    return lax.dot_general(
        left, right, (((left_dim,), (right_dim,)), ((), ())), preferred_element_type=WIDE
    )


def flip(value, axis, bit, size):
    return lax.ppermute(value, axis, [(i, i ^ bit) for i in range(size)])


def pick(value, index, width, axis):
    return lax.dynamic_slice_in_dim(value, index * width, width, axis)


def after(value, *others):
    return lax.optimization_barrier((value,) + others)[0]


def total(*items):
    result = items[0].astype(WIDE)
    for item in items[1:]:
        result = result + item.astype(WIDE)
    return result.astype(LOW)


def resident(shape):
    return pl.BlockSpec(shape, lambda *_: (0,) * len(shape), pipeline_mode=pl.Buffered(1))


ANYWHERE = pl.BlockSpec(memory_space=pl.ANY)


def attend_kernel(spot_ref, count_ref, rows_ref, *refs):
    weights, biases = refs[:6], refs[6:10]
    qkv_ref, context_ref, weight_ref, bias_ref = refs[-4:]
    pair = pl.program_id(1)

    @pl.when(pair == 0)
    def _():
        for i in range(6):
            weight_ref[0, :, i * LANES : (i + 1) * LANES] = weights[i][...]
        bias_ref[...] = jnp.zeros_like(bias_ref)
        for i in range(2):
            bias_ref[:, i * LANES : (i + 1) * LANES] = biases[i][...].astype(WIDE)
            bias_ref[:, (4 + i) * LANES : (5 + i) * LANES] = biases[2 + i][...].astype(WIDE)

    qkv = (dot(rows_ref[0], weight_ref[0], 1, 0) + bias_ref[...]).astype(LOW)
    qkv_ref[0, 0] = qkv
    length = TEXT + count_ref[pair]
    lane = lax.broadcasted_iota(jnp.int32, (SEQ, LANES), 1)
    padding = lax.broadcasted_iota(jnp.int32, (SEQ, SEQ), 1) >= length
    lane_low = lane < HEAD_DIM
    everything = []
    for tile in range(2):
        query, key, value = (
            qkv[:, i * 256 + tile * LANES : i * 256 + (tile + 1) * LANES] for i in range(3)
        )
        query = query * SCALE
        for side in range(2):
            mine = lane_low if side == 0 else jnp.logical_not(lane_low)
            everything.append((dot(jnp.where(mine, query, jnp.zeros_like(query)), key, 1, 1), value))
    heads = []
    for scores, value in everything:
        scores = jnp.where(padding, NEGATIVE, scores)
        power = jnp.exp(scores - jnp.max(scores, -1, keepdims=True))
        inverse = 1.0 / jnp.sum(power, -1, keepdims=True)
        heads.append(dot(power.astype(LOW), value, 1, 0) * inverse)
    for tile in range(2):
        context_ref[0, 0, :, tile * LANES : (tile + 1) * LANES] = jnp.where(
            lane_low, heads[2 * tile], heads[2 * tile + 1]
        ).astype(LOW)


def attend(slot, groups, spots, counts, rows, weights, biases, buffers):
    pairs, seq, width = rows.shape
    shapes = [
        ((4, pairs, seq, 768), (1, 1, seq, 768), lambda g, p, *_: (slot + g, p, 0, 0)),
        ((4, pairs, seq, 256), (1, 1, seq, 256), lambda g, p, *_: (slot + g, p, 0, 0)),
        ((4, width, 768), (1, width, 768), lambda g, p, *_: (slot + g, 0, 0)),
    ]
    operands = list(weights) + list(biases)
    aliases = {3 + len(operands) + i: i for i in range(len(buffers))}
    return pl.pallas_call(
        attend_kernel,
        grid_spec=pltpu.PrefetchScalarGridSpec(
            num_scalar_prefetch=2,
            grid=(groups, pairs),
            in_specs=[pl.BlockSpec((1, seq, width), lambda g, p, *_: (p, 0, 0))]
            + [spec for _, spec in operands]
            + [ANYWHERE] * len(buffers),
            out_specs=[pl.BlockSpec(block, index) for _, block, index in shapes],
            scratch_shapes=[pltpu.VMEM((1, 768), WIDE)],
        ),
        out_shape=[jax.ShapeDtypeStruct(shape, LOW) for shape, _, _ in shapes],
        input_output_aliases=aliases,
        name="attend",
        compiler_params=pltpu.CompilerParams(vmem_limit_bytes=56 * 1024 * 1024),
    )(spots, counts, rows, *[array for array, _ in operands], *buffers)


def attend_back_kernel(
    count_ref, place_ref, rows_hbm, cots_hbm, cot_ref, qkv_ref, context_ref, upper_ref, lower_ref, *refs
):
    near_ref, bias_ref, qkv_grad_ref, grad_buf, context_buf, rows_buf, cots_buf, out_buf, sems = refs[-9:]
    pair = pl.program_id(0)
    copies = [
        pltpu.make_async_copy(rows_hbm, rows_buf, sems.at[0]),
        pltpu.make_async_copy(cots_hbm, cots_buf, sems.at[1]),
    ]

    @pl.when(pair == 0)
    def _():
        for copy in copies:
            copy.start()
        out_buf[:LANES, :] = upper_ref[...]
        out_buf[LANES:, :] = lower_ref[...]

    at = pl.ds(pl.multiple_of(pair * SEQ, 8), SEQ)
    context_grad = dot(cot_ref[0], out_buf[...], 1, 1).astype(LOW)
    qkv = qkv_ref[0, 0]
    context_buf[at, :] = context_ref[0, 0].astype(WIDE)
    length = TEXT + count_ref[pair]
    lane = lax.broadcasted_iota(jnp.int32, (SEQ, LANES), 1)
    padding = lax.broadcasted_iota(jnp.int32, (SEQ, SEQ), 0) >= length
    grads = [[], [], []]
    lane_low = lane < HEAD_DIM
    work = []
    for tile in range(2):
        query, key, value = (
            qkv[:, i * 256 + tile * LANES : i * 256 + (tile + 1) * LANES] for i in range(3)
        )
        query = query * SCALE
        outer = context_grad[:, tile * LANES : (tile + 1) * LANES]
        for side in range(2):
            mine = lane_low if side == 0 else jnp.logical_not(lane_low)
            scores = dot(jnp.where(mine, key, jnp.zeros_like(key)), query, 1, 1)
            probs_grad = dot(jnp.where(mine, value, jnp.zeros_like(value)), outer, 1, 1)
            work.append((scores, probs_grad, query, key, outer))
    heads = []
    for scores, probs_grad, query, key, outer in work:
        scores = jnp.where(padding, NEGATIVE, scores)
        power = jnp.exp(scores - jnp.max(scores, 0, keepdims=True))
        probs = power * (1.0 / jnp.sum(power, 0, keepdims=True))
        both = probs * probs_grad
        score_grad = (both - probs * jnp.sum(both, 0, keepdims=True)).astype(LOW)
        heads.append(
            (dot(score_grad, key, 0, 0), dot(score_grad, query, 1, 0), dot(probs.astype(LOW), outer, 1, 0))
        )
    for tile in range(2):
        for i, scale in enumerate((SCALE, 1.0, 1.0)):
            pair_of = [heads[2 * tile + side][i] for side in range(2)]
            grads[i].append((jnp.where(lane_low, *pair_of) * scale).astype(LOW))
    joined = jnp.concatenate(grads[0] + grads[1] + grads[2], 1)
    qkv_grad_ref[0] = joined
    grad_buf[at, :] = joined.astype(WIDE)

    @pl.when(pair == pl.num_programs(0) - 1)
    def _():
        for copy in copies:
            copy.wait()
        stacked = dot(grad_buf[...].astype(LOW), rows_buf[...], 0, 0).astype(LOW)
        outs = dot(context_buf[...].astype(LOW), cots_buf[...], 0, 0).astype(LOW)
        for i in range(2):
            near_ref[i, :3] = stacked.reshape(3, 2, LANES, -1)[:, i]
            near_ref[i, 3] = outs[i * LANES : (i + 1) * LANES]
        bias_ref[...] = jnp.sum(grad_buf[...], 0, keepdims=True)


def attend_back(slot, first, counts, places, rows, cot, kept, out):
    qkv, context, _ = kept
    _, pairs, seq, _ = qkv.shape
    width = rows.shape[1]
    return pl.pallas_call(
        attend_back_kernel,
        grid_spec=pltpu.PrefetchScalarGridSpec(
            num_scalar_prefetch=2,
            grid=(pairs,),
            in_specs=[
                ANYWHERE,
                ANYWHERE,
                pl.BlockSpec((1, seq, width), lambda p, *_: (p, 0, 0)),
                pl.BlockSpec((1, 1, seq, 768), lambda p, *_: (slot, p, 0, 0)),
                pl.BlockSpec((1, 1, seq, 256), lambda p, *_: (slot, p, 0, 0)),
                pl.BlockSpec((LANES, width), lambda p, count, at: (at[first], 0)),
                pl.BlockSpec((LANES, width), lambda p, count, at: (at[first + 1], 0)),
            ],
            out_specs=[
                pl.BlockSpec((2, 4, LANES, width), lambda p, *_: (0, 0, 0, 0)),
                pl.BlockSpec((1, 768), lambda p, *_: (0, 0)),
                pl.BlockSpec((1, seq, 768), lambda p, *_: (p, 0, 0)),
            ],
            scratch_shapes=[
                pltpu.VMEM((pairs * seq, 768), WIDE),
                pltpu.VMEM((pairs * seq, 256), WIDE),
                pltpu.VMEM(rows.shape, LOW),
                pltpu.VMEM(cot.shape, LOW),
                pltpu.VMEM((2 * LANES, width), LOW),
                pltpu.SemaphoreType.DMA((2,)),
            ],
        ),
        out_shape=[
            jax.ShapeDtypeStruct((2, 4, LANES, width), LOW),
            jax.ShapeDtypeStruct((1, 768), WIDE),
            jax.ShapeDtypeStruct(qkv.shape[1:], LOW),
        ],
        name="attend_back",
        compiler_params=pltpu.CompilerParams(vmem_limit_bytes=56 * 1024 * 1024),
    )(counts, places, rows, cot, cot.reshape(pairs, seq, width), qkv, context, out, out)


def middle_kernel(
    spot_ref, rows_ref, context_ref, own_ref, near_ref, far_ref, bias_ref, gain_ref, shift_ref, *refs
):
    middle_ref, hidden_ref, out_ref = refs

    @pl.when(pl.program_id(0) == 0)
    def _():
        for i in range(8):
            source = own_ref if i < 4 else (near_ref if i < 6 else far_ref)
            start = pl.multiple_of(spot_ref[i] * LANES, LANES)
            out_ref[i * LANES : (i + 1) * LANES, :] = source[pl.ds(start, LANES), :]

    context = jnp.concatenate([context_ref[i, 0] for i in range(4)], 1)
    attended = dot(context, out_ref[...], 1, 0)
    middle = rows_ref[0].astype(WIDE) + attended + bias_ref[...].astype(WIDE)
    middle_ref[0] = middle
    center = middle - jnp.mean(middle, -1, keepdims=True)
    spread = jnp.mean(center * center, -1, keepdims=True)
    hidden = center * lax.rsqrt(spread + EPS) * gain_ref[...].astype(WIDE)
    hidden_ref[0] = (hidden + shift_ref[...].astype(WIDE)).astype(LOW)


def middle_step(spots, rows, context, own, near, far, bias, gain, shift):
    pairs, seq, width = rows.shape
    block = lambda: pl.BlockSpec((1, seq, width), lambda p, *_: (p, 0, 0))
    return pl.pallas_call(
        middle_kernel,
        grid_spec=pltpu.PrefetchScalarGridSpec(
            num_scalar_prefetch=1,
            grid=(pairs,),
            in_specs=[
                block(),
                pl.BlockSpec((4, 1, seq, 256), lambda p, *_: (0, p, 0, 0)),
                resident(own.shape),
                resident(near.shape),
                resident(far.shape),
            ]
            + [resident((1, width))] * 3,
            out_specs=[block(), block()],
            scratch_shapes=[pltpu.VMEM((8 * LANES, width), LOW)],
        ),
        out_shape=[
            jax.ShapeDtypeStruct(rows.shape, WIDE),
            jax.ShapeDtypeStruct(rows.shape, LOW),
        ],
        name="middle",
        compiler_params=pltpu.CompilerParams(vmem_limit_bytes=56 * 1024 * 1024),
    )(spots, rows, context, own, near, far, bias, gain, shift)


def mlp_kernel(step, turned, spot_ref, hidden_ref, cot_ref, *refs):
    ups, downs, biases = refs[:4], refs[4:8], refs[8:12]
    near_ref, far_ref, bias_out, act_ref, pre_ref, up_ref, down_ref, bias_ref = refs[-8:]
    rows = hidden_ref.shape[0]
    for r in range(4):
        span = slice(r * LANES, (r + 1) * LANES)
        if turned:
            up_ref[0, :, span] = ups[r][:, 0].reshape(LANES, -1).T
            down_ref[0, span, :] = downs[r][:, 0].reshape(LANES, -1)
        else:
            up_ref[0, :, span] = ups[r][...]
            down_ref[0, span, :] = downs[r][...]
        bias_ref[:, span] = biases[r][...].astype(WIDE)

    def one(i, carry):
        at = pl.ds(i * step, step)
        pre_act = dot(hidden_ref[at, :], up_ref[0], 1, 0) + bias_ref[...]
        act_grad = dot(cot_ref[at, :], down_ref[0], 1, 1)
        chance = 0.5 + 0.5 * lax.erf(pre_act * ROOT_HALF)
        act_ref[0, at, :] = (pre_act * chance).astype(LOW)
        slope = chance + pre_act * (NORMAL * jnp.exp(-0.5 * pre_act * pre_act))
        pre_ref[0, at, :] = (act_grad * slope).astype(LOW)
        return carry

    for i in range(rows // step):
        one(i, 0)
    up_grad = dot(pre_ref[0], hidden_ref[...], 0, 0).astype(LOW).reshape(4, LANES, -1)
    down_grad = dot(act_ref[0], cot_ref[...], 0, 0).astype(LOW).reshape(4, LANES, -1)
    bias_out[0] = jnp.sum(pre_ref[0].astype(WIDE), 0, keepdims=True)
    for i in range(2):
        near_ref[i, 0] = up_grad[i]
        near_ref[i, 1] = down_grad[i]
        far_ref[i, 0] = up_grad[2 + i]
        far_ref[i, 1] = down_grad[2 + i]


def mlp(first, turned, spots, hidden, cot, ups, downs, biases, buffers):
    rows, width = hidden.shape
    operands = list(ups) + list(downs) + list(biases)
    tile = 4 * LANES
    grad = jax.ShapeDtypeStruct((2, 4, LANES, width), LOW)
    grad_block = pl.BlockSpec((2, 2, LANES, width), lambda j, *_: (0, j, 0, 0))
    return pl.pallas_call(
        functools.partial(mlp_kernel, rows // 2, turned),
        grid_spec=pltpu.PrefetchScalarGridSpec(
            num_scalar_prefetch=1,
            grid=(2,),
            in_specs=[pl.BlockSpec(memory_space=pltpu.VMEM)] * 2
            + [spec for _, spec in operands]
            + [ANYWHERE] * len(buffers),
            out_specs=[grad_block] * 2
            + [
                pl.BlockSpec((1, 1, tile), lambda j, *_: (j, 0, 0)),
                pl.BlockSpec((1, rows, tile), lambda j, *_: (first // 2, 0, j)),
                pl.BlockSpec((1, rows, tile), lambda j, *_: (first // 2, 0, j)),
                pl.BlockSpec((1, width, tile), lambda j, *_: (first // 2, 0, j)),
                pl.BlockSpec((1, tile, width), lambda j, *_: (first // 2, j, 0)),
            ],
            scratch_shapes=[pltpu.VMEM((1, tile), WIDE)],
        ),
        out_shape=[grad] * 2
        + [
            jax.ShapeDtypeStruct((2, 1, tile), WIDE),
            jax.ShapeDtypeStruct((4, rows, 2 * tile), LOW),
            jax.ShapeDtypeStruct((4, rows, 2 * tile), LOW),
            jax.ShapeDtypeStruct((4, width, 2 * tile), LOW),
            jax.ShapeDtypeStruct((4, 2 * tile, width), LOW),
        ],
        input_output_aliases={3 + len(operands) + i: 3 + i for i in range(len(buffers))},
        name="mlp",
        compiler_params=pltpu.CompilerParams(vmem_limit_bytes=36 * 1024 * 1024),
    )(spots, hidden, cot, *[array for array, _ in operands], *buffers)


def norm_back(values, gain, grad):
    center = values - jnp.mean(values, -1, keepdims=True)
    scale = lax.rsqrt(jnp.mean(center * center, -1, keepdims=True) + EPS)
    unit = center * scale
    inner = grad * gain
    pulled = scale * (
        inner
        - jnp.mean(inner, -1, keepdims=True)
        - unit * jnp.mean(inner * unit, -1, keepdims=True)
    )
    return pulled, jnp.sum(grad * unit, 0, keepdims=True), jnp.sum(grad, 0, keepdims=True)


def mlp_back_kernel(pre_ref, up_ref, middle_hbm, cot_hbm, gain_ref, grad_ref, low_ref, sums_ref, *refs):
    sum_buf, middle_buf, cot_buf, sems = refs
    step = pl.program_id(0)
    copies = [
        pltpu.make_async_copy(middle_hbm, middle_buf, sems.at[0]),
        pltpu.make_async_copy(cot_hbm, cot_buf, sems.at[1]),
    ]
    part = dot(pre_ref[0], up_ref[0], 1, 1)

    @pl.when(step == 0)
    def _():
        for copy in copies:
            copy.start()
        sum_buf[...] = part

    @pl.when(step > 0)
    def _():
        sum_buf[...] += part

    @pl.when(step == pl.num_programs(0) - 1)
    def _():
        for copy in copies:
            copy.wait()
        sums_ref[...] = jnp.zeros_like(sums_ref)
        chunk = 224

        def one(i, carry):
            at = pl.ds(i * chunk, chunk)
            cot = cot_buf[at, :].astype(WIDE)
            pulled, gain_grad, shift_grad = norm_back(
                middle_buf[at, :], gain_ref[...].astype(WIDE), sum_buf[at, :]
            )
            grad = cot + pulled
            low = grad.astype(LOW)
            grad_ref[at, :] = grad
            low_ref[at, :] = low
            sums_ref[0:1, :] += gain_grad
            sums_ref[1:2, :] += shift_grad
            sums_ref[2:3, :] += jnp.sum(low.astype(WIDE), 0, keepdims=True)
            sums_ref[3:4, :] += jnp.sum(cot, 0, keepdims=True)
            return carry

        for i in range(grad_ref.shape[0] // chunk):
            one(i, 0)


def mlp_back(pre_grads, ups, middle, cot, gain):
    tiles, rows, tile = pre_grads.shape
    width = cot.shape[1]
    return pl.pallas_call(
        mlp_back_kernel,
        grid=(tiles,),
        in_specs=[
            pl.BlockSpec((1, rows, tile), lambda j: (j, 0, 0)),
            pl.BlockSpec((1, width, tile), lambda j: (j, 0, 0)),
            ANYWHERE,
            ANYWHERE,
            resident((1, width)),
        ],
        out_specs=[resident((rows, width)), resident((rows, width)), resident((8, width))],
        out_shape=[
            jax.ShapeDtypeStruct((rows, width), WIDE),
            jax.ShapeDtypeStruct((rows, width), LOW),
            jax.ShapeDtypeStruct((8, width), WIDE),
        ],
        scratch_shapes=[
            pltpu.VMEM((rows, width), WIDE),
            pltpu.VMEM((rows, width), WIDE),
            pltpu.VMEM((rows, width), LOW),
            pltpu.SemaphoreType.DMA((2,)),
        ],
        name="mlp_back",
        compiler_params=pltpu.CompilerParams(vmem_limit_bytes=44 * 1024 * 1024),
    )(pre_grads, ups, middle, cot, gain)


def mlp_out_kernel(half, act_ref, down_ref, middle_hbm, bias_ref, *refs):
    out_ref, sum_buf, middle_buf, sem = refs[-4:]
    step = pl.program_id(0)
    rows = out_ref.shape[0]
    copy = pltpu.make_async_copy(middle_hbm.at[pl.ds(half * rows, rows), :], middle_buf, sem)
    part = dot(act_ref[0], down_ref[0], 1, 0)

    @pl.when(step == 0)
    def _():
        copy.start()
        sum_buf[...] = part

    @pl.when(step > 0)
    def _():
        sum_buf[...] += part

    @pl.when(step == pl.num_programs(0) - 1)
    def _():
        copy.wait()
        out_ref[...] = (sum_buf[...] + middle_buf[...] + bias_ref[...].astype(WIDE)).astype(LOW)


def mlp_out(half, acts, downs, middle, bias, buffers):
    tiles, rows, tile = acts.shape
    width = middle.shape[1]
    count = rows // 2
    return pl.pallas_call(
        functools.partial(mlp_out_kernel, half),
        grid=(tiles,),
        in_specs=[
            pl.BlockSpec((1, count, tile), lambda j: (j, half, 0)),
            pl.BlockSpec((1, tile, width), lambda j: (j, 0, 0)),
            ANYWHERE,
            resident((1, width)),
        ]
        + [ANYWHERE] * len(buffers),
        out_specs=pl.BlockSpec((count, width), lambda j: (half, 0)),
        out_shape=jax.ShapeDtypeStruct((rows, width), LOW),
        scratch_shapes=[
            pltpu.VMEM((count, width), WIDE),
            pltpu.VMEM((count, width), WIDE),
            pltpu.SemaphoreType.DMA(()),
        ],
        input_output_aliases={4: 0} if buffers else {},
        name="mlp_out",
        compiler_params=pltpu.CompilerParams(vmem_limit_bytes=56 * 1024 * 1024),
    )(acts, downs, middle, bias, *buffers)


def pack_kernel(spot_ref, *refs):
    out_refs = refs[-2:]
    shared_one, shared_two = refs[8:10]
    for side in range(2):
        near, far, first, second = refs[4 * side : 4 * side + 4]
        out = out_refs[side]
        for r in range(4):
            at = spot_ref[r]
            source = near if r < 2 else far
            lanes = (r % 2) * LANES
            out[pl.ds(at, 1), :] = source[:, lanes : lanes + LANES]
            out[pl.ds(4 + at, 1), :] = source[:, 512 + lanes : 512 + lanes + LANES]
            for j in range(4):
                sums = first if j < 2 else second
                out[pl.ds(8 + at * 4 + j, 1), :] = sums[j % 2, :, r * LANES : (r + 1) * LANES]
        rows = [(shared_one, 0), (shared_one, 1), (shared_two, 2), (shared_two, 0), (shared_two, 1), (shared_two, 3)]
        for k, (source, row) in enumerate(rows):
            for i in range(8):
                at = 24 + 8 * k + i
                out[at : at + 1, :] = source[row : row + 1, i * LANES : (i + 1) * LANES]


def pack(spots, own, other, sums_one, sums_two):
    return pl.pallas_call(
        pack_kernel,
        grid_spec=pltpu.PrefetchScalarGridSpec(
            num_scalar_prefetch=1,
            grid=(1,),
            in_specs=[resident(item.shape) for item in (*own, *other, sums_one, sums_two)],
            out_specs=[resident((72, LANES))] * 2,
        ),
        out_shape=[jax.ShapeDtypeStruct((72, LANES), WIDE)] * 2,
        name="pack",
        compiler_params=pltpu.CompilerParams(vmem_limit_bytes=8 * 1024 * 1024),
    )(spots, *own, *other, sums_one, sums_two)


def input_kernel(zero_ref, one_ref, two_ref, three_ref, weight_ref, rows_ref, above_ref, gain_ref, out_ref, sums_ref):
    pulled_sum = dot(zero_ref[0], weight_ref[0], 1, 1)
    for i, grad_ref in enumerate((one_ref, two_ref, three_ref)):
        pulled_sum = pulled_sum + dot(grad_ref[0], weight_ref[i + 1], 1, 1)
    pulled, gain_grad, shift_grad = norm_back(
        rows_ref[0].astype(WIDE), gain_ref[...].astype(WIDE), pulled_sum
    )
    out_ref[0] = (above_ref[0] + pulled).astype(LOW)

    @pl.when(pl.program_id(0) == 0)
    def _():
        sums_ref[...] = jnp.zeros_like(sums_ref)

    sums_ref[0:1, :] += gain_grad
    sums_ref[1:2, :] += shift_grad


def input_step(grads, weights, rows, above, gain):
    pairs, seq, width = rows.shape
    block = lambda: pl.BlockSpec((1, seq, width), lambda p: (p, 0, 0))
    return pl.pallas_call(
        input_kernel,
        grid=(pairs,),
        in_specs=[
            pl.BlockSpec((1, seq, 768), lambda p: (p, 0, 0)),
            pl.BlockSpec((1, seq, 768), lambda p: (p, 0, 0)),
            pl.BlockSpec((1, seq, 768), lambda p: (p, 0, 0)),
            pl.BlockSpec((1, seq, 768), lambda p: (p, 0, 0)),
            resident(weights.shape),
            block(),
            block(),
            resident((1, width)),
        ],
        out_specs=[block(), resident((8, width))],
        out_shape=[
            jax.ShapeDtypeStruct(rows.shape, LOW),
            jax.ShapeDtypeStruct((8, width), WIDE),
        ],
        name="input_grad",
        compiler_params=pltpu.CompilerParams(vmem_limit_bytes=28 * 1024 * 1024),
    )(*grads, weights, rows, above, gain)


def place_kernel(turned, spot_ref, near_ref, far_ref, *refs):
    outs = refs[-len(turned) :]
    core = pl.program_id(1) ^ spot_ref[0]
    for i, turn in enumerate(turned):
        parts = []
        for z in range(4):
            at = z ^ spot_ref[2]
            parts.append(
                jnp.where(core == 0, near_ref[at, i], far_ref[at, i])
            )
        block = jnp.concatenate(parts, 0)
        outs[i][...] = (block.T if turn else block).astype(WIDE)


def place(turned, chunk, chunks, spots, near, far, shapes, buffers):
    _, kinds, rows, width = near.shape
    source = lambda: pl.BlockSpec(
        (4, kinds, rows, width), lambda x, c, spot: (x ^ spot[1], 0, 0, 0)
    )
    specs = [
        pl.BlockSpec((width, LANES), lambda x, c, spot: (0, (c * 2 + x) * chunks + chunk))
        if turn
        else pl.BlockSpec((LANES, width), lambda x, c, spot: ((c * 2 + x) * chunks + chunk, 0))
        for turn in turned
    ]
    return pl.pallas_call(
        functools.partial(place_kernel, turned),
        grid_spec=pltpu.PrefetchScalarGridSpec(
            num_scalar_prefetch=1,
            grid=(2, 2),
            in_specs=[source(), source()] + [ANYWHERE] * len(buffers),
            out_specs=specs,
        ),
        out_shape=[jax.ShapeDtypeStruct(shape, WIDE) for shape in shapes],
        input_output_aliases={3 + i: i for i in range(len(buffers))},
        name="place",
        compiler_params=pltpu.CompilerParams(vmem_limit_bytes=20 * 1024 * 1024),
    )(spots, near, far, *buffers)


def gathered_kernel(source_ref, *refs):
    up_ref, down_ref = refs[-2:]
    rows = [[source_ref[high, low, 0, 0] for high in range(2)] for low in range(2)]
    for kind, out_ref in enumerate((up_ref, down_ref)):
        parts = []
        for sub in range(2):
            for low in range(2):
                for high in range(2):
                    parts.append(rows[low][high][2 * sub + kind])
        block = jnp.concatenate(parts, 0)
        out_ref[...] = (block.T if kind == 0 else block).astype(WIDE)


def gathered(chunk, chunks, source, shapes, buffers):
    kinds, rows, width = source.shape[1:]
    source = source.reshape((2, 2, 2, 2, kinds, rows, width))
    span = 2 * LANES
    return pl.pallas_call(
        gathered_kernel,
        grid=(2, 2),
        in_specs=[
            pl.BlockSpec((2, 2, 1, 1, kinds, rows, width), lambda c, x: (0, 0, x, c, 0, 0, 0))
        ]
        + [ANYWHERE] * len(buffers),
        out_specs=[
            pl.BlockSpec((width, span), lambda c, x: (0, (c * 2 + x) * chunks + chunk)),
            pl.BlockSpec((span, width), lambda c, x: ((c * 2 + x) * chunks + chunk, 0)),
        ],
        out_shape=[jax.ShapeDtypeStruct(shape, WIDE) for shape in shapes],
        input_output_aliases={1 + i: i for i in range(len(buffers))},
        name="gathered",
        compiler_params=pltpu.CompilerParams(vmem_limit_bytes=24 * 1024 * 1024),
    )(source, *buffers)


def paired_body(
    layer_in,
    patch_count,
    attn_gain,
    attn_shift,
    query_weight,
    query_bias,
    key_weight,
    value_weight,
    value_bias,
    out_weight,
    out_bias,
    mlp_gain,
    mlp_shift,
    up_weight,
    up_bias,
    down_weight,
    down_bias,
    layer_cot,
):
    groups = lax.axis_size("dp")
    rank = lax.axis_index("dp")
    half_id = lax.axis_index("mp")
    core_id, x_id, zlow_id, zhigh_id = rank & 1, (rank >> 1) & 1, (rank >> 2) & 1, (rank >> 3) & 1
    part = core_id * 2 + x_id
    spots = jnp.stack([part, part ^ 1, part ^ 2, part ^ 3]).astype(jnp.int32)
    sides = jnp.stack([x_id, x_id ^ 1, x_id, x_id ^ 1]).astype(jnp.int32)
    place_spots = jnp.stack([core_id, x_id, zlow_id * 2 + zhigh_id]).astype(jnp.int32)

    swap = lambda value, bit: flip(value, "dp", bit, groups)
    across = lambda value: flip(value, "mp", 1, 2)

    rows, width = layer_in.shape
    heads_width = query_weight.shape[1]
    hidden_width = up_weight.shape[1]
    block = hidden_width // 4
    pairs = rows // SEQ
    counts = pick(patch_count, half_id, pairs, 0)
    row_vec = lambda vec: vec.reshape(1, -1)

    gate = lambda value, *waits: after(value, *waits) if waits else value
    shape_three = (pairs, SEQ, width)
    subs = block // LANES

    slice_rows = LANES // 2
    slice_at = (rank // 4) * 2 * subs + rank % 4
    slices = jnp.stack(
        [
            jnp.stack(
                [
                    pick(up_weight, slice_at + 4 * i, slice_rows, 1).T,
                    pick(down_weight, slice_at + 4 * i, slice_rows, 0),
                ]
            )
            for i in range(2)
        ]
    )
    slices = across(slices)
    sent_qk = jnp.stack([pick(w, core_id, heads_width // 2, 1) for w in (query_weight, key_weight)])
    value_near = across(pick(value_weight, part, LANES, 1))
    sent_bias = row_vec(jnp.concatenate([query_bias, value_bias, up_bias]))
    raw_out = pick(out_weight, core_id, heads_width // 2, 0)
    rows_in = layer_in.astype(WIDE)
    normed = layer_norm(
        rows_in, attn_gain.astype(WIDE), attn_shift.astype(WIDE)
    ).astype(LOW)
    normed_three = normed.reshape(shape_three)

    def own_inputs():
        weights = [
            (w, pl.BlockSpec((width, LANES), lambda g, p, spot, count, i=i: (0, spot[2 * g + i])))
            for w in (query_weight, key_weight, value_weight)
            for i in range(2)
        ]
        biases = [
            (row_vec(b), pl.BlockSpec((1, LANES), lambda g, p, spot, count, i=i: (0, spot[2 * g + i])))
            for b in (query_bias, value_bias)
            for i in range(2)
        ]
        return weights, biases

    def other_inputs(group, qk, values):
        weights = [
            (qk, pl.BlockSpec((None, width, LANES), lambda g, p, side, count, k=k, i=i: (k, 0, side[i])))
            for k in range(2)
            for i in range(2)
        ]
        weights += [(item, pl.BlockSpec((width, LANES), lambda g, p, *_: (0, 0))) for item in values]
        biases = [
            (bias_other, pl.BlockSpec((1, LANES), lambda g, p, side, count, k=k, i=i: (0, 4 * k + side[4 + 2 * group + i])))
            for k in range(2)
            for i in range(2)
        ]
        return weights, biases

    other_spots = jnp.concatenate([sides, spots])
    slices, value_near, sent_qk, raw_out, sent_bias, normed, spots, other_spots, counts = lax.optimization_barrier(
        (slices, value_near, sent_qk, raw_out, sent_bias, normed, spots, other_spots, counts)
    )
    normed_three = normed.reshape(shape_three)
    near_qk = across(sent_qk)
    bias_other = across(sent_bias)
    value_side = swap(value_near, XBIT)
    gathered_weights = [lax.all_gather(slices[0], "dp"), lax.all_gather(slices[1], "dp")]
    kept = attend(
        0, 2, spots, counts, normed_three, *own_inputs(), []
    )
    near_qk, bias_other, value_side, _ = lax.optimization_barrier((near_qk, bias_other, value_side, kept[1]))
    sent_out = after(raw_out, near_qk)
    near_out = across(sent_out)
    far_qk, far_values = swap(near_qk, CORE), [swap(value_near, CORE), swap(value_side, CORE)]
    kept = attend(
        2, 1, gate(other_spots, sent_out), counts, normed_three, *other_inputs(0, near_qk, (value_near, value_side)), kept
    )
    near_out, far_qk, far_values, _ = lax.optimization_barrier((near_out, far_qk, far_values, kept[1]))
    far_out = swap(near_out, CORE)
    kept = attend(
        3, 1, gate(other_spots, near_out), counts, normed_three, *other_inputs(1, far_qk, far_values), kept
    )
    places = jnp.concatenate([spots, sides])
    middle, hidden = middle_step(
        places,
        layer_in.reshape(shape_three),
        kept[1],
        out_weight,
        near_out,
        far_out,
        row_vec(out_bias),
        row_vec(mlp_gain),
        row_vec(mlp_shift),
    )
    middle = middle.reshape(rows, width)
    hidden = hidden.reshape(rows, width)

    def own_mlp(first):
        ups = [
            (up_weight, pl.BlockSpec((width, LANES), lambda j, spot, r=r: (0, spot[r] * subs + first + j)))
            for r in range(4)
        ]
        downs = [
            (down_weight, pl.BlockSpec((LANES, width), lambda j, spot, r=r: (spot[r] * subs + first + j, 0)))
            for r in range(4)
        ]
        biases = [
            (row_vec(up_bias), pl.BlockSpec((1, LANES), lambda j, spot, r=r: (0, spot[r] * subs + first + j)))
            for r in range(4)
        ]
        return ups, downs, biases

    def other_mlp(first):
        source = gathered_weights[first // 2]
        ups, downs = (
            [
                (source, pl.BlockSpec((2, 1, slice_rows, width), lambda j, spot, r=r, k=k: (spot[r] * 2 + j, k, 0, 0)))
                for r in range(4)
            ]
            for k in range(2)
        )
        biases = [
            (bias_other, pl.BlockSpec((1, LANES), lambda j, spot, r=r: (0, 8 + spot[r] * subs + first + j)))
            for r in range(4)
        ]
        return ups, downs, biases

    def cut(item, index):
        count, lanes, cols = item.shape
        return pick(item.reshape(count, 2, lanes // 2, cols), index, 1, 1)[:, 0]

    def outbound(near, far, first, last):
        return total(near[:, first:last], far[:, first:last])

    def sideways(near, far, beyond, first, last):
        return total(near[1, first:last], far[1, first:last], beyond[1])

    def collected(near, far, beyond, side, first, last):
        return total(near[0, first:last], far[0, first:last], beyond[0], side)

    def halves(item):
        return cut(item, zlow_id ^ 1), cut(item, zlow_id)

    def quarters(item):
        return cut(item, zhigh_id ^ 1), cut(item, zhigh_id)

    back = lambda slot, *wait: attend_back(
        slot,
        2 * slot,
        gate(counts, *wait),
        places,
        normed,
        attn_grad,
        kept,
        (out_weight, out_weight, near_out, far_out)[slot],
    )

    together = lambda *items: lax.optimization_barrier(items)
    other_a = mlp(2, True, spots, hidden, layer_cot, *other_mlp(0), [])
    far_other_a = swap(other_a[1], CORE)
    own_a = mlp(0, False, spots, hidden, layer_cot, *own_mlp(0), other_a[3:])
    far_other_a, far, _ = together(far_other_a, own_a[1], own_a[2])
    far_own_a = swap(far, CORE)
    out_a = [outbound(other_a[0], far_other_a, *span) for span in ((0, 1), (1, 2), (2, 4))]
    own_b = mlp(6, False, gate(spots, *out_a), hidden, layer_cot, *own_mlp(2), own_a[3:])
    beyond_a0, far_own_a, far, _ = together(across(out_a[0]), far_own_a, own_b[1], own_b[2])
    far_own_b = swap(far, CORE)
    other_b = mlp(
        4, True, gate(spots, beyond_a0, far_own_a), hidden, layer_cot, *other_mlp(2), own_b[3:]
    )
    acts, pre_grads, ups_all, downs_all = other_b[3:]
    beyond_a1, far_own_b, far, _ = together(
        across(after(out_a[1], beyond_a0)), far_own_b, other_b[1], other_b[2]
    )
    far_other_b = swap(far, CORE)
    beyond_a01 = jnp.concatenate([beyond_a0, beyond_a1], 1)
    side_a01 = sideways(own_a[0], far_own_a, beyond_a01, 0, 2)
    middle_grad, attn_grad, sums_two = mlp_back(
        pre_grads, ups_all, middle, layer_cot, gate(row_vec(mlp_gain), side_a01, beyond_a01, far_own_b)
    )
    beyond_a23, arrived_a01, far_other_b, _ = together(
        across(after(out_a[2], beyond_a1)), swap(side_a01, XBIT), far_other_b, sums_two
    )
    side_a23 = sideways(own_a[0], far_own_a, beyond_a23, 2, 4)
    out_b = [outbound(other_b[0], far_other_b, *span) for span in ((0, 2), (2, 4))]
    other_far, bias_other_far, grads_three = back(3, side_a23, arrived_a01, *out_b)
    beyond_b01, arrived_a23, far, _ = together(
        across(out_b[0]), swap(side_a23, XBIT), other_far, bias_other_far
    )
    late_other_far = swap(far, CORE)
    sum_a = jnp.concatenate(
        [
            collected(own_a[0], far_own_a, beyond_a01, arrived_a01, 0, 2),
            collected(own_a[0], far_own_a, beyond_a23, arrived_a23, 2, 4),
        ]
    )
    low_a, keep_a = halves(sum_a)
    side_b01 = sideways(own_b[0], far_own_b, beyond_b01, 0, 2)
    other_near, bias_other_near, grads_two = back(2, low_a, sum_a, side_b01, grads_three)
    beyond_b23, arrived_b01, low_a, late_other_far, _ = together(
        across(after(out_b[1], beyond_b01)), swap(side_b01, XBIT), swap(low_a, ZLOW), late_other_far, bias_other_near
    )
    high_a, keep_a = quarters(total(keep_a, low_a))
    side_b23 = sideways(own_b[0], far_own_b, beyond_b23, 2, 4)
    late_out = [outbound(other_near, late_other_far, *span) for span in ((0, 2), (2, 4))]
    own_far, bias_own_far, grads_one = back(1, high_a, side_b23, arrived_b01, *late_out, grads_two)
    late_beyond0, arrived_b23, high_a, far, _ = together(
        across(late_out[0]), swap(side_b23, XBIT), swap(high_a, ZHIGH), own_far, bias_own_far
    )
    late_own_far = swap(far, CORE)
    one_a = total(keep_a, high_a)
    sum_b = jnp.concatenate(
        [
            collected(own_b[0], far_own_b, beyond_b01, arrived_b01, 0, 2),
            collected(own_b[0], far_own_b, beyond_b23, arrived_b23, 2, 4),
        ]
    )
    low_b, keep_b = halves(sum_b)
    gathered_a = lax.all_gather(one_a, "dp")
    own_near, bias_own_near, grads_zero = back(0, one_a, low_b, sum_b, late_beyond0, grads_one)
    late_beyond1, late_own_far, low_b, _ = together(
        across(after(late_out[1], late_beyond0)), late_own_far, swap(low_b, ZLOW), bias_own_near
    )
    high_b, keep_b = quarters(total(keep_b, low_b))
    late_side0 = sideways(own_near, late_own_far, late_beyond0, 0, 2)
    late_side1 = sideways(own_near, late_own_far, late_beyond1, 2, 4)
    grad_in, sums_one = input_step(
        (grads_zero, grads_one, grads_two, grads_three),
        kept[2],
        layer_in.reshape(shape_three),
        middle_grad.reshape(shape_three),
        gate(row_vec(attn_gain), high_b, late_side0, late_side1),
    )
    high_b, late_arrived0, sums_one = together(swap(high_b, ZHIGH), swap(late_side0, XBIT), sums_one)
    one_b = total(keep_b, high_b)
    gathered_b = lax.all_gather(one_b, "dp")
    quarter_id = zlow_id * 2 + zhigh_id
    z_bits = [None, ZHIGH, ZLOW, ZLOW | ZHIGH]

    def four(item):
        count, lanes, cols = item.shape
        item = item.reshape(count, 4, lanes // 4, cols)
        return [pick(item, quarter_id ^ r, 1, 1)[:, 0] for r in range(4)]

    def send_four(items):
        return [swap(items[r], z_bits[r]) for r in range(1, 4)]

    late_four0 = four(collected(own_near, late_own_far, late_beyond0, late_arrived0, 0, 2))
    own_vec, other_vec = pack(
        spots,
        (bias_own_near, bias_own_far, own_a[2], own_b[2]),
        (bias_other_near, bias_other_far, other_a[2], other_b[2]),
        sums_one,
        sums_two,
    )
    layer_out = mlp_out(
        0, acts, downs_all, middle, gate(row_vec(down_bias), one_b, other_vec, *late_four0), []
    )
    late_arrived1, late_got0, vec_got, mark = together(
        swap(after(late_side1, late_arrived0), XBIT), send_four(late_four0), across(other_vec), layer_out
    )
    late_one0 = total(late_four0[0], *late_got0)
    late_four1 = four(collected(own_near, late_own_far, late_beyond1, late_arrived1, 2, 4))
    vec = own_vec + vec_got
    layer_out = mlp_out(
        1, acts, downs_all, middle, gate(row_vec(down_bias), late_one0, vec, *late_four1), [mark]
    )
    late_got1, late_have0, layer_out = together(
        send_four(late_four1), send_four([late_one0] * 4), layer_out
    )
    late_one1 = total(late_four1[0], *late_got1)
    late_have0 = jnp.stack([late_one0, *late_have0])
    up_shape, down_shape = up_weight.shape, down_weight.shape
    placed = gathered(
        0, 2, gate(gathered_a, late_one1, late_have0), (up_shape, down_shape), []
    )
    late_have1, late_side0, vec_got, *placed = together(
        send_four([late_one1] * 4), swap(late_have0, XBIT), swap(vec, CORE), *placed
    )
    late_have1 = jnp.stack([late_one1, *late_have1])
    late_have0 = jnp.concatenate([late_have0, late_side0])
    vec = vec + vec_got
    placed = gathered(
        1, 2, gate(gathered_b, late_have1, late_have0, vec), (up_shape, down_shape), placed
    )
    late_side1, late_far0, vec_got, grad_up_weight, grad_down_weight = together(
        swap(late_have1, XBIT), swap(late_have0, CORE), swap(vec, XBIT), *placed
    )
    late_have1 = jnp.concatenate([late_have1, late_side1])
    vec = vec + vec_got
    grad_query_weight, grad_key_weight = place(
        (True, True), 0, 1, gate(place_spots, late_have1, vec), late_have0, late_far0, (query_weight.shape,) * 2, []
    )
    late_far1, vec_got, grad_query_weight, grad_key_weight = together(
        swap(late_have1, CORE), send_four([vec] * 4), grad_query_weight, grad_key_weight
    )
    vec = ((vec + vec_got[0]) + (vec_got[1] + vec_got[2])).reshape(-1)
    grad_value_weight, grad_out_weight = place(
        (True, False), 0, 1, place_spots, late_have1, late_far1, (value_weight.shape, out_weight.shape), []
    )
    grad_query_bias = vec[:heads_width]
    grad_value_bias = vec[heads_width : 2 * heads_width]
    grad_up_bias = vec[2 * heads_width : 2 * heads_width + hidden_width]
    (
        grad_attn_gain,
        grad_attn_shift,
        grad_out_bias,
        grad_mlp_gain,
        grad_mlp_shift,
        grad_down_bias,
    ) = jnp.split(vec[2 * heads_width + hidden_width :], 6)
    return (
        layer_out,
        grad_in.reshape(rows, width),
        grad_attn_gain,
        grad_attn_shift,
        grad_query_weight,
        grad_query_bias,
        grad_key_weight,
        grad_value_weight,
        grad_value_bias,
        grad_out_weight,
        grad_out_bias,
        grad_mlp_gain,
        grad_mlp_shift,
        grad_up_weight,
        grad_up_bias,
        grad_down_weight,
        grad_down_bias,
    )


def solution(mesh):
    paired = mesh.shape["mp"] == 2 and mesh.shape["dp"] == 16
    body = paired_body if paired else general_body
    placed = (
        P(("dp", "mp"), None),
        P("dp"),
        P(),
        P(),
        P(None, "mp"),
        P("mp"),
        P(None, "mp"),
        P(None, "mp"),
        P("mp"),
        P("mp", None),
        P(),
        P(),
        P(),
        P(None, "mp"),
        P("mp"),
        P("mp", None),
        P(),
        P(("dp", "mp"), None),
    )
    return jax.shard_map(
        body,
        mesh=mesh,
        in_specs=placed,
        out_specs=(
            P(("dp", "mp"), None),
            P(("dp", "mp"), None),
            P(),
            P(),
            P(None, "mp"),
            P("mp"),
            P(None, "mp"),
            P(None, "mp"),
            P("mp"),
            P("mp", None),
            P(),
            P(),
            P(),
            P(None, "mp"),
            P("mp"),
            P("mp", None),
            P(),
        ),
        check_vma=False,
    )
```
